256 devices in a mesh: role: 2 (over z_hi), dp: 32 (over x, z_lo, core), mp: 4 (over y).
Axes of the slice: x: 4, y: 4, z: 8 (z_hi: 2, z_lo: 4; z = z_hi * 4 + z_lo), core: 2. Of those that a mesh axis runs over, the one named last changes fastest.
Arguments:
- state: float32 [2, 2, 8, 2048, 512], P('role', None, None, 'dp', 'mp'), may hold values from 0 to 1
- embed: bfloat16 [2, 1024, 4096], P('role', 'dp', 'mp'), may hold values from -0.09375 to 0.09375
- mlp: bfloat16 [2, 2, 1024, 4096], P('role', None, 'dp', 'mp'), may hold values from -0.1875 to 0.1875
- mom_embed: float32 [2, 1024, 4096], P('role', 'dp', 'mp'), may hold values from -6 to 6
- mom_mlp: float32 [2, 2, 1024, 4096], P('role', None, 'dp', 'mp'), may hold values from -6 to 6
Outputs:
- state_out: float32 [2, 8, 2048, 512], P(None, None, 'dp', 'mp')
- embed_out: bfloat16 [2, 1024, 4096], P('role', 'dp', 'mp')
- mlp_out: bfloat16 [2, 2, 1024, 4096], P('role', None, 'dp', 'mp')
- mom_embed_out: float32 [2, 1024, 4096], P('role', 'dp', 'mp')
- mom_mlp_out: float32 [2, 2, 1024, 4096], P('role', None, 'dp', 'mp')
The draws below stay inside these ranges and needn't reach their ends.
All inputs are finite; a program needn't handle non-finite values.
Results may differ from the reference program's by a relative error of at most 0.0034.
Values may be sent and summed in bfloat16 or wider, within the bound.
A program may use at most 128 MiB of HBM per device.

```python
import jax
import jax.numpy as jnp
from jax import lax

PLANES = 8
PATCH = 16
STEPS = 4
D = 1024
FF = 4096
P_SIZE = 4096
NY = 2048
NZ = 512
ROWS = 128
NPATCH = 4096
N_ROLE = 2
N_DP = 32


def level_of(own_key, shape, split, smallest, top_value):
    gain = 1.0
    for dim, blocks in split:
        heights = jax.random.uniform(jax.random.fold_in(jax.random.fold_in(own_key, 6), dim), (blocks,), jnp.float32, smallest / len(split), top_value / len(split))
        gain = gain * jnp.repeat(jnp.exp(heights), shape[dim] // blocks).reshape((-1,) + (1,) * (len(shape) - 1 - dim))
    return gain


def normal_values(key, dims, scale, most, cuts=(), dtype=jnp.bfloat16):
    array = scale * jax.random.normal(key, dims, jnp.float32)
    if cuts:
        array = array * level_of(key, dims, cuts, -0.22, 0.18)
    return jnp.clip(array, -most, most).astype(dtype)


def setup_inputs(seed: int = 0) -> dict:
    key_list = jax.random.split(jax.random.key(seed), 6)
    state = jnp.clip(1.0 * jax.random.uniform(key_list[0], (N_ROLE, 2, PLANES, NY, NZ), jnp.float32) ** level_of(key_list[0], (N_ROLE, 2, PLANES, NY, NZ), ((0, 2), (3, 32), (4, 4)), -0.2, 0.2), 0.0, 1.0)
    embed = normal_values(key_list[1], (N_ROLE, D, P_SIZE), P_SIZE ** -0.5, 0.09375, ((0, 2), (1, 32), (2, 4)))
    mlp = normal_values(key_list[2], (N_ROLE, 2, D, FF), D ** -0.5, 0.1875, ((0, 2), (2, 32), (3, 4)))
    mom_embed = normal_values(key_list[3], (N_ROLE, D, P_SIZE), 1.0, 6.0, ((0, 2), (1, 32), (2, 4)), jnp.float32)
    mom_mlp = normal_values(key_list[4], (N_ROLE, 2, D, FF), 1.0, 6.0, ((0, 2), (2, 32), (3, 4)), jnp.float32)
    return dict(state=state, embed=embed, mlp=mlp, mom_embed=mom_embed, mom_mlp=mom_mlp)


SUBSTRATE_DIFFUSION = 0.2
CATALYST_DIFFUSION = 0.1
FEED_RATE = 0.037
KILL_RATE = 0.06
TIME_STEP = 0.8
GELU_FACTOR = 0.7978845608028654
MOMENTUM_DECAY = 0.9
LEARNING_RATE = 0.003

def react(padded):
    center = padded[:, :, 1:-1, 1:-1]
    below_plane = jnp.concatenate([center[:, :1], center[:, :-1]], axis=1)
    above_plane = jnp.concatenate([center[:, 1:], center[:, -1:]], axis=1)
    beside = below_plane + above_plane + padded[:, :, :-2, 1:-1] + padded[:, :, 2:, 1:-1]
    beside = beside + padded[:, :, 1:-1, :-2] + padded[:, :, 1:-1, 2:]
    laplace = beside - 6.0 * center
    substrate = center[0]
    catalyst = center[1]
    growth = substrate * catalyst * catalyst
    new_substrate = substrate + TIME_STEP * (SUBSTRATE_DIFFUSION * laplace[0] - growth + FEED_RATE * (1.0 - substrate))
    new_catalyst = catalyst + TIME_STEP * (CATALYST_DIFFUSION * laplace[1] + growth - (FEED_RATE + KILL_RATE) * catalyst)
    return jnp.stack([new_substrate, new_catalyst])

def gelu_slope(preact):
    cubic = 0.044715 * preact * preact * preact
    tangent = jnp.tanh(GELU_FACTOR * (preact + cubic))
    return 0.5 * (1.0 + tangent) + 0.5 * preact * (1.0 - tangent * tangent) * GELU_FACTOR * (1.0 + 3.0 * 0.044715 * preact * preact)

def to_patches(brick):
    extent = brick.shape
    blocks = brick.reshape(extent[0], extent[1], extent[2] // PATCH, PATCH, extent[3] // PATCH, PATCH)
    blocks = blocks.transpose(2, 4, 0, 1, 3, 5)
    return blocks.reshape(extent[2] // PATCH * (extent[3] // PATCH), extent[0] * extent[1] * PATCH * PATCH)

def shard_terms(inputs, targets, embed_full, up_full, down_full, loss_scale):
    embedded = jnp.dot(inputs, embed_full.T, preferred_element_type=jnp.float32)
    recip = lax.rsqrt(lax.optimization_barrier(jnp.mean(embedded * embedded, axis=1, keepdims=True)) + 1e-06)
    normed = (embedded * recip).astype(jnp.bfloat16)
    hidden_pre = jnp.dot(normed, up_full, preferred_element_type=jnp.float32)
    active = jax.nn.gelu(hidden_pre, approximate=True).astype(jnp.bfloat16)
    branch = jnp.dot(active, down_full.T, preferred_element_type=jnp.float32)
    stream = (embedded + branch).astype(jnp.bfloat16)
    predicted = inputs.astype(jnp.float32) + jnp.dot(stream, embed_full, preferred_element_type=jnp.float32)
    residual_grad = ((predicted - targets.astype(jnp.float32)) * loss_scale).astype(jnp.bfloat16)
    stream_grad = jnp.dot(residual_grad, embed_full.T, preferred_element_type=jnp.float32)
    stream_sent = stream_grad.astype(jnp.bfloat16)
    hidden_grad = (jnp.dot(stream_sent, down_full, preferred_element_type=jnp.float32) * gelu_slope(hidden_pre)).astype(jnp.bfloat16)
    normed_grad = jnp.dot(hidden_grad, up_full.T, preferred_element_type=jnp.float32)
    embed_grad = stream_grad + recip * normed_grad - embedded * (recip * recip * recip) * lax.optimization_barrier(jnp.mean(normed_grad * embedded, axis=1, keepdims=True))
    embed_sent = embed_grad.astype(jnp.bfloat16)
    embed_term = jnp.dot(stream.T, residual_grad, preferred_element_type=jnp.float32) + jnp.dot(embed_sent.T, inputs, preferred_element_type=jnp.float32)
    up_term = jnp.dot(normed.T, hidden_grad, preferred_element_type=jnp.float32)
    down_term = jnp.dot(stream_sent.T, active, preferred_element_type=jnp.float32)
    return (embed_term, up_term, down_term)

def reference(state, embed, mlp, mom_embed, mom_mlp):
    cells = state[0]
    for iteration in range(STEPS):
        cells = react(jnp.pad(cells, ((0, 0), (0, 0), (1, 1), (1, 1)), mode='wrap'))
    inputs = to_patches(state[0].astype(jnp.bfloat16)).reshape(N_DP, ROWS, P_SIZE)
    targets = to_patches(cells.astype(jnp.bfloat16)).reshape(N_DP, ROWS, P_SIZE)
    embed_full = embed[1]
    up_full = mlp[1, 0]
    down_full = mlp[1, 1]
    loss_scale = float(NPATCH) ** (-0.5)

    def accumulate(totals, pair):
        terms = shard_terms(pair[0], pair[1], embed_full, up_full, down_full, loss_scale)
        return ((totals[0] + terms[0], totals[1] + terms[1], totals[2] + terms[2]), None)
    start = (jnp.zeros((D, P_SIZE), jnp.float32), jnp.zeros((D, FF), jnp.float32), jnp.zeros((D, FF), jnp.float32))
    grads, unused = lax.scan(accumulate, start, (inputs, targets))
    mom_embed_out = MOMENTUM_DECAY * mom_embed + grads[0][None]
    mom_mlp_out = MOMENTUM_DECAY * mom_mlp + jnp.stack([grads[1], grads[2]])[None]
    embed_out = (embed.astype(jnp.float32) - LEARNING_RATE * mom_embed_out).astype(jnp.bfloat16)
    mlp_out = (mlp.astype(jnp.float32) - LEARNING_RATE * mom_mlp_out).astype(jnp.bfloat16)
    return (cells, embed_out, mlp_out, mom_embed_out, mom_mlp_out)
```

```python
import jax
import jax.numpy as jnp
from jax import lax
from jax.experimental import pallas as pl
from jax.experimental.pallas import tpu as pltpu
from jax.sharding import PartitionSpec as P

PATCH = 16
STEPS = 4


SUBSTRATE_DIFFUSION = 0.2
CATALYST_DIFFUSION = 0.1
FEED_RATE = 0.037
KILL_RATE = 0.06
TIME_STEP = 0.8
GELU_FACTOR = 0.7978845608028654
MOMENTUM_DECAY = 0.9
LEARNING_RATE = 0.003

BF16 = jnp.bfloat16
F32 = jnp.float32
MESH = pl.DeviceIdType.MESH
ROWS = 128
OWN = 32
D = 1024
COLS = 1024
E, U, W = 0, 1, 2


def extended(cells, sides, width):
    for axis, dim in sides:
        count = lax.axis_size(axis)
        head = lax.slice_in_dim(cells, 0, width, axis=dim)
        tail = lax.slice_in_dim(cells, cells.shape[dim] - width, cells.shape[dim], axis=dim)
        cells = jnp.concatenate(
            [
                lax.ppermute(tail, axis, [(i, (i + 1) % count) for i in range(count)]),
                cells,
                lax.ppermute(head, axis, [((i + 1) % count, i) for i in range(count)]),
            ],
            axis=dim,
        )
    return cells


def react(padded):
    center = padded[:, :, 1:-1, 1:-1]
    below_plane = jnp.concatenate([center[:, :1], center[:, :-1]], axis=1)
    above_plane = jnp.concatenate([center[:, 1:], center[:, -1:]], axis=1)
    beside = below_plane + above_plane + padded[:, :, :-2, 1:-1] + padded[:, :, 2:, 1:-1]
    beside = beside + padded[:, :, 1:-1, :-2] + padded[:, :, 1:-1, 2:]
    laplace = beside - 6.0 * center
    substrate = center[0]
    catalyst = center[1]
    growth = substrate * catalyst * catalyst
    new_substrate = substrate + TIME_STEP * (
        SUBSTRATE_DIFFUSION * laplace[0] - growth + FEED_RATE * (1.0 - substrate)
    )
    new_catalyst = catalyst + TIME_STEP * (
        CATALYST_DIFFUSION * laplace[1] + growth - (FEED_RATE + KILL_RATE) * catalyst
    )
    return jnp.stack([new_substrate, new_catalyst])


def to_blocks(brick):
    extent = brick.shape
    parts = brick.reshape(
        extent[0], 2, extent[1] // 2, extent[2] // PATCH, PATCH, extent[3] // PATCH, PATCH
    )
    parts = parts.transpose(0, 1, 3, 5, 2, 4, 6)
    return parts.reshape(4, OWN, COLS)


def advance(cells):
    padded = extended(cells, (("dp", 2), ("mp", 3)), STEPS)
    for iteration in range(STEPS):
        padded = react(padded)
    return padded


def kernel(
    xs, ts, w, out,
    wf, px, yd, tg, part, sbuf, rbuf, nf, dyf, act, slope, dhid, ered, dyred,
    acc, cs, cr, xs1, xr1, xs2, xr2, vsum, zs1, zr1, zs2, zr2,
    role_s, role_r, x_s, x_r, ag_s, ag_r, rs_s, rs_r, mg_s, mg_r, gr_s, gr_r,
):
    role = lax.axis_index("role")
    dp = lax.axis_index("dp")
    mp = lax.axis_index("mp")
    x, z, c = dp // 8, (dp // 2) % 4, dp % 2

    def dev(x_, z_, c_):
        return {"dp": (x_ * 4 + z_) * 2 + c_}

    x1, x2, x3 = x + 1 - 2 * (x % 2), (x + 2) % 4, 3 - x
    z1, z2 = z + 1 - 2 * (z % 2), (z + 2) % 4
    z3 = (z1 + 2) % 4
    c1 = 1 - c
    to_c, to_x1, to_x3 = dev(x, z, c1), dev(x1, z, c), dev(x3, z, c)
    to_z1, to_z2 = dev(x, z1, c), dev(x, z2, c)
    other = [(mp + o) % 4 for o in range(4)]

    def at(start, size):
        return pl.ds(pl.multiple_of(start, 32), size)

    barrier = pltpu.get_barrier_semaphore()
    friends = [to_c, to_x1, to_x3, to_z1, to_z2]
    friends += [{"mp": other[o]} for o in (1, 2, 3)]
    friends += [{"role": 1 - role, "mp": other[o]} for o in range(4)]
    for friend in friends:
        pl.semaphore_signal(barrier, inc=1, device_id=friend, device_id_type=MESH)
    pl.semaphore_wait(barrier, len(friends))

    started = []

    def copy(src, dst, ssem, rsem, to):
        return pltpu.make_async_remote_copy(
            src_ref=src, dst_ref=dst, send_sem=ssem, recv_sem=rsem, device_id=to, device_id_type=MESH
        )

    def send(src, dst, ssem, rsem, to):
        made = copy(src, dst, ssem, rsem, to)
        made.start()
        started.append(made)

    def arrive(dst, ssem, rsem, frm):
        copy(dst, dst, ssem, rsem, frm).wait_recv()

    own_rows = at(c * 512 + x * 128 + z * 32, 32)

    def weights_across(k):
        return copy(w.at[k], wf.at[k, own_rows], role_s.at[k], role_r.at[k], {"role": 0})

    def weights_here(k):
        return pltpu.make_async_copy(w.at[k], wf.at[k, own_rows], role_r.at[k])

    def patches(which, src, dst, base):
        made = []
        for o in range(4):
            rows = at(base + 32 * mp, 32)
            for r in (1, 0):
                if o == 0 and r == 0:
                    continue
                made.append(
                    copy(src.at[other[o]], dst.at[rows], x_s.at[which, r, o], x_r.at[which, o],
                         {"role": r, "mp": other[o]})
                )
        return made

    def patches_here(which, src, dst, base):
        return pltpu.make_async_copy(src.at[mp], dst.at[at(base + 32 * mp, 32)], x_r.at[which, 0])

    @pl.when(role == 1)
    def _():
        for k in (E, U, W):
            weights_across(k).start()
            weights_here(k).start()

    @pl.when(role == 0)
    def _():
        for made in patches(0, xs, px, 128):
            made.start()
        patches_here(0, xs, px, 128).start()
        for made in patches(1, ts, tg, 0):
            made.start()
        patches_here(1, ts, tg, 0).start()

    def patches_arrive(which, dst, base):
        for o in range(4):
            frm = (mp + 4 - o) % 4
            arrive(dst.at[at(base + 32 * frm, 32)], x_s.at[which, 1, o], x_r.at[which, o], {"mp": other[1]})

    def block(x_, z_=0, c_=c):
        return c_ * 512 + x_ * 128 + z_ * 32

    def g_send(k, i, start, size, to):
        rows = at(start, size)
        send(wf.at[k, rows], wf.at[k, rows], ag_s.at[k, i], ag_r.at[k, i], to)

    def g_arrive(k, i, start, size, frm):
        arrive(wf.at[k, at(start, size)], ag_s.at[k, i], ag_r.at[k, i], frm)

    def gather0(k):
        arrive(wf.at[k, own_rows], role_s.at[k], role_r.at[k], {"role": 1 - role})
        g_send(k, 0, block(x, z), 32, to_z2)
        g_send(k, 1, block(x, z), 32, to_z1)

    def gather1(k):
        g_arrive(k, 0, block(x, z2), 32, to_z2)
        g_send(k, 2, block(x, z2), 32, to_z1)

    def gather2(k):
        g_arrive(k, 1, block(x, z1), 32, to_z1)
        g_arrive(k, 2, block(x, z3), 32, to_z1)
        g_send(k, 3, block(x), 128, to_x1)
        g_send(k, 4, block(x), 128, to_x3)
        g_send(k, 7, block(x), 128, to_c)

    def gather3(k):
        g_arrive(k, 3, block(x1), 128, to_x1)
        g_send(k, 5, block(x1), 64, to_x3)
        g_send(k, 8, block(x1), 128, to_c)
        g_arrive(k, 4, block(x3), 128, to_x3)
        g_send(k, 6, block(x3) + 64, 64, to_x1)
        g_send(k, 9, block(x3), 128, to_c)

    def gather4(k):
        g_arrive(k, 5, block(x2), 64, to_x3)
        g_send(k, 10, block(x2), 64, to_c)
        g_arrive(k, 6, block(x2) + 64, 64, to_x1)
        g_send(k, 11, block(x2) + 64, 64, to_c)

    def gather5(k):
        g_arrive(k, 7, block(x, 0, c1), 128, to_c)
        g_arrive(k, 8, block(x1, 0, c1), 128, to_c)
        g_arrive(k, 9, block(x3, 0, c1), 128, to_c)
        g_arrive(k, 10, block(x2, 0, c1), 64, to_c)
        g_arrive(k, 11, block(x2, 0, c1) + 64, 64, to_c)

    def tiles(width, body):
        @pl.loop(0, COLS // width)
        def _(t):
            body(pl.ds(pl.multiple_of(t * width, width), width))

    def with_rows(lhs, k, rows):
        return lax.dot_general(lhs, wf[k, rows, :], (((1,), (1,)), ((), ())), preferred_element_type=F32)

    def with_cols(lhs, k, cols):
        return jnp.dot(lhs, wf[k, :, cols], preferred_element_type=F32)

    mine = at(32 * mp, 32)

    def partial_sums(i, lhs, k):
        def body(cols):
            value = with_rows(lhs[...], k, cols)
            part[:, cols] = value
            sbuf[i, :, cols] = value.astype(BF16)

        tiles(256, body)
        for o in (2, 1, 3):
            send(sbuf.at[i, at(32 * other[o], 32)], rbuf.at[i, o - 1], rs_s.at[i, o - 1], rs_r.at[i, o - 1],
                 {"mp": other[o]})

    def summed(i):
        total = part[mine, :]
        for o in (1, 3, 2):
            arrive(rbuf.at[i, o - 1], rs_s.at[i, o - 1], rs_r.at[i, o - 1], {"mp": other[o]})
            total = total + rbuf[i, o - 1].astype(F32)
        return total

    def spread(i, dst, base, value):
        rows = at(base + 32 * mp, 32)
        dst[rows, :] = value
        for o in (2, 1, 3):
            send(dst.at[rows], dst.at[rows], mg_s.at[i, o - 1], mg_r.at[i, o - 1], {"mp": other[o]})

    def spread_arrive(i, dst, base):
        for o in (1, 3, 2):
            rows = at(base + 32 * ((mp + 4 - o) % 4), 32)
            arrive(dst.at[rows], mg_s.at[i, o - 1], mg_r.at[i, o - 1], {"mp": other[o]})

    def terms(k, lhs, rhs):
        def product(rows, cols):
            return lax.dot_general(lhs[:, rows], rhs[:, cols], (((0,), (0,)), ((), ())), preferred_element_type=F32)

        @pl.loop(0, 2)
        def _(t):
            rows = pl.ds(pl.multiple_of(c1 * 512 + t * 256, 256), 256)
            for s in (0, 1):
                cols = pl.ds(512 * s, 512)
                cs[k, pl.ds(pl.multiple_of(t * 256, 256), 256), cols] = product(rows, cols).astype(BF16)

        send(cs.at[k], cr.at[k], gr_s.at[k, 0], gr_r.at[k, 0], to_c)

        @pl.loop(0, 2)
        def _(t):
            rows = pl.ds(pl.multiple_of(c * 512 + t * 256, 256), 256)
            for s in (0, 1):
                cols = pl.ds(512 * s, 512)
                acc[k, pl.ds(pl.multiple_of(t * 256, 256), 256), cols] = product(rows, cols)

    def chunks(count, body):
        @pl.loop(0, count)
        def _(t):
            body(pl.multiple_of(t * 32, 32))

    def pair(k, start):
        return acc[k, pl.ds(start, 32), :] + cr[k, pl.ds(start, 32), :].astype(F32)

    def reduce1(k):
        arrive(cr.at[k], gr_s.at[k, 0], gr_r.at[k, 0], to_c)

        def body(t):
            for h, far in ((0, x3), (1, x1)):
                for i, xb in ((0, far), (1, x2)):
                    xs1[k, h, i, pl.ds(t, 32), :] = pair(k, pl.multiple_of(xb * 128 + h * 64 + t, 32)).astype(BF16)

        chunks(2, body)
        send(xs1.at[k, 0], xr1.at[k, 0], gr_s.at[k, 1], gr_r.at[k, 1], to_x3)
        send(xs1.at[k, 1], xr1.at[k, 1], gr_s.at[k, 2], gr_r.at[k, 2], to_x1)

    def reduce2(k):
        arrive(xr1.at[k, 0], gr_s.at[k, 1], gr_r.at[k, 1], to_x3)
        arrive(xr1.at[k, 1], gr_s.at[k, 2], gr_r.at[k, 2], to_x1)

        def body(t):
            for h, near in ((0, x1), (1, x3)):
                value = pair(k, pl.multiple_of(near * 128 + h * 64 + t, 32)) + xr1[k, h, 1, pl.ds(t, 32), :].astype(F32)
                xs2[k, h, pl.ds(t, 32), :] = value.astype(BF16)

        chunks(2, body)
        send(xs2.at[k, 0], xr2.at[k, 0], gr_s.at[k, 3], gr_r.at[k, 3], to_x1)
        send(xs2.at[k, 1], xr2.at[k, 1], gr_s.at[k, 4], gr_r.at[k, 4], to_x3)

    def reduce3(k):
        arrive(xr2.at[k, 0], gr_s.at[k, 3], gr_r.at[k, 3], to_x1)
        arrive(xr2.at[k, 1], gr_s.at[k, 4], gr_r.at[k, 4], to_x3)

        def body(t):
            for h in (0, 1):
                value = pair(k, pl.multiple_of(x * 128 + h * 64 + t, 32))
                value = value + xr1[k, h, 0, pl.ds(t, 32), :].astype(F32) + xr2[k, h, pl.ds(t, 32), :].astype(F32)
                vsum[k, pl.ds(pl.multiple_of(h * 64 + t, 32), 32), :] = value

        chunks(2, body)
        zs1[k, 0] = vsum[k, at(z1 * 32, 32), :].astype(BF16)
        zs1[k, 1] = vsum[k, at(z3 * 32, 32), :].astype(BF16)
        send(zs1.at[k], zr1.at[k], gr_s.at[k, 5], gr_r.at[k, 5], to_z1)

    def reduce4(k):
        arrive(zr1.at[k], gr_s.at[k, 5], gr_r.at[k, 5], to_z1)
        zs2[k] = (vsum[k, at(z2 * 32, 32), :] + zr1[k, 1].astype(F32)).astype(BF16)
        send(zs2.at[k], zr2.at[k], gr_s.at[k, 6], gr_r.at[k, 6], to_z2)

    def reduce5(k):
        arrive(zr2.at[k], gr_s.at[k, 6], gr_r.at[k, 6], to_z2)
        out[k] = vsum[k, at(z * 32, 32), :] + zr1[k, 0].astype(F32) + zr2[k].astype(F32)

    for k in (E, U, W):
        gather0(k)
    gather1(E)
    gather2(E)
    gather1(U)
    gather1(W)
    gather3(E)
    gather2(U)
    gather4(E)
    gather5(E)

    patches_arrive(0, px, 128)
    xin = px.at[128:256]
    partial_sums(0, xin, E)
    gather2(W)
    gather3(U)
    e = summed(0)
    recip = lax.rsqrt(jnp.mean(e * e, axis=1, keepdims=True) + 1e-06)
    ered[...] = e
    spread(0, nf, 0, (e * recip).astype(BF16))
    gather4(U)
    gather3(W)
    gather5(U)
    spread_arrive(0, nf, 0)

    def hidden(cols):
        pre = with_cols(nf[...], U, cols)
        square = pre * pre
        tangent = jnp.tanh(GELU_FACTOR * (pre + 0.044715 * square * pre))
        act[:, cols] = (0.5 * pre * (1.0 + tangent)).astype(BF16)
        slope[:, cols] = 0.5 * (1.0 + tangent) + 0.5 * pre * (1.0 - tangent * tangent) * GELU_FACTOR * (
            1.0 + 3.0 * 0.044715 * square
        )

    tiles(256, hidden)
    gather4(W)
    gather5(W)
    partial_sums(1, act, W)
    spread(1, yd, 0, (ered[...] + summed(1)).astype(BF16))
    patches_arrive(1, tg, 0)
    spread_arrive(1, yd, 0)

    def residual(cols):
        pred = px[128:256, cols].astype(F32) + with_cols(yd[0:128, :], E, cols)
        px[0:128, cols] = ((pred - tg[:, cols].astype(F32)) * (1.0 / 64.0)).astype(BF16)

    tiles(256, residual)
    partial_sums(2, px.at[0:128], E)
    dy = summed(2)
    dyred[...] = dy
    spread(2, dyf, 0, dy.astype(BF16))
    spread_arrive(2, dyf, 0)

    def hidden_back(cols):
        dhid[:, cols] = (with_cols(dyf[...], W, cols) * slope[:, cols]).astype(BF16)

    tiles(256, hidden_back)
    partial_sums(3, dhid, U)
    terms(W, dyf, act)
    dn = summed(3)
    e = ered[...]
    recip = lax.rsqrt(jnp.mean(e * e, axis=1, keepdims=True) + 1e-06)
    de = dyred[...] + recip * dn - e * (recip * recip * recip) * jnp.mean(dn * e, axis=1, keepdims=True)
    spread(3, yd, 128, de.astype(BF16))
    reduce1(W)
    terms(U, nf, dhid)
    spread_arrive(3, yd, 128)
    terms(E, yd, px)
    reduce1(U)
    reduce2(W)
    reduce1(E)
    reduce2(U)
    reduce3(W)
    reduce2(E)
    reduce3(U)
    reduce4(W)
    reduce3(E)
    reduce4(U)
    reduce5(W)
    reduce4(E)
    reduce5(U)
    reduce5(E)

    for made in started:
        made.wait_send()

    @pl.when(role == 1)
    def _():
        for k in (E, U, W):
            weights_across(k).wait_send()

    @pl.when(role == 0)
    def _():
        for made in patches(0, xs, px, 128) + patches(1, ts, tg, 0):
            made.wait_send()


def gradients(xs, ts, w):
    vmem = pl.BlockSpec(memory_space=pltpu.VMEM)
    dma = pltpu.SemaphoreType.DMA
    return pl.pallas_call(
        kernel,
        name="train",
        out_shape=jax.ShapeDtypeStruct((3, OWN, COLS), F32),
        in_specs=[vmem] * 3,
        out_specs=vmem,
        scratch_shapes=[
            pltpu.VMEM((3, D, COLS), BF16),
            pltpu.VMEM((2 * ROWS, COLS), BF16),
            pltpu.VMEM((2 * ROWS, D), BF16),
            pltpu.VMEM((ROWS, COLS), BF16),
            pltpu.VMEM((ROWS, D), F32),
            pltpu.VMEM((4, ROWS, D), BF16),
            pltpu.VMEM((4, 3, OWN, D), BF16),
            pltpu.VMEM((ROWS, D), BF16),
            pltpu.VMEM((ROWS, D), BF16),
            pltpu.VMEM((ROWS, COLS), BF16),
            pltpu.VMEM((ROWS, COLS), F32),
            pltpu.VMEM((ROWS, COLS), BF16),
            pltpu.VMEM((OWN, D), F32),
            pltpu.VMEM((OWN, D), F32),
            pltpu.VMEM((3, 512, COLS), F32),
            pltpu.VMEM((3, 512, COLS), BF16),
            pltpu.VMEM((3, 512, COLS), BF16),
            pltpu.VMEM((3, 2, 2, 64, COLS), BF16),
            pltpu.VMEM((3, 2, 2, 64, COLS), BF16),
            pltpu.VMEM((3, 2, 64, COLS), BF16),
            pltpu.VMEM((3, 2, 64, COLS), BF16),
            pltpu.VMEM((3, 128, COLS), F32),
            pltpu.VMEM((3, 2, OWN, COLS), BF16),
            pltpu.VMEM((3, 2, OWN, COLS), BF16),
            pltpu.VMEM((3, OWN, COLS), BF16),
            pltpu.VMEM((3, OWN, COLS), BF16),
            dma((3,)), dma((3,)),
            dma((2, 2, 4)), dma((2, 4)),
            dma((3, 12)), dma((3, 12)),
            dma((4, 3)), dma((4, 3)),
            dma((4, 3)), dma((4, 3)),
            dma((3, 7)), dma((3, 7)),
        ],
        compiler_params=pltpu.CompilerParams(
            collective_id=0, has_side_effects=True, vmem_limit_bytes=52 * 1024 * 1024
        ),
        cost_estimate=pl.CostEstimate(flops=6 * 10**9, bytes_accessed=4 * 10**8, transcendentals=10**5),
    )(xs, ts, w)


def shards(state, embed, mlp, mom_embed, mom_mlp):
    group_index = lax.axis_index("role")
    start_cells = state[0]
    cells = advance(start_cells)
    arrived = lax.ppermute(cells, "role", [(0, 1)])
    state_out = jnp.where(group_index == 0, cells, arrived)
    grads = gradients(
        to_blocks(start_cells.astype(BF16)),
        to_blocks(cells.astype(BF16)),
        jnp.concatenate([embed, mlp[0]], axis=0),
    )
    mom_embed_out = MOMENTUM_DECAY * mom_embed + grads[:1]
    mom_mlp_out = MOMENTUM_DECAY * mom_mlp + grads[None, 1:]
    embed_out = (embed.astype(F32) - LEARNING_RATE * mom_embed_out).astype(BF16)
    mlp_out = (mlp.astype(F32) - LEARNING_RATE * mom_mlp_out).astype(BF16)
    return (state_out, embed_out, mlp_out, mom_embed_out, mom_mlp_out)


def solution(mesh):
    placed = (
        P("role", None, None, "dp", "mp"),
        P("role", "dp", "mp"),
        P("role", None, "dp", "mp"),
        P("role", "dp", "mp"),
        P("role", None, "dp", "mp"),
    )
    return jax.shard_map(
        shards,
        mesh=mesh,
        in_specs=placed,
        out_specs=(
            P(None, None, "dp", "mp"),
            P("role", "dp", "mp"),
            P("role", None, "dp", "mp"),
            P("role", "dp", "mp"),
            P("role", None, "dp", "mp"),
        ),
        check_vma=False,
    )
```

```python
import jax
import jax.numpy as jnp
from jax import lax
from jax.experimental import pallas as pl
from jax.experimental.pallas import tpu as pltpu
from jax.sharding import PartitionSpec as P

PATCH = 16
STEPS = 4


SUBSTRATE_DIFFUSION = 0.2
CATALYST_DIFFUSION = 0.1
FEED_RATE = 0.037
KILL_RATE = 0.06
TIME_STEP = 0.8
GELU_FACTOR = 0.7978845608028654
MOMENTUM_DECAY = 0.9
LEARNING_RATE = 0.003

BF16 = jnp.bfloat16
F32 = jnp.float32
MESH = pl.DeviceIdType.MESH
ROWS = 128
OWN = 32
D = 1024
COLS = 1024
E, U, W = 0, 1, 2


def kernel(
    state, embed, mlp, out, state_out,
    field, edge, edges, onehot, spread_in, xs, ts, wf, px, yd, tg, part, sbuf, rbuf, nf, dyf, act, slope, dhid, ered, dyred,
    acc, cs, cr, xs1, xr1, xs2, xr2, vsum, zs1, zr1, zs2, zr2,
    in_s, halo_s, halo_r, state_s, state_r, role_s, role_r, x_s, x_r, ag_s, ag_r, rs_s, rs_r, mg_s, mg_r, gr_s, gr_r,
):
    role = lax.axis_index("role")
    dp = lax.axis_index("dp")
    mp = lax.axis_index("mp")
    x, z, c = dp // 8, (dp // 2) % 4, dp % 2

    def dev(x_, z_, c_):
        return {"dp": (x_ * 4 + z_) * 2 + c_}

    x1, x2, x3 = x + 1 - 2 * (x % 2), (x + 2) % 4, 3 - x
    z1, z2 = z + 1 - 2 * (z % 2), (z + 2) % 4
    z3 = (z1 + 2) % 4
    c1 = 1 - c
    zm = 3 - z
    zl = jnp.where(role == 1, z, zm)
    to_c, to_x1, to_x3 = dev(x, z, c1), dev(x1, z, c), dev(x3, z, c)
    to_z1, to_z2 = dev(x, z1, c), dev(x, z2, c)
    after, before = {"dp": (dp + 1) % 32}, {"dp": (dp + 31) % 32}
    east, west = {"mp": (mp + 1) % 4}, {"mp": (mp + 3) % 4}
    mirror = dev(x, zm, c)["dp"]
    center = pltpu.make_async_copy(
        state.at[0], field.at[0, :, :, pl.ds(8, 64), pl.ds(0, 128)], in_s.at[0]
    )
    center.start()
    other = [(mp + o) % 4 for o in range(4)]

    def at(start, size):
        return pl.ds(pl.multiple_of(start, 32), size)

    barrier = pltpu.get_barrier_semaphore()
    friends = [to_c, to_x1, to_x3, to_z1, to_z2, after, before, {"role": 1 - role}]
    friends += [{"mp": other[o]} for o in (1, 2, 3)]
    friends += [{"role": 1 - role, "dp": mirror, "mp": other[o]} for o in range(4)]
    for friend in friends:
        pl.semaphore_signal(barrier, inc=1, device_id=friend, device_id_type=MESH)
    pl.semaphore_wait(barrier, len(friends))

    started = []

    def copy(src, dst, ssem, rsem, to):
        return pltpu.make_async_remote_copy(
            src_ref=src, dst_ref=dst, send_sem=ssem, recv_sem=rsem, device_id=to, device_id_type=MESH
        )

    def send(src, dst, ssem, rsem, to):
        made = copy(src, dst, ssem, rsem, to)
        made.start()
        started.append(made)

    def arrive(dst, ssem, rsem, frm):
        copy(dst, dst, ssem, rsem, frm).wait_recv()

    own_rows = at(c * 512 + x * 128 + zl * 32, 32)
    far_rows = at(c * 512 + x * 128 + z * 32, 32)
    w = (embed.at[0], mlp.at[0, 0], mlp.at[0, 1])

    def weights_across(k):
        return copy(w[k], wf.at[k, far_rows], role_s.at[k], role_r.at[k], {"role": 0, "dp": mirror})

    def weights_here(k):
        return pltpu.make_async_copy(w[k], wf.at[k, far_rows], role_r.at[k])

    def patches(which, src, dst, base, o):
        rows = at(base + 32 * mp, 32)
        made = []
        for r in (1, 0):
            if o == 0 and r == 0:
                continue
            to = {"role": 1, "dp": mirror, "mp": other[o]} if r == 1 else {"role": 0, "mp": other[o]}
            made.append(copy(src.at[other[o]], dst.at[rows], x_s.at[which, r, o], x_r.at[which, o], to))
        return made

    def patches_here(which, src, dst, base):
        return pltpu.make_async_copy(src.at[mp], dst.at[at(base + 32 * mp, 32)], x_r.at[which, 0])

    def patches_go(which, src, dst, base):
        @pl.when(role == 0)
        def _():
            for o in range(4):
                for made in patches(which, src, dst, base, o):
                    made.start()
            patches_here(which, src, dst, base).start()

    def final_state():
        return copy(state_out, state_out, state_s.at[0], state_r.at[0], {"role": 1})

    @pl.when(role == 1)
    def _():
        for k in (E, U, W):
            weights_across(k).start()
            weights_here(k).start()

    def patches_arrive(which, dst, base):
        for o in range(4):
            frm = (mp + 4 - o) % 4
            arrive(dst.at[at(base + 32 * frm, 32)], x_s.at[which, 1, o], x_r.at[which, o], east)

    lane = lax.broadcasted_iota(jnp.int32, (80, 128), 1)

    def halo_rows(i, src, dst, to):
        ends = [field.at[0, :, :, pl.ds(start, 8), pl.ds(0, 128)] for start in (src, dst)]
        return copy(ends[0], ends[1], halo_s.at[i], halo_r.at[i], to)

    def rows_go():
        for i, src, dst, to in ((0, 8, 72, before), (1, 64, 0, after)):
            halo_rows(i, src, dst, to).start()

    def columns_go():
        halo_rows(0, 72, 72, after).wait_recv()
        halo_rows(1, 0, 0, before).wait_recv()
        halo_rows(0, 8, 72, before).wait_send()
        halo_rows(1, 64, 0, after).wait_send()
        edge[...] = jnp.zeros_like(edge)
        for p in range(16):
            cells = field[0, p // 8, p % 8, :, 0:128]
            inside = (lane >= 4 * p) & (lane < 4 * p + 4)
            edge[0] = jnp.where(inside, pltpu.roll(cells, 4 * p, 1) if p else cells, edge[0])
            edge[1] = jnp.where(inside, pltpu.roll(cells, 4 * p + 4, 1), edge[1])
        send(edge.at[0], edges.at[0], halo_s.at[2], halo_r.at[2], west)
        send(edge.at[1], edges.at[1], halo_s.at[3], halo_r.at[3], east)

    def columns_arrive():
        arrive(edges.at[0], halo_s.at[2], halo_r.at[2], east)
        arrive(edges.at[1], halo_s.at[3], halo_r.at[3], west)
        for p in range(16):
            behind = edges[0] if p == 0 else pltpu.roll(edges[0], 128 - 4 * p, 1)
            ahead = pltpu.roll(edges[1], 124 - 4 * p, 1)
            field[0, p // 8, p % 8, :, 128:256] = jnp.where(lane < 4, behind, jnp.where(lane >= 124, ahead, 0.0))

    def advance(step):
        now, later = step % 2, (step + 1) % 2

        @pl.loop(0, 8)
        def _(p):
            low, high = jnp.maximum(p - 1, 0), jnp.minimum(p + 1, 7)

            def laplace(s):
                mid = field[now, s, p]
                total = field[now, s, low] + field[now, s, high]
                total = total + pltpu.roll(mid, 1, 0) + pltpu.roll(mid, 79, 0)
                total = total + pltpu.roll(mid, 1, 1) + pltpu.roll(mid, 255, 1)
                return mid, total - 6.0 * mid

            substrate, first = laplace(0)
            catalyst, second = laplace(1)
            growth = substrate * catalyst * catalyst
            field[later, 0, p] = substrate + TIME_STEP * (
                SUBSTRATE_DIFFUSION * first - growth + FEED_RATE * (1.0 - substrate)
            )
            field[later, 1, p] = catalyst + TIME_STEP * (
                CATALYST_DIFFUSION * second + growth - (FEED_RATE + KILL_RATE) * catalyst
            )

    def selection():
        feature = lax.broadcasted_iota(jnp.int32, (128, 256), 1)
        inner = lax.broadcasted_iota(jnp.int32, (128, 256), 0) % PATCH
        for r in range(PATCH):
            onehot[128 * r : 128 * r + 128, :] = jnp.where(feature == PATCH * r + inner, 1.0, 0.0).astype(BF16)

    def to_patches(dst):
        patch = lax.broadcasted_iota(jnp.int32, (8, 128), 0)
        own = lax.broadcasted_iota(jnp.int32, (8, 128), 1) // PATCH == patch

        @pl.loop(0, 4)
        def _(j):
            @pl.loop(0, 4)
            def _(q):
                species, plane = j // 2, 4 * (j % 2) + q
                for r in range(PATCH):
                    pieces = []
                    for by in range(4):
                        row = field[0, species, plane, pl.ds(8 + PATCH * by + r, 1), 0:128]
                        pieces.append(jnp.where(own, jnp.broadcast_to(row, (8, 128)), 0.0))
                    rows = pl.ds(pl.multiple_of(32 * q, 32), 32)
                    spread_in[rows, 128 * r : 128 * r + 128] = jnp.concatenate(pieces, axis=0).astype(BF16)

            moved = jnp.dot(spread_in[...], onehot[...], preferred_element_type=F32).astype(BF16)
            for q in range(4):
                dst[j, :, 256 * q : 256 * q + 256] = moved[32 * q : 32 * q + 32, :]

    def block(x_, z_=0, c_=c):
        return c_ * 512 + x_ * 128 + z_ * 32

    def g_send(k, i, start, size, to):
        rows = at(start, size)
        send(wf.at[k, rows], wf.at[k, rows], ag_s.at[k, i], ag_r.at[k, i], to)

    def g_arrive(k, i, start, size, frm):
        arrive(wf.at[k, at(start, size)], ag_s.at[k, i], ag_r.at[k, i], frm)

    zl1, zl2 = zl + 1 - 2 * (zl % 2), (zl + 2) % 4
    zl3 = (zl1 + 2) % 4

    def gather0(k):
        arrive(wf.at[k, own_rows], role_s.at[k], role_r.at[k], {"role": 1 - role})
        g_send(k, 0, block(x, zl), 32, to_z2)
        g_send(k, 1, block(x, zl), 32, to_z1)

    def gather1(k):
        g_arrive(k, 0, block(x, zl2), 32, to_z2)
        g_send(k, 2, block(x, zl2), 32, to_z1)

    def gather2(k):
        g_arrive(k, 1, block(x, zl1), 32, to_z1)
        g_arrive(k, 2, block(x, zl3), 32, to_z1)
        g_send(k, 3, block(x), 128, to_x1)
        g_send(k, 4, block(x), 128, to_x3)
        g_send(k, 7, block(x), 128, to_c)

    def gather3(k):
        g_arrive(k, 3, block(x1), 128, to_x1)
        g_send(k, 5, block(x1), 64, to_x3)
        g_send(k, 8, block(x1), 128, to_c)
        g_arrive(k, 4, block(x3), 128, to_x3)
        g_send(k, 6, block(x3) + 64, 64, to_x1)
        g_send(k, 9, block(x3), 128, to_c)

    def gather4(k):
        g_arrive(k, 5, block(x2), 64, to_x3)
        g_send(k, 10, block(x2), 64, to_c)
        g_arrive(k, 6, block(x2) + 64, 64, to_x1)
        g_send(k, 11, block(x2) + 64, 64, to_c)

    def gather5(k):
        g_arrive(k, 7, block(x, 0, c1), 128, to_c)
        g_arrive(k, 8, block(x1, 0, c1), 128, to_c)
        g_arrive(k, 9, block(x3, 0, c1), 128, to_c)
        g_arrive(k, 10, block(x2, 0, c1), 64, to_c)
        g_arrive(k, 11, block(x2, 0, c1) + 64, 64, to_c)

    def tiles(width, body):
        @pl.loop(0, COLS // width)
        def _(t):
            body(pl.ds(pl.multiple_of(t * width, width), width))

    def with_rows(lhs, k, rows):
        return lax.dot_general(lhs, wf[k, rows, :], (((1,), (1,)), ((), ())), preferred_element_type=F32)

    def with_cols(lhs, k, cols):
        return jnp.dot(lhs, wf[k, :, cols], preferred_element_type=F32)

    mine = at(32 * mp, 32)

    def partial_sums(i, lhs, k):
        def body(cols):
            value = with_rows(lhs[...], k, cols)
            part[:, cols] = value
            sbuf[i, :, cols] = value.astype(BF16)

        tiles(256, body)
        for o in (2, 1, 3):
            send(sbuf.at[i, at(32 * other[o], 32)], rbuf.at[i, o - 1], rs_s.at[i, o - 1], rs_r.at[i, o - 1],
                 {"mp": other[o]})

    def summed(i):
        total = part[mine, :]
        for o in (1, 3, 2):
            arrive(rbuf.at[i, o - 1], rs_s.at[i, o - 1], rs_r.at[i, o - 1], {"mp": other[o]})
            total = total + rbuf[i, o - 1].astype(F32)
        return total

    def spread(i, dst, base, value):
        rows = at(base + 32 * mp, 32)
        dst[rows, :] = value
        for o in (2, 1, 3):
            send(dst.at[rows], dst.at[rows], mg_s.at[i, o - 1], mg_r.at[i, o - 1], {"mp": other[o]})

    def spread_arrive(i, dst, base):
        for o in (1, 3, 2):
            rows = at(base + 32 * ((mp + 4 - o) % 4), 32)
            arrive(dst.at[rows], mg_s.at[i, o - 1], mg_r.at[i, o - 1], {"mp": other[o]})

    def terms(k, lhs, rhs):
        def product(rows, cols):
            return lax.dot_general(lhs[:, rows], rhs[:, cols], (((0,), (0,)), ((), ())), preferred_element_type=F32)

        @pl.loop(0, 2)
        def _(t):
            rows = pl.ds(pl.multiple_of(c1 * 512 + t * 256, 256), 256)
            for s in (0, 1):
                cols = pl.ds(512 * s, 512)
                cs[k, pl.ds(pl.multiple_of(t * 256, 256), 256), cols] = product(rows, cols).astype(BF16)

        send(cs.at[k], cr.at[k], gr_s.at[k, 0], gr_r.at[k, 0], to_c)

        @pl.loop(0, 2)
        def _(t):
            rows = pl.ds(pl.multiple_of(c * 512 + t * 256, 256), 256)
            for s in (0, 1):
                cols = pl.ds(512 * s, 512)
                acc[k, pl.ds(pl.multiple_of(t * 256, 256), 256), cols] = product(rows, cols)

    def chunks(count, body):
        @pl.loop(0, count)
        def _(t):
            body(pl.multiple_of(t * 32, 32))

    def pair(k, start):
        return acc[k, pl.ds(start, 32), :] + cr[k, pl.ds(start, 32), :].astype(F32)

    def reduce1(k):
        arrive(cr.at[k], gr_s.at[k, 0], gr_r.at[k, 0], to_c)

        def body(t):
            for h, far in ((0, x3), (1, x1)):
                for i, xb in ((0, far), (1, x2)):
                    xs1[k, h, i, pl.ds(t, 32), :] = pair(k, pl.multiple_of(xb * 128 + h * 64 + t, 32)).astype(BF16)

        chunks(2, body)
        send(xs1.at[k, 0], xr1.at[k, 0], gr_s.at[k, 1], gr_r.at[k, 1], to_x3)
        send(xs1.at[k, 1], xr1.at[k, 1], gr_s.at[k, 2], gr_r.at[k, 2], to_x1)

    def reduce2(k):
        arrive(xr1.at[k, 0], gr_s.at[k, 1], gr_r.at[k, 1], to_x3)
        arrive(xr1.at[k, 1], gr_s.at[k, 2], gr_r.at[k, 2], to_x1)

        def body(t):
            for h, near in ((0, x1), (1, x3)):
                value = pair(k, pl.multiple_of(near * 128 + h * 64 + t, 32)) + xr1[k, h, 1, pl.ds(t, 32), :].astype(F32)
                xs2[k, h, pl.ds(t, 32), :] = value.astype(BF16)

        chunks(2, body)
        send(xs2.at[k, 0], xr2.at[k, 0], gr_s.at[k, 3], gr_r.at[k, 3], to_x1)
        send(xs2.at[k, 1], xr2.at[k, 1], gr_s.at[k, 4], gr_r.at[k, 4], to_x3)

    def reduce3(k):
        arrive(xr2.at[k, 0], gr_s.at[k, 3], gr_r.at[k, 3], to_x1)
        arrive(xr2.at[k, 1], gr_s.at[k, 4], gr_r.at[k, 4], to_x3)

        def body(t):
            for h in (0, 1):
                value = pair(k, pl.multiple_of(x * 128 + h * 64 + t, 32))
                value = value + xr1[k, h, 0, pl.ds(t, 32), :].astype(F32) + xr2[k, h, pl.ds(t, 32), :].astype(F32)
                vsum[k, pl.ds(pl.multiple_of(h * 64 + t, 32), 32), :] = value

        chunks(2, body)
        zs1[k, 0] = vsum[k, at(z1 * 32, 32), :].astype(BF16)
        zs1[k, 1] = vsum[k, at(z3 * 32, 32), :].astype(BF16)
        send(zs1.at[k], zr1.at[k], gr_s.at[k, 5], gr_r.at[k, 5], to_z1)

    def reduce4(k):
        arrive(zr1.at[k], gr_s.at[k, 5], gr_r.at[k, 5], to_z1)
        zs2[k] = (vsum[k, at(z2 * 32, 32), :] + zr1[k, 1].astype(F32)).astype(BF16)
        send(zs2.at[k], zr2.at[k], gr_s.at[k, 6], gr_r.at[k, 6], to_z2)

    def reduce5(k):
        arrive(zr2.at[k], gr_s.at[k, 6], gr_r.at[k, 6], to_z2)
        out[k] = vsum[k, at(z * 32, 32), :] + zr1[k, 0].astype(F32) + zr2[k].astype(F32)

    center.wait()
    rows_go()
    gather0(E)
    selection()
    to_patches(xs)
    patches_go(0, xs, px, 128)
    gather1(E)
    gather0(U)
    columns_go()
    gather2(E)
    gather1(U)
    gather0(W)
    columns_arrive()
    gather3(E)
    advance(0)
    gather4(E)
    gather2(U)
    gather1(W)
    advance(1)
    gather5(E)

    patches_arrive(0, px, 128)
    xin = px.at[128:256]
    partial_sums(0, xin, E)
    gather2(W)
    gather3(U)
    advance(2)
    e = summed(0)
    recip = lax.rsqrt(jnp.mean(e * e, axis=1, keepdims=True) + 1e-06)
    ered[...] = e
    spread(0, nf, 0, (e * recip).astype(BF16))
    gather4(U)
    gather3(W)
    gather5(U)
    advance(3)
    spread_arrive(0, nf, 0)

    def hidden(cols):
        pre = with_cols(nf[...], U, cols)
        square = pre * pre
        tangent = jnp.tanh(GELU_FACTOR * (pre + 0.044715 * square * pre))
        act[:, cols] = (0.5 * pre * (1.0 + tangent)).astype(BF16)
        slope[:, cols] = 0.5 * (1.0 + tangent) + 0.5 * pre * (1.0 - tangent * tangent) * GELU_FACTOR * (
            1.0 + 3.0 * 0.044715 * square
        )

    tiles(256, hidden)
    gather4(W)
    gather5(W)
    partial_sums(1, act, W)
    to_patches(ts)
    patches_go(1, ts, tg, 0)

    @pl.when(role == 0)
    def _():
        state_out[...] = field[0, :, :, 8:72, 0:128]
        final_state().start()

    spread(1, yd, 0, (ered[...] + summed(1)).astype(BF16))
    patches_arrive(1, tg, 0)
    spread_arrive(1, yd, 0)

    def residual(cols):
        pred = px[128:256, cols].astype(F32) + with_cols(yd[0:128, :], E, cols)
        px[0:128, cols] = ((pred - tg[:, cols].astype(F32)) * (1.0 / 64.0)).astype(BF16)

    tiles(256, residual)
    partial_sums(2, px.at[0:128], E)
    dy = summed(2)
    dyred[...] = dy
    spread(2, dyf, 0, dy.astype(BF16))
    spread_arrive(2, dyf, 0)

    def hidden_back(cols):
        dhid[:, cols] = (with_cols(dyf[...], W, cols) * slope[:, cols]).astype(BF16)

    tiles(256, hidden_back)
    partial_sums(3, dhid, U)
    terms(W, dyf, act)
    dn = summed(3)
    e = ered[...]
    recip = lax.rsqrt(jnp.mean(e * e, axis=1, keepdims=True) + 1e-06)
    de = dyred[...] + recip * dn - e * (recip * recip * recip) * jnp.mean(dn * e, axis=1, keepdims=True)
    spread(3, yd, 128, de.astype(BF16))
    reduce1(W)
    terms(U, nf, dhid)
    spread_arrive(3, yd, 128)
    terms(E, yd, px)
    reduce1(U)
    reduce2(W)
    reduce1(E)
    reduce2(U)
    reduce3(W)
    reduce2(E)
    reduce3(U)
    reduce4(W)
    reduce3(E)
    reduce4(U)
    reduce5(W)
    reduce4(E)
    reduce5(U)
    reduce5(E)

    for made in started:
        made.wait_send()

    @pl.when(role == 1)
    def _():
        for k in (E, U, W):
            weights_across(k).wait_send()
        final_state().wait_recv()

    @pl.when(role == 0)
    def _():
        for o in range(4):
            for made in patches(0, xs, px, 128, o) + patches(1, ts, tg, 0, o):
                made.wait_send()
        final_state().wait_send()


def train(state, embed, mlp):
    vmem = pl.BlockSpec(memory_space=pltpu.VMEM)
    dma = pltpu.SemaphoreType.DMA
    return pl.pallas_call(
        kernel,
        name="train",
        out_shape=(jax.ShapeDtypeStruct((3, OWN, COLS), F32), jax.ShapeDtypeStruct(state.shape[1:], F32)),
        in_specs=[pl.BlockSpec(memory_space=pl.ANY), vmem, vmem],
        out_specs=(vmem, vmem),
        scratch_shapes=[
            pltpu.VMEM((2, 2, 8, 80, 256), F32),
            pltpu.VMEM((2, 80, 128), F32),
            pltpu.VMEM((2, 80, 128), F32),
            pltpu.VMEM((2048, 256), BF16),
            pltpu.VMEM((128, 2048), BF16),
            pltpu.VMEM((4, OWN, COLS), BF16),
            pltpu.VMEM((4, OWN, COLS), BF16),
            pltpu.VMEM((3, D, COLS), BF16),
            pltpu.VMEM((2 * ROWS, COLS), BF16),
            pltpu.VMEM((2 * ROWS, D), BF16),
            pltpu.VMEM((ROWS, COLS), BF16),
            pltpu.VMEM((ROWS, D), F32),
            pltpu.VMEM((4, ROWS, D), BF16),
            pltpu.VMEM((4, 3, OWN, D), BF16),
            pltpu.VMEM((ROWS, D), BF16),
            pltpu.VMEM((ROWS, D), BF16),
            pltpu.VMEM((ROWS, COLS), BF16),
            pltpu.VMEM((ROWS, COLS), F32),
            pltpu.VMEM((ROWS, COLS), BF16),
            pltpu.VMEM((OWN, D), F32),
            pltpu.VMEM((OWN, D), F32),
            pltpu.VMEM((3, 512, COLS), F32),
            pltpu.VMEM((3, 512, COLS), BF16),
            pltpu.VMEM((3, 512, COLS), BF16),
            pltpu.VMEM((3, 2, 2, 64, COLS), BF16),
            pltpu.VMEM((3, 2, 2, 64, COLS), BF16),
            pltpu.VMEM((3, 2, 64, COLS), BF16),
            pltpu.VMEM((3, 2, 64, COLS), BF16),
            pltpu.VMEM((3, 128, COLS), F32),
            pltpu.VMEM((3, 2, OWN, COLS), BF16),
            pltpu.VMEM((3, 2, OWN, COLS), BF16),
            pltpu.VMEM((3, OWN, COLS), BF16),
            pltpu.VMEM((3, OWN, COLS), BF16),
            dma((1,)), dma((4,)), dma((4,)), dma((1,)), dma((1,)),
            dma((3,)), dma((3,)),
            dma((2, 2, 4)), dma((2, 4)),
            dma((3, 12)), dma((3, 12)),
            dma((4, 3)), dma((4, 3)),
            dma((4, 3)), dma((4, 3)),
            dma((3, 7)), dma((3, 7)),
        ],
        compiler_params=pltpu.CompilerParams(
            collective_id=0, has_side_effects=True, vmem_limit_bytes=52 * 1024 * 1024
        ),
        cost_estimate=pl.CostEstimate(flops=6 * 10**9, bytes_accessed=4 * 10**8, transcendentals=10**5),
    )(state, embed, mlp)


def shards(state, embed, mlp, mom_embed, mom_mlp):
    grads, state_out = train(state, embed, mlp)
    mom_embed_out = MOMENTUM_DECAY * mom_embed + grads[:1]
    mom_mlp_out = MOMENTUM_DECAY * mom_mlp + grads[None, 1:]
    embed_out = (embed.astype(F32) - LEARNING_RATE * mom_embed_out).astype(BF16)
    mlp_out = (mlp.astype(F32) - LEARNING_RATE * mom_mlp_out).astype(BF16)
    return (state_out, embed_out, mlp_out, mom_embed_out, mom_mlp_out)


def solution(mesh):
    placed = (
        P("role", None, None, "dp", "mp"),
        P("role", "dp", "mp"),
        P("role", None, "dp", "mp"),
        P("role", "dp", "mp"),
        P("role", None, "dp", "mp"),
    )
    return jax.shard_map(
        shards,
        mesh=mesh,
        in_specs=placed,
        out_specs=(
            P(None, None, "dp", "mp"),
            P("role", "dp", "mp"),
            P("role", None, "dp", "mp"),
            P("role", "dp", "mp"),
            P("role", None, "dp", "mp"),
        ),
        check_vma=False,
    )
```

```python
import jax
import jax.numpy as jnp
from jax import lax
from jax.experimental import pallas as pl
from jax.experimental.pallas import tpu as pltpu
from jax.sharding import PartitionSpec as P

PATCH = 16
STEPS = 4


SUBSTRATE_DIFFUSION = 0.2
CATALYST_DIFFUSION = 0.1
FEED_RATE = 0.037
KILL_RATE = 0.06
TIME_STEP = 0.8
GELU_FACTOR = 0.7978845608028654
MOMENTUM_DECAY = 0.9
LEARNING_RATE = 0.003

BF16 = jnp.bfloat16
F32 = jnp.float32
MESH = pl.DeviceIdType.MESH
ROWS = 128
OWN = 32
D = 1024
COLS = 1024
E, U, W = 0, 1, 2


def kernel(
    state, embed, mlp, out, state_out,
    field, passed, edge, edges, onehot, spread_in, xs, ts, wf, px, yd, tg, part, sbuf, rbuf, nf, dyf, act, slope, dhid, ered, dyred,
    acc, cs, cr, xs1, xr1, xs2, xr2, vsum, zs1, zr1, zs2, zr2,
    in_s, halo_s, halo_r, state_s, state_r, role_s, role_r, x_s, x_r, ag_s, ag_r, rs_s, rs_r, mg_s, mg_r, gr_s, gr_r,
):
    role = lax.axis_index("role")
    dp = lax.axis_index("dp")
    mp = lax.axis_index("mp")
    x, z, c = dp // 8, (dp // 2) % 4, dp % 2

    def dev(x_, z_, c_):
        return {"dp": (x_ * 4 + z_) * 2 + c_}

    x1, x2, x3 = x + 1 - 2 * (x % 2), (x + 2) % 4, 3 - x
    z1, z2 = z + 1 - 2 * (z % 2), (z + 2) % 4
    z3 = (z1 + 2) % 4
    c1 = 1 - c
    zm = 3 - z
    zl = jnp.where(role == 1, z, zm)
    to_c, to_x1, to_x3 = dev(x, z, c1), dev(x1, z, c), dev(x3, z, c)
    to_z1, to_z2 = dev(x, z1, c), dev(x, z2, c)
    after, before = {"dp": (dp + 1) % 32}, {"dp": (dp + 31) % 32}
    east, west = {"mp": (mp + 1) % 4}, {"mp": (mp + 3) % 4}
    mirror = dev(x, zm, c)["dp"]
    center = pltpu.make_async_copy(
        state.at[0], field.at[0, :, :, pl.ds(8, 64), pl.ds(0, 128)], in_s.at[0]
    )
    center.start()
    other = [(mp + o) % 4 for o in range(4)]

    def at(start, size):
        return pl.ds(pl.multiple_of(start, 32), size)

    barrier = pltpu.get_barrier_semaphore()
    friends = [to_c, to_x1, to_x3, to_z1, to_z2, after, before, {"dp": mirror}]
    friends += [{"mp": other[o]} for o in (1, 2, 3)]
    friends += [{"role": 1 - role, "dp": mirror, "mp": other[o]} for o in range(4)]
    for friend in friends:
        pl.semaphore_signal(barrier, inc=1, device_id=friend, device_id_type=MESH)
    pl.semaphore_wait(barrier, len(friends))

    started = []

    def copy(src, dst, ssem, rsem, to):
        return pltpu.make_async_remote_copy(
            src_ref=src, dst_ref=dst, send_sem=ssem, recv_sem=rsem, device_id=to, device_id_type=MESH
        )

    def send(src, dst, ssem, rsem, to):
        made = copy(src, dst, ssem, rsem, to)
        made.start()
        started.append(made)

    def arrive(dst, ssem, rsem, frm):
        copy(dst, dst, ssem, rsem, frm).wait_recv()

    own_rows = at(c * 512 + x * 128 + zl * 32, 32)
    far_rows = at(c * 512 + x * 128 + z * 32, 32)
    w = (embed.at[0], mlp.at[0, 0], mlp.at[0, 1])

    def weights_across(k):
        return copy(w[k], wf.at[k, far_rows], role_s.at[k], role_r.at[k], {"role": 0, "dp": mirror})

    def weights_here(k):
        return pltpu.make_async_copy(w[k], wf.at[k, far_rows], role_r.at[k])

    def patches(which, src, dst, base, o):
        rows = at(base + 32 * mp, 32)
        made = []
        for r in (1, 0):
            if o == 0 and r == 0:
                continue
            to = {"role": 1, "dp": mirror, "mp": other[o]} if r == 1 else {"role": 0, "mp": other[o]}
            made.append(copy(src.at[other[o]], dst.at[rows], x_s.at[which, r, o], x_r.at[which, o], to))
        return made

    def patches_here(which, src, dst, base):
        return pltpu.make_async_copy(src.at[mp], dst.at[at(base + 32 * mp, 32)], x_r.at[which, 0])

    def patches_go(which, src, dst, base, some=(0, 1, 2, 3)):
        @pl.when(role == 0)
        def _():
            for o in some:
                for made in patches(which, src, dst, base, o):
                    made.start()
            if 0 in some:
                patches_here(which, src, dst, base).start()

    def state_part(whole, part):
        return whole.at[part // 2, pl.ds(4 * (part % 2), 4)]

    def state_across(part):
        return copy(state_part(state_out, part), state_part(passed, part), state_s.at[part], state_r.at[part],
                    {"role": 1, "dp": mirror})

    def state_home(part):
        return copy(state_part(passed, part), state_part(state_out, part), state_s.at[4 + part], state_r.at[4 + part],
                    {"dp": mirror})

    def state_go():
        @pl.when(role == 0)
        def _():
            state_out[...] = field[0, :, :, 8:72, 0:128]
            for part in range(4):
                state_across(part).start()

    def state_pass(part):
        @pl.when(role == 1)
        def _():
            state_across(part).wait_recv()
            state_home(part).start()

    @pl.when(role == 1)
    def _():
        weights_across(E).start()
        for k in (E, U, W):
            weights_here(k).start()

    def weights_go(k):
        @pl.when(role == 1)
        def _():
            weights_across(k).start()

    def patches_arrive(which, dst, base):
        for o in range(4):
            frm = (mp + 4 - o) % 4
            arrive(dst.at[at(base + 32 * frm, 32)], x_s.at[which, 1, o], x_r.at[which, o], east)

    lane = lax.broadcasted_iota(jnp.int32, (80, 128), 1)

    def halo_rows(i, src, dst, to):
        ends = [field.at[0, :, :, pl.ds(start, 8), pl.ds(0, 128)] for start in (src, dst)]
        return copy(ends[0], ends[1], halo_s.at[i], halo_r.at[i], to)

    def rows_go():
        for i, src, dst, to in ((0, 8, 72, before), (1, 64, 0, after)):
            halo_rows(i, src, dst, to).start()

    def columns_go():
        halo_rows(0, 72, 72, after).wait_recv()
        halo_rows(1, 0, 0, before).wait_recv()
        halo_rows(0, 8, 72, before).wait_send()
        halo_rows(1, 64, 0, after).wait_send()
        edge[...] = jnp.zeros_like(edge)
        for p in range(16):
            cells = field[0, p // 8, p % 8, :, 0:128]
            inside = (lane >= 4 * p) & (lane < 4 * p + 4)
            edge[0] = jnp.where(inside, pltpu.roll(cells, 4 * p, 1) if p else cells, edge[0])
            edge[1] = jnp.where(inside, pltpu.roll(cells, 4 * p + 4, 1), edge[1])
        send(edge.at[0], edges.at[0], halo_s.at[2], halo_r.at[2], west)
        send(edge.at[1], edges.at[1], halo_s.at[3], halo_r.at[3], east)

    def columns_arrive():
        arrive(edges.at[0], halo_s.at[2], halo_r.at[2], east)
        arrive(edges.at[1], halo_s.at[3], halo_r.at[3], west)
        for p in range(16):
            behind = edges[0] if p == 0 else pltpu.roll(edges[0], 128 - 4 * p, 1)
            ahead = pltpu.roll(edges[1], 124 - 4 * p, 1)
            field[0, p // 8, p % 8, :, 128:256] = jnp.where(lane < 4, behind, jnp.where(lane >= 124, ahead, 0.0))

    def advance(step):
        now, later = step % 2, (step + 1) % 2

        @pl.loop(0, 8)
        def _(p):
            low, high = jnp.maximum(p - 1, 0), jnp.minimum(p + 1, 7)

            def laplace(s):
                mid = field[now, s, p]
                total = field[now, s, low] + field[now, s, high]
                total = total + pltpu.roll(mid, 1, 0) + pltpu.roll(mid, 79, 0)
                total = total + pltpu.roll(mid, 1, 1) + pltpu.roll(mid, 255, 1)
                return mid, total - 6.0 * mid

            substrate, first = laplace(0)
            catalyst, second = laplace(1)
            growth = substrate * catalyst * catalyst
            field[later, 0, p] = substrate + TIME_STEP * (
                SUBSTRATE_DIFFUSION * first - growth + FEED_RATE * (1.0 - substrate)
            )
            field[later, 1, p] = catalyst + TIME_STEP * (
                CATALYST_DIFFUSION * second + growth - (FEED_RATE + KILL_RATE) * catalyst
            )

    def selection():
        feature = lax.broadcasted_iota(jnp.int32, (128, 256), 1)
        inner = lax.broadcasted_iota(jnp.int32, (128, 256), 0) % PATCH
        for r in range(PATCH):
            onehot[128 * r : 128 * r + 128, :] = jnp.where(feature == PATCH * r + inner, 1.0, 0.0).astype(BF16)

    def to_patches(dst):
        patch = lax.broadcasted_iota(jnp.int32, (8, 128), 0)
        own = lax.broadcasted_iota(jnp.int32, (8, 128), 1) // PATCH == patch

        @pl.loop(0, 4)
        def _(j):
            @pl.loop(0, 4)
            def _(q):
                species, plane = j // 2, 4 * (j % 2) + q
                for r in range(PATCH):
                    pieces = []
                    for by in range(4):
                        row = field[0, species, plane, pl.ds(8 + PATCH * by + r, 1), 0:128]
                        pieces.append(jnp.where(own, jnp.broadcast_to(row, (8, 128)), 0.0))
                    rows = pl.ds(pl.multiple_of(32 * q, 32), 32)
                    spread_in[rows, 128 * r : 128 * r + 128] = jnp.concatenate(pieces, axis=0).astype(BF16)

            moved = jnp.dot(spread_in[...], onehot[...], preferred_element_type=F32).astype(BF16)
            for q in range(4):
                dst[j, :, 256 * q : 256 * q + 256] = moved[32 * q : 32 * q + 32, :]

    def block(x_, z_=0, c_=c):
        return c_ * 512 + x_ * 128 + z_ * 32

    def g_send(k, i, start, size, to):
        rows = at(start, size)
        send(wf.at[k, rows], wf.at[k, rows], ag_s.at[k, i], ag_r.at[k, i], to)

    def g_arrive(k, i, start, size, frm):
        arrive(wf.at[k, at(start, size)], ag_s.at[k, i], ag_r.at[k, i], frm)

    zl1, zl2 = zl + 1 - 2 * (zl % 2), (zl + 2) % 4
    zl3 = (zl1 + 2) % 4

    def gather0(k):
        arrive(wf.at[k, own_rows], role_s.at[k], role_r.at[k], {"role": 1 - role})
        g_send(k, 0, block(x, zl), 32, to_z2)
        g_send(k, 1, block(x, zl), 32, to_z1)

    def gather1(k):
        g_arrive(k, 0, block(x, zl2), 32, to_z2)
        g_send(k, 2, block(x, zl2), 32, to_z1)

    def gather2(k):
        g_arrive(k, 1, block(x, zl1), 32, to_z1)
        g_arrive(k, 2, block(x, zl3), 32, to_z1)
        g_send(k, 3, block(x), 128, to_x1)
        g_send(k, 4, block(x), 128, to_x3)
        g_send(k, 7, block(x), 128, to_c)

    def gather3(k):
        g_arrive(k, 3, block(x1), 128, to_x1)
        g_send(k, 5, block(x1), 64, to_x3)
        g_send(k, 8, block(x1), 128, to_c)
        g_arrive(k, 4, block(x3), 128, to_x3)
        g_send(k, 6, block(x3) + 64, 64, to_x1)
        g_send(k, 9, block(x3), 128, to_c)

    def gather4(k):
        g_arrive(k, 5, block(x2), 64, to_x3)
        g_send(k, 10, block(x2), 64, to_c)
        g_arrive(k, 6, block(x2) + 64, 64, to_x1)
        g_send(k, 11, block(x2) + 64, 64, to_c)

    def gather5(k):
        g_arrive(k, 7, block(x, 0, c1), 128, to_c)
        g_arrive(k, 8, block(x1, 0, c1), 128, to_c)
        g_arrive(k, 9, block(x3, 0, c1), 128, to_c)
        g_arrive(k, 10, block(x2, 0, c1), 64, to_c)
        g_arrive(k, 11, block(x2, 0, c1) + 64, 64, to_c)

    def tiles(width, body):
        @pl.loop(0, COLS // width)
        def _(t):
            body(pl.ds(pl.multiple_of(t * width, width), width))

    def with_rows(lhs, k, rows):
        return lax.dot_general(lhs, wf[k, rows, :], (((1,), (1,)), ((), ())), preferred_element_type=F32)

    def with_cols(lhs, k, cols):
        return jnp.dot(lhs, wf[k, :, cols], preferred_element_type=F32)

    mine = at(32 * mp, 32)

    def partial_sums(i, lhs, k):
        def body(cols):
            value = with_rows(lhs[...], k, cols)
            part[:, cols] = value
            sbuf[i, :, cols] = value.astype(BF16)

        tiles(256, body)
        for o in (2, 1, 3):
            send(sbuf.at[i, at(32 * other[o], 32)], rbuf.at[i, o - 1], rs_s.at[i, o - 1], rs_r.at[i, o - 1],
                 {"mp": other[o]})

    def summed(i):
        total = part[mine, :]
        for o in (1, 3, 2):
            arrive(rbuf.at[i, o - 1], rs_s.at[i, o - 1], rs_r.at[i, o - 1], {"mp": other[o]})
            total = total + rbuf[i, o - 1].astype(F32)
        return total

    def spread(i, dst, base, value):
        rows = at(base + 32 * mp, 32)
        dst[rows, :] = value
        for o in (2, 1, 3):
            send(dst.at[rows], dst.at[rows], mg_s.at[i, o - 1], mg_r.at[i, o - 1], {"mp": other[o]})

    def spread_arrive(i, dst, base):
        for o in (1, 3, 2):
            rows = at(base + 32 * ((mp + 4 - o) % 4), 32)
            arrive(dst.at[rows], mg_s.at[i, o - 1], mg_r.at[i, o - 1], {"mp": other[o]})

    pieces = {"W": (0, W, 0, COLS), "U": (1, U, 0, COLS), "E0": (2, E, 0, 512), "E1": (3, E, 512, 512)}

    def product(piece, lhs, rhs, core, store):
        _, _, first, width = pieces[piece]

        @pl.loop(0, 2)
        def _(t):
            rows = pl.ds(pl.multiple_of(core * 512 + t * 256, 256), 256)
            local = pl.ds(pl.multiple_of(t * 256, 256), 256)
            for start in range(first, first + width, 512):
                cols = pl.ds(start, 512)
                store(local, cols, lax.dot_general(
                    lhs[:, rows], rhs[:, cols], (((0,), (0,)), ((), ())), preferred_element_type=F32
                ))

    def r_copy(piece, i, src, dst, to):
        n = pieces[piece][0]
        return copy(src, dst, gr_s.at[n, i], gr_r.at[n, i], to)

    def r_send(piece, i, src, dst, to):
        made = r_copy(piece, i, src, dst, to)
        made.start()
        started.append(made)

    def terms_across(piece, lhs, rhs):
        _, k, first, width = pieces[piece]

        def store(local, cols, value):
            cs[k, local, cols] = value.astype(BF16)

        product(piece, lhs, rhs, c1, store)
        whole = (k, slice(None), pl.ds(first, width))
        r_send(piece, 0, cs.at[whole], cr.at[whole], to_c)

    def terms_here(piece, lhs, rhs):
        k = pieces[piece][1]

        def store(local, cols, value):
            acc[k, local, cols] = value

        product(piece, lhs, rhs, c, store)

    def chunks(count, body):
        @pl.loop(0, count)
        def _(t):
            body(pl.multiple_of(t * 32, 32))

    def pair(k, start, cols):
        return acc[k, pl.ds(start, 32), cols] + cr[k, pl.ds(start, 32), cols].astype(F32)

    def reduce1(piece):
        _, k, first, width = pieces[piece]
        cols = pl.ds(first, width)
        r_copy(piece, 0, cr.at[k, :, cols], cr.at[k, :, cols], to_c).wait_recv()

        def body(t):
            for h, far in ((0, x3), (1, x1)):
                for i, xb in ((0, far), (1, x2)):
                    value = pair(k, pl.multiple_of(xb * 128 + h * 64 + t, 32), cols)
                    xs1[k, h, i, pl.ds(t, 32), cols] = value.astype(BF16)

        chunks(2, body)
        for h, to in ((0, to_x3), (1, to_x1)):
            r_send(piece, 1 + h, xs1.at[k, h, :, :, cols], xr1.at[k, h, :, :, cols], to)

    def reduce2(piece):
        _, k, first, width = pieces[piece]
        cols = pl.ds(first, width)
        for h, frm in ((0, to_x3), (1, to_x1)):
            r_copy(piece, 1 + h, xr1.at[k, h, :, :, cols], xr1.at[k, h, :, :, cols], frm).wait_recv()

        def body(t):
            for h, near in ((0, x1), (1, x3)):
                value = pair(k, pl.multiple_of(near * 128 + h * 64 + t, 32), cols)
                xs2[k, h, pl.ds(t, 32), cols] = (value + xr1[k, h, 1, pl.ds(t, 32), cols].astype(F32)).astype(BF16)

        chunks(2, body)
        for h, to in ((0, to_x1), (1, to_x3)):
            r_send(piece, 3 + h, xs2.at[k, h, :, cols], xr2.at[k, h, :, cols], to)

    def reduce3(piece):
        _, k, first, width = pieces[piece]
        cols = pl.ds(first, width)
        for h, frm in ((0, to_x1), (1, to_x3)):
            r_copy(piece, 3 + h, xr2.at[k, h, :, cols], xr2.at[k, h, :, cols], frm).wait_recv()

        def body(t):
            for h in (0, 1):
                value = pair(k, pl.multiple_of(x * 128 + h * 64 + t, 32), cols)
                value = value + xr1[k, h, 0, pl.ds(t, 32), cols].astype(F32) + xr2[k, h, pl.ds(t, 32), cols].astype(F32)
                vsum[k, pl.ds(pl.multiple_of(h * 64 + t, 32), 32), cols] = value

        chunks(2, body)
        zs1[k, 0, :, cols] = vsum[k, at(z1 * 32, 32), cols].astype(BF16)
        zs1[k, 1, :, cols] = vsum[k, at(z3 * 32, 32), cols].astype(BF16)
        r_send(piece, 5, zs1.at[k, :, :, cols], zr1.at[k, :, :, cols], to_z1)

    def reduce4(piece):
        _, k, first, width = pieces[piece]
        cols = pl.ds(first, width)
        r_copy(piece, 5, zr1.at[k, :, :, cols], zr1.at[k, :, :, cols], to_z1).wait_recv()
        zs2[k, :, cols] = (vsum[k, at(z2 * 32, 32), cols] + zr1[k, 1, :, cols].astype(F32)).astype(BF16)
        r_send(piece, 6, zs2.at[k, :, cols], zr2.at[k, :, cols], to_z2)

    def reduce5(piece):
        _, k, first, width = pieces[piece]
        cols = pl.ds(first, width)
        r_copy(piece, 6, zr2.at[k, :, cols], zr2.at[k, :, cols], to_z2).wait_recv()
        total = vsum[k, at(z * 32, 32), cols] + zr1[k, 0, :, cols].astype(F32)
        out[k, :, cols] = total + zr2[k, :, cols].astype(F32)

    center.wait()
    rows_go()
    selection()
    to_patches(xs)
    gather0(E)
    weights_go(U)
    columns_go()
    gather1(E)
    weights_go(W)
    gather0(U)
    patches_go(0, xs, px, 128, (2, 0))
    gather2(E)
    columns_arrive()
    gather1(U)
    patches_go(0, xs, px, 128, (1, 3))
    gather0(W)
    advance(0)
    advance(1)
    gather3(E)
    gather2(U)
    gather1(W)
    advance(2)
    advance(3)
    gather4(E)
    gather5(E)

    patches_arrive(0, px, 128)
    partial_sums(0, px.at[128:256], E)
    gather3(U)
    gather2(W)
    to_patches(ts)
    patches_go(1, ts, tg, 0)
    state_go()
    e = summed(0)
    recip = lax.rsqrt(jnp.mean(e * e, axis=1, keepdims=True) + 1e-06)
    ered[...] = e
    spread(0, nf, 0, (e * recip).astype(BF16))
    gather4(U)
    gather5(U)
    gather3(W)
    spread_arrive(0, nf, 0)

    def hidden(cols):
        pre = with_cols(nf[...], U, cols)
        square = pre * pre
        tangent = jnp.tanh(GELU_FACTOR * (pre + 0.044715 * square * pre))
        act[:, cols] = (0.5 * pre * (1.0 + tangent)).astype(BF16)
        slope[:, cols] = 0.5 * (1.0 + tangent) + 0.5 * pre * (1.0 - tangent * tangent) * GELU_FACTOR * (
            1.0 + 3.0 * 0.044715 * square
        )

    tiles(256, hidden)
    gather4(W)
    gather5(W)
    partial_sums(1, act, W)
    spread(1, yd, 0, (ered[...] + summed(1)).astype(BF16))
    patches_arrive(1, tg, 0)
    spread_arrive(1, yd, 0)

    def residual(cols):
        pred = px[128:256, cols].astype(F32) + with_cols(yd[0:128, :], E, cols)
        px[0:128, cols] = ((pred - tg[:, cols].astype(F32)) * (1.0 / 64.0)).astype(BF16)

    tiles(256, residual)
    partial_sums(2, px.at[0:128], E)
    state_pass(0)
    state_pass(1)
    dy = summed(2)
    dyred[...] = dy
    spread(2, dyf, 0, dy.astype(BF16))
    state_pass(2)
    state_pass(3)
    spread_arrive(2, dyf, 0)
    terms_across("W", dyf, act)
    terms_here("W", dyf, act)

    def hidden_back(cols):
        dhid[:, cols] = (with_cols(dyf[...], W, cols) * slope[:, cols]).astype(BF16)

    reduce1("W")
    tiles(256, hidden_back)
    partial_sums(3, dhid, U)
    terms_across("U", nf, dhid)
    terms_here("U", nf, dhid)
    dn = summed(3)
    e = ered[...]
    recip = lax.rsqrt(jnp.mean(e * e, axis=1, keepdims=True) + 1e-06)
    de = dyred[...] + recip * dn - e * (recip * recip * recip) * jnp.mean(dn * e, axis=1, keepdims=True)
    spread(3, yd, 128, de.astype(BF16))
    reduce1("U")
    reduce2("W")
    spread_arrive(3, yd, 128)
    terms_across("E0", yd, px)
    terms_here("E0", yd, px)
    terms_across("E1", yd, px)
    reduce2("U")
    reduce1("E0")
    terms_here("E1", yd, px)
    reduce1("E1")
    reduce3("W")
    reduce2("E0")
    reduce2("E1")
    reduce3("U")
    reduce4("W")
    reduce3("E0")
    reduce4("U")
    reduce3("E1")
    reduce5("W")
    reduce4("E0")
    reduce4("E1")
    reduce5("U")
    reduce5("E0")
    reduce5("E1")

    for made in started:
        made.wait_send()

    @pl.when(role == 1)
    def _():
        for k in (E, U, W):
            weights_across(k).wait_send()
        for part in range(4):
            state_home(part).wait()

    @pl.when(role == 0)
    def _():
        for o in range(4):
            for made in patches(0, xs, px, 128, o) + patches(1, ts, tg, 0, o):
                made.wait_send()
        for part in range(4):
            state_across(part).wait_send()


def train(state, embed, mlp):
    vmem = pl.BlockSpec(memory_space=pltpu.VMEM)
    dma = pltpu.SemaphoreType.DMA
    return pl.pallas_call(
        kernel,
        name="train",
        out_shape=(jax.ShapeDtypeStruct((3, OWN, COLS), F32), jax.ShapeDtypeStruct(state.shape[1:], F32)),
        in_specs=[pl.BlockSpec(memory_space=pltpu.HBM)] * 3,
        out_specs=(vmem, vmem),
        scratch_shapes=[
            pltpu.VMEM((2, 2, 8, 80, 256), F32),
            pltpu.VMEM((2, 8, 64, 128), F32),
            pltpu.VMEM((2, 80, 128), F32),
            pltpu.VMEM((2, 80, 128), F32),
            pltpu.VMEM((2048, 256), BF16),
            pltpu.VMEM((128, 2048), BF16),
            pltpu.VMEM((4, OWN, COLS), BF16),
            pltpu.VMEM((4, OWN, COLS), BF16),
            pltpu.VMEM((3, D, COLS), BF16),
            pltpu.VMEM((2 * ROWS, COLS), BF16),
            pltpu.VMEM((2 * ROWS, D), BF16),
            pltpu.VMEM((ROWS, COLS), BF16),
            pltpu.VMEM((ROWS, D), F32),
            pltpu.VMEM((4, ROWS, D), BF16),
            pltpu.VMEM((4, 3, OWN, D), BF16),
            pltpu.VMEM((ROWS, D), BF16),
            pltpu.VMEM((ROWS, D), BF16),
            pltpu.VMEM((ROWS, COLS), BF16),
            pltpu.VMEM((ROWS, COLS), F32),
            pltpu.VMEM((ROWS, COLS), BF16),
            pltpu.VMEM((OWN, D), F32),
            pltpu.VMEM((OWN, D), F32),
            pltpu.VMEM((3, 512, COLS), F32),
            pltpu.VMEM((3, 512, COLS), BF16),
            pltpu.VMEM((3, 512, COLS), BF16),
            pltpu.VMEM((3, 2, 2, 64, COLS), BF16),
            pltpu.VMEM((3, 2, 2, 64, COLS), BF16),
            pltpu.VMEM((3, 2, 64, COLS), BF16),
            pltpu.VMEM((3, 2, 64, COLS), BF16),
            pltpu.VMEM((3, 128, COLS), F32),
            pltpu.VMEM((3, 2, OWN, COLS), BF16),
            pltpu.VMEM((3, 2, OWN, COLS), BF16),
            pltpu.VMEM((3, OWN, COLS), BF16),
            pltpu.VMEM((3, OWN, COLS), BF16),
            dma((1,)), dma((4,)), dma((4,)), dma((8,)), dma((8,)),
            dma((3,)), dma((3,)),
            dma((2, 2, 4)), dma((2, 4)),
            dma((3, 12)), dma((3, 12)),
            dma((4, 3)), dma((4, 3)),
            dma((4, 3)), dma((4, 3)),
            dma((4, 7)), dma((4, 7)),
        ],
        compiler_params=pltpu.CompilerParams(
            collective_id=0, has_side_effects=True, vmem_limit_bytes=52 * 1024 * 1024
        ),
        cost_estimate=pl.CostEstimate(flops=6 * 10**9, bytes_accessed=4 * 10**8, transcendentals=10**5),
    )(state, embed, mlp)


def shards(state, embed, mlp, mom_embed, mom_mlp):
    grads, state_out = train(state, embed, mlp)
    mom_embed_out = MOMENTUM_DECAY * mom_embed + grads[:1]
    mom_mlp_out = MOMENTUM_DECAY * mom_mlp + grads[None, 1:]
    embed_out = (embed.astype(F32) - LEARNING_RATE * mom_embed_out).astype(BF16)
    mlp_out = (mlp.astype(F32) - LEARNING_RATE * mom_mlp_out).astype(BF16)
    return (state_out, embed_out, mlp_out, mom_embed_out, mom_mlp_out)


def solution(mesh):
    placed = (
        P("role", None, None, "dp", "mp"),
        P("role", "dp", "mp"),
        P("role", None, "dp", "mp"),
        P("role", "dp", "mp"),
        P("role", None, "dp", "mp"),
    )
    return jax.shard_map(
        shards,
        mesh=mesh,
        in_specs=placed,
        out_specs=(
            P(None, None, "dp", "mp"),
            P("role", "dp", "mp"),
            P("role", None, "dp", "mp"),
            P("role", "dp", "mp"),
            P("role", None, "dp", "mp"),
        ),
        check_vma=False,
    )
```

```python
import jax
import jax.numpy as jnp
from jax import lax
from jax.experimental import pallas as pl
from jax.experimental.pallas import tpu as pltpu
from jax.sharding import PartitionSpec as P

PATCH = 16
STEPS = 4


SUBSTRATE_DIFFUSION = 0.2
CATALYST_DIFFUSION = 0.1
FEED_RATE = 0.037
KILL_RATE = 0.06
TIME_STEP = 0.8
GELU_FACTOR = 0.7978845608028654
MOMENTUM_DECAY = 0.9
LEARNING_RATE = 0.003

BF16 = jnp.bfloat16
F32 = jnp.float32
MESH = pl.DeviceIdType.MESH
ROWS = 128
OWN = 32
D = 1024
COLS = 1024
E, U, W = 0, 1, 2


def kernel(
    state, embed, mlp, out, state_out,
    total_rows, field, passed, edge, edges, onehot, spread_in, xs, ts, wf, px, yd, tg, part, sbuf, rbuf, nf, dyf, act, slope, dhid, ered, dyred,
    acc, cs, cr, xs1, xr1, xs2, xr2, vsum, zs1, zr1, zs2, zr2,
    in_s, halo_s, halo_r, state_s, state_r, role_s, role_r, x_s, x_r, ag_s, ag_r, rs_s, rs_r, mg_s, mg_r, gr_s, gr_r,
):
    role = lax.axis_index("role")
    dp = lax.axis_index("dp")
    mp = lax.axis_index("mp")
    x, z, c = dp // 8, (dp // 2) % 4, dp % 2

    def dev(x_, z_, c_):
        return {"dp": (x_ * 4 + z_) * 2 + c_}

    x1, x2, x3 = x + 1 - 2 * (x % 2), (x + 2) % 4, 3 - x
    z1, z2 = z + 1 - 2 * (z % 2), (z + 2) % 4
    z3 = (z1 + 2) % 4
    c1 = 1 - c
    zm = 3 - z
    zl = jnp.where(role == 1, z, zm)
    to_c, to_x1, to_x3 = dev(x, z, c1), dev(x1, z, c), dev(x3, z, c)
    to_z1, to_z2 = dev(x, z1, c), dev(x, z2, c)
    after, before = {"dp": (dp + 1) % 32}, {"dp": (dp + 31) % 32}
    east, west = {"mp": (mp + 1) % 4}, {"mp": (mp + 3) % 4}
    mirror = dev(x, zm, c)["dp"]
    center = pltpu.make_async_copy(
        state.at[0], field.at[0, :, :, pl.ds(8, 64), pl.ds(0, 128)], in_s.at[0]
    )
    center.start()
    other = [(mp + o) % 4 for o in range(4)]

    def at(start, size):
        return pl.ds(pl.multiple_of(start, 16), size)

    barrier = pltpu.get_barrier_semaphore()
    friends = [to_c, to_x1, to_x3, to_z1, to_z2, after, before, {"dp": mirror}, {"role": 1 - role}]
    friends += [{"mp": other[o]} for o in (1, 2, 3)]
    friends += [{"role": 1 - role, "dp": mirror, "mp": other[o]} for o in range(4)]
    for friend in friends:
        pl.semaphore_signal(barrier, inc=1, device_id=friend, device_id_type=MESH)
    pl.semaphore_wait(barrier, len(friends))

    started = []

    def copy(src, dst, ssem, rsem, to):
        return pltpu.make_async_remote_copy(
            src_ref=src, dst_ref=dst, send_sem=ssem, recv_sem=rsem, device_id=to, device_id_type=MESH
        )

    def send(src, dst, ssem, rsem, to):
        made = copy(src, dst, ssem, rsem, to)
        made.start()
        started.append(made)

    def arrive(dst, ssem, rsem, frm):
        copy(dst, dst, ssem, rsem, frm).wait_recv()

    def post(src, dst, ssem, rsem, to):
        copy(src, dst, ssem, rsem, to).start()

    def all_posted(whole, ssem):
        pltpu.make_async_copy(whole, whole, ssem).wait()

    own_rows = at(c * 512 + x * 128 + zl * 32, 32)
    far_rows = at(c * 512 + x * 128 + z * 32, 32)
    w = (embed.at[0], mlp.at[0, 0], mlp.at[0, 1])

    def weights_across(k):
        return copy(w[k], wf.at[k, far_rows], role_s.at[k], role_r.at[k], {"role": 0, "dp": mirror})

    def weights_here(k):
        return pltpu.make_async_copy(w[k], wf.at[k, far_rows], role_r.at[k])

    def patches(which, src, dst, base, o):
        rows = at(base + 32 * mp, 32)
        made = []
        for r in (1, 0):
            if o == 0 and r == 0:
                continue
            to = {"role": 1, "dp": mirror, "mp": other[o]} if r == 1 else {"role": 0, "mp": other[o]}
            made.append(copy(src.at[other[o]], dst.at[rows], x_s.at[which], x_r.at[which], to))
        return made

    def patches_here(which, src, dst, base):
        return pltpu.make_async_copy(src.at[mp], dst.at[at(base + 32 * mp, 32)], x_r.at[which])

    def patches_go(which, src, dst, base, some=(0, 1, 2, 3)):
        @pl.when(role == 0)
        def _():
            for o in some:
                for made in patches(which, src, dst, base, o):
                    made.start()
            if 0 in some:
                patches_here(which, src, dst, base).start()

    def state_part(whole, part):
        return whole.at[part // 2, pl.ds(4 * (part % 2), 4)]

    def final_part(part):
        return field.at[0, part // 2, pl.ds(4 * (part % 2), 4), pl.ds(8, 64), pl.ds(0, 128)]

    def state_across(part):
        return copy(final_part(part), state_part(passed, part), state_s.at[part], state_r.at[part],
                    {"role": 1, "dp": mirror})

    def state_here(part):
        return pltpu.make_async_copy(final_part(part), state_part(state_out, part), in_s.at[1 + part])

    def state_home(part):
        return copy(state_part(passed, part), state_part(state_out, part), state_s.at[4 + part], state_r.at[4 + part],
                    {"dp": mirror})

    def state_go(first):
        @pl.when(role == 0)
        def _():
            for part in (first, first + 1):
                state_across(part).start()
                state_here(part).start()

    def state_pass(part):
        @pl.when(role == 1)
        def _():
            state_across(part).wait_recv()
            state_home(part).start()

    @pl.when(role == 1)
    def _():
        weights_across(E).start()
        for k in (E, U, W):
            weights_here(k).start()

    def weights_go(k):
        @pl.when(role == 1)
        def _():
            weights_across(k).start()

    def patches_arrive(which, dst, base):
        arrive(dst.at[base : base + 128], x_s.at[which], x_r.at[which], east)

    lane = lax.broadcasted_iota(jnp.int32, (80, 128), 1)

    def halo_rows(i, src, dst, to):
        ends = [field.at[0, :, :, pl.ds(start, 8), pl.ds(0, 128)] for start in (src, dst)]
        return copy(ends[0], ends[1], halo_s.at[i], halo_r.at[i], to)

    def rows_go():
        for i, src, dst, to in ((0, 8, 72, before), (1, 64, 0, after)):
            halo_rows(i, src, dst, to).start()

    def columns_go():
        halo_rows(0, 72, 72, after).wait_recv()
        halo_rows(1, 0, 0, before).wait_recv()
        halo_rows(0, 8, 72, before).wait_send()
        halo_rows(1, 64, 0, after).wait_send()
        edge[...] = jnp.zeros_like(edge)
        for p in range(16):
            cells = field[0, p // 8, p % 8, :, 0:128]
            inside = (lane >= 4 * p) & (lane < 4 * p + 4)
            edge[0] = jnp.where(inside, pltpu.roll(cells, 4 * p, 1) if p else cells, edge[0])
            edge[1] = jnp.where(inside, pltpu.roll(cells, 4 * p + 4, 1), edge[1])
        send(edge.at[0], edges.at[0], halo_s.at[2], halo_r.at[2], west)
        send(edge.at[1], edges.at[1], halo_s.at[3], halo_r.at[3], east)

    def columns_arrive():
        arrive(edges.at[0], halo_s.at[2], halo_r.at[2], east)
        arrive(edges.at[1], halo_s.at[3], halo_r.at[3], west)
        for p in range(16):
            behind = edges[0] if p == 0 else pltpu.roll(edges[0], 128 - 4 * p, 1)
            ahead = pltpu.roll(edges[1], 124 - 4 * p, 1)
            field[0, p // 8, p % 8, :, 128:256] = jnp.where(lane < 4, behind, jnp.where(lane >= 124, ahead, 0.0))

    def advance(step):
        now, later = step % 2, (step + 1) % 2

        @pl.loop(0, 8)
        def _(p):
            low, high = jnp.maximum(p - 1, 0), jnp.minimum(p + 1, 7)

            def laplace(s):
                mid = field[now, s, p]
                total = field[now, s, low] + field[now, s, high]
                total = total + pltpu.roll(mid, 1, 0) + pltpu.roll(mid, 79, 0)
                total = total + pltpu.roll(mid, 1, 1) + pltpu.roll(mid, 255, 1)
                return mid, total - 6.0 * mid

            substrate, first = laplace(0)
            catalyst, second = laplace(1)
            growth = substrate * catalyst * catalyst
            field[later, 0, p] = substrate + TIME_STEP * (
                SUBSTRATE_DIFFUSION * first - growth + FEED_RATE * (1.0 - substrate)
            )
            field[later, 1, p] = catalyst + TIME_STEP * (
                CATALYST_DIFFUSION * second + growth - (FEED_RATE + KILL_RATE) * catalyst
            )

    def selection():
        feature = lax.broadcasted_iota(jnp.int32, (128, 256), 1)
        inner = lax.broadcasted_iota(jnp.int32, (128, 256), 0) % PATCH
        for r in range(PATCH):
            onehot[128 * r : 128 * r + 128, :] = jnp.where(feature == PATCH * r + inner, 1.0, 0.0).astype(BF16)

    def to_patches(dst):
        patch = lax.broadcasted_iota(jnp.int32, (8, 128), 0)
        own = lax.broadcasted_iota(jnp.int32, (8, 128), 1) // PATCH == patch

        @pl.loop(0, 4)
        def _(j):
            @pl.loop(0, 4)
            def _(q):
                species, plane = j // 2, 4 * (j % 2) + q
                for r in range(PATCH):
                    pieces = []
                    for by in range(4):
                        row = field[0, species, plane, pl.ds(8 + PATCH * by + r, 1), 0:128]
                        pieces.append(jnp.where(own, jnp.broadcast_to(row, (8, 128)), 0.0))
                    rows = pl.ds(pl.multiple_of(32 * q, 32), 32)
                    spread_in[rows, 128 * r : 128 * r + 128] = jnp.concatenate(pieces, axis=0).astype(BF16)

            moved = jnp.dot(spread_in[...], onehot[...], preferred_element_type=F32).astype(BF16)
            for q in range(4):
                dst[j, :, 256 * q : 256 * q + 256] = moved[32 * q : 32 * q + 32, :]

    zl1, zl2 = zl + 1 - 2 * (zl % 2), (zl + 2) % 4
    label = (zl, zl2, zl1, (zl1 + 2) % 4)

    def block(x_, b, c_=c):
        return c_ * 512 + x_ * 128 + label[b] * 32

    def g_send(k, i, start, size, to):
        rows = at(start, size)
        post(wf.at[k, rows], wf.at[k, rows], ag_s.at[k], ag_r.at[k, i], to)

    def g_arrive(k, i, start, size, frm):
        arrive(wf.at[k, at(start, size)], ag_s.at[k], ag_r.at[k, i], frm)

    def along_x(k, b):
        g_send(k, 3 + b, block(x, b), 32, to_x1)
        g_send(k, 7 + b, block(x, b), 32, to_x3)
        g_send(k, 12, block(x, b), 32, to_c)

    def gather0(k):
        arrive(wf.at[k, own_rows], role_s.at[k], role_r.at[k], {"role": 1 - role})
        g_send(k, 0, block(x, 0), 32, to_z2)
        g_send(k, 1, block(x, 0), 32, to_z1)
        along_x(k, 0)

    def gather1(k):
        g_arrive(k, 0, block(x, 1), 32, to_z2)
        g_send(k, 2, block(x, 1), 32, to_z1)
        along_x(k, 1)

    def gather2(k):
        g_arrive(k, 1, block(x, 2), 32, to_z1)
        along_x(k, 2)
        g_arrive(k, 2, block(x, 3), 32, to_z1)
        along_x(k, 3)

    def gather3(k, some):
        for b in some:
            g_arrive(k, 3 + b, block(x1, b), 32, to_x1)
            g_send(k, 11, block(x1, b), 16, to_x3)
            g_send(k, 12, block(x1, b), 32, to_c)
            g_arrive(k, 7 + b, block(x3, b), 32, to_x3)
            g_send(k, 11, block(x3, b) + 16, 16, to_x1)
            g_send(k, 12, block(x3, b), 32, to_c)

    def gather4(k):
        g_arrive(k, 11, c * 512 + x2 * 128, 128, to_x1)
        g_send(k, 12, c * 512 + x2 * 128, 128, to_c)

    def gather5(k):
        g_arrive(k, 12, c1 * 512, 512, to_c)

    def tiles(width, body):
        @pl.loop(0, COLS // width)
        def _(t):
            body(pl.ds(pl.multiple_of(t * width, width), width))

    def with_rows(lhs, k, rows):
        return lax.dot_general(lhs, wf[k, rows, :], (((1,), (1,)), ((), ())), preferred_element_type=F32)

    def with_cols(lhs, k, cols):
        return jnp.dot(lhs, wf[k, :, cols], preferred_element_type=F32)

    mine = at(32 * mp, 32)

    def half(s):
        return pl.ds(512 * s, 512)

    def partial_sums(i, lhs, k):
        for s in (0, 1):

            @pl.loop(0, 2)
            def _(t):
                cols = pl.ds(pl.multiple_of(512 * s + 256 * t, 256), 256)
                value = with_rows(lhs[...], k, cols)
                part[:, cols] = value
                sbuf[i, :, cols] = value.astype(BF16)

            for o in (2, 1, 3):
                post(sbuf.at[i, at(32 * other[o], 32), half(s)], rbuf.at[i, o - 1, :, half(s)],
                     rs_s.at[0], rs_r.at[i, s], {"mp": other[o]})

    def summed(i, s):
        total = part[mine, half(s)]
        arrive(rbuf.at[i, :, :, half(s)], rs_s.at[0], rs_r.at[i, s], east)
        for o in (1, 2, 3):
            total = total + rbuf[i, o - 1, :, half(s)].astype(F32)
        return total

    def all_summed(i):
        return jnp.concatenate([summed(i, 0), summed(i, 1)], axis=1)

    def spread(i, s, dst, base, value):
        rows = at(base + 32 * mp, 32)
        dst[rows, half(s)] = value
        for o in (2, 1, 3):
            post(dst.at[rows, half(s)], dst.at[rows, half(s)], mg_s.at[0], mg_r.at[i], {"mp": other[o]})

    def spread_all(i, dst, base, value):
        for s in (0, 1):
            spread(i, s, dst, base, value[:, 512 * s : 512 * s + 512])

    def spread_arrive(i, dst, base):
        arrive(dst.at[base : base + 96], mg_s.at[0], mg_r.at[i], east)

    pieces = {"W": (0, W, 0, 512), "U": (1, U, 0, 512), "E0": (2, E, 0, 512), "E1": (3, E, 512, 512)}

    def in_matrix(group, k, first, width):
        return pl.ds(first, width) if k == E else pl.ds(pl.multiple_of(512 * group + first, 512), width)

    def product(piece, lhs, rhs, core, store):
        _, k, first, width = pieces[piece]

        @pl.loop(0, 2)
        def _(t):
            rows = pl.ds(pl.multiple_of(core * 512 + t * 256, 256), 256)
            local = pl.ds(pl.multiple_of(t * 256, 256), 256)
            store(local, pl.ds(first, width), lax.dot_general(
                lhs[:, rows], rhs[:, in_matrix(role, k, first, width)], (((0,), (0,)), ((), ())),
                preferred_element_type=F32,
            ))

    def r_copy(piece, i, src, dst, to):
        n = pieces[piece][0]
        return copy(src, dst, gr_s.at[n, i], gr_r.at[n, i], to)

    def r_send(piece, i, src, dst, to):
        made = r_copy(piece, i, src, dst, to)
        made.start()
        started.append(made)

    def terms_across(piece, lhs, rhs):
        _, k, first, width = pieces[piece]

        def store(local, cols, value):
            cs[k, local, cols] = value.astype(BF16)

        product(piece, lhs, rhs, c1, store)
        whole = (k, slice(None), pl.ds(first, width))
        r_send(piece, 0, cs.at[whole], cr.at[whole], to_c)

    def terms_here(piece, lhs, rhs):
        k = pieces[piece][1]

        def store(local, cols, value):
            acc[k, local, cols] = value

        product(piece, lhs, rhs, c, store)

    def chunks(count, body):
        @pl.loop(0, count)
        def _(t):
            body(pl.multiple_of(t * 32, 32))

    def pair(k, start, cols):
        return acc[k, pl.ds(start, 32), cols] + cr[k, pl.ds(start, 32), cols].astype(F32)

    def reduce1(piece):
        _, k, first, width = pieces[piece]
        cols = pl.ds(first, width)
        r_copy(piece, 0, cr.at[k, :, cols], cr.at[k, :, cols], to_c).wait_recv()

        def body(t):
            for h, far in ((0, x3), (1, x1)):
                for i, xb in ((0, far), (1, x2)):
                    value = pair(k, pl.multiple_of(xb * 128 + h * 64 + t, 32), cols)
                    xs1[k, h, i, pl.ds(t, 32), cols] = value.astype(BF16)

        chunks(2, body)
        for h, to in ((0, to_x3), (1, to_x1)):
            r_send(piece, 1 + h, xs1.at[k, h, :, :, cols], xr1.at[k, h, :, :, cols], to)

    def reduce2(piece):
        _, k, first, width = pieces[piece]
        cols = pl.ds(first, width)
        for h, frm in ((0, to_x3), (1, to_x1)):
            r_copy(piece, 1 + h, xr1.at[k, h, :, :, cols], xr1.at[k, h, :, :, cols], frm).wait_recv()

        def body(t):
            for h, near in ((0, x1), (1, x3)):
                value = pair(k, pl.multiple_of(near * 128 + h * 64 + t, 32), cols)
                xs2[k, h, pl.ds(t, 32), cols] = (value + xr1[k, h, 1, pl.ds(t, 32), cols].astype(F32)).astype(BF16)

        chunks(2, body)
        for h, to in ((0, to_x1), (1, to_x3)):
            r_send(piece, 3 + h, xs2.at[k, h, :, cols], xr2.at[k, h, :, cols], to)

    def reduce3(piece):
        _, k, first, width = pieces[piece]
        cols = pl.ds(first, width)
        for h, frm in ((0, to_x1), (1, to_x3)):
            r_copy(piece, 3 + h, xr2.at[k, h, :, cols], xr2.at[k, h, :, cols], frm).wait_recv()

        def body(t):
            for h in (0, 1):
                value = pair(k, pl.multiple_of(x * 128 + h * 64 + t, 32), cols)
                value = value + xr1[k, h, 0, pl.ds(t, 32), cols].astype(F32) + xr2[k, h, pl.ds(t, 32), cols].astype(F32)
                vsum[k, pl.ds(pl.multiple_of(h * 64 + t, 32), 32), cols] = value

        chunks(2, body)
        zs1[k, 0, :, cols] = vsum[k, at(z1 * 32, 32), cols].astype(BF16)
        zs1[k, 1, :, cols] = vsum[k, at(z3 * 32, 32), cols].astype(BF16)
        r_send(piece, 5, zs1.at[k, :, :, cols], zr1.at[k, :, :, cols], to_z1)

    def reduce4(piece):
        _, k, first, width = pieces[piece]
        cols = pl.ds(first, width)
        r_copy(piece, 5, zr1.at[k, :, :, cols], zr1.at[k, :, :, cols], to_z1).wait_recv()
        zs2[k, :, cols] = (vsum[k, at(z2 * 32, 32), cols] + zr1[k, 1, :, cols].astype(F32)).astype(BF16)
        r_send(piece, 6, zs2.at[k, :, cols], zr2.at[k, :, cols], to_z2)

    def result(piece):
        n, k, first, width = pieces[piece]
        part = (k, slice(None), pl.ds(first, width) if k == E else slice(None))
        return pltpu.make_async_copy(total_rows.at[part], out.at[part], in_s.at[5 + n])

    def reduce5(piece):
        _, k, first, width = pieces[piece]
        cols = pl.ds(first, width)
        r_copy(piece, 6, zr2.at[k, :, cols], zr2.at[k, :, cols], to_z2).wait_recv()
        total = vsum[k, at(z * 32, 32), cols] + zr1[k, 0, :, cols].astype(F32)
        here = total_rows.at[k, :, in_matrix(role, k, first, width)]
        here[...] = total + zr2[k, :, cols].astype(F32)
        if k != E:
            r_send(piece, 7, here, here, {"role": 1 - role})
        else:
            result(piece).start()

    def reduced(piece):
        _, k, first, width = pieces[piece]
        there = total_rows.at[k, :, in_matrix(1 - role, k, first, width)]
        r_copy(piece, 7, there, there, {"role": 1 - role}).wait_recv()
        result(piece).start()

    center.wait()
    rows_go()
    selection()
    to_patches(xs)
    gather0(E)
    weights_go(U)
    patches_go(0, xs, px, 128, (2, 0))
    columns_go()
    gather1(E)
    weights_go(W)
    patches_go(0, xs, px, 128, (1, 3))
    gather0(U)
    gather3(E, (0,))
    gather2(E)
    columns_arrive()
    gather3(E, (1,))
    advance(0)
    gather1(U)
    gather0(W)
    advance(1)
    gather3(E, (2, 3))
    gather2(U)
    advance(2)
    gather1(W)
    advance(3)
    gather3(U, (0, 1))
    gather4(E)
    to_patches(ts)
    patches_go(1, ts, tg, 0)
    gather5(E)

    patches_arrive(0, px, 128)
    partial_sums(0, px.at[128:256], E)
    gather3(U, (2, 3))
    gather2(W)
    gather3(W, (0, 1))
    e = all_summed(0)
    recip = lax.rsqrt(jnp.mean(e * e, axis=1, keepdims=True) + 1e-06)
    ered[...] = e
    spread_all(0, nf, 0, (e * recip).astype(BF16))
    gather4(U)
    gather3(W, (2, 3))
    gather5(U)
    spread_arrive(0, nf, 0)

    def hidden(cols):
        pre = with_cols(nf[...], U, cols)
        square = pre * pre
        tangent = jnp.tanh(GELU_FACTOR * (pre + 0.044715 * square * pre))
        act[:, cols] = (0.5 * pre * (1.0 + tangent)).astype(BF16)
        slope[:, cols] = 0.5 * (1.0 + tangent) + 0.5 * pre * (1.0 - tangent * tangent) * GELU_FACTOR * (
            1.0 + 3.0 * 0.044715 * square
        )

    tiles(256, hidden)
    gather4(W)
    gather5(W)
    partial_sums(1, act, W)
    state_go(0)
    for s in (0, 1):
        spread(1, s, yd, 0, (ered[:, half(s)] + summed(1, s)).astype(BF16))
    patches_arrive(1, tg, 0)
    spread_arrive(1, yd, 0)

    def residual(cols):
        pred = px[128:256, cols].astype(F32) + with_cols(yd[0:128, :], E, cols)
        px[0:128, cols] = ((pred - tg[:, cols].astype(F32)) * (1.0 / 64.0)).astype(BF16)

    tiles(256, residual)
    partial_sums(2, px.at[0:128], E)
    state_go(2)
    for s in (0, 1):
        dy = summed(2, s)
        dyred[:, half(s)] = dy
        spread(2, s, dyf, 0, dy.astype(BF16))
    state_pass(0)
    state_pass(1)
    spread_arrive(2, dyf, 0)
    terms_across("W", dyf, act)
    terms_here("W", dyf, act)

    def hidden_back(cols):
        dhid[:, cols] = (with_cols(dyf[...], W, cols) * slope[:, cols]).astype(BF16)

    reduce1("W")
    tiles(256, hidden_back)
    partial_sums(3, dhid, U)
    state_pass(2)
    state_pass(3)
    terms_across("U", nf, dhid)
    terms_here("U", nf, dhid)
    reduce1("U")
    reduce2("W")
    dn = all_summed(3)
    e = ered[...]
    recip = lax.rsqrt(jnp.mean(e * e, axis=1, keepdims=True) + 1e-06)
    de = dyred[...] + recip * dn - e * (recip * recip * recip) * jnp.mean(dn * e, axis=1, keepdims=True)
    spread_all(3, yd, 128, de.astype(BF16))
    reduce3("W")
    reduce2("U")
    spread_arrive(3, yd, 128)
    terms_across("E0", yd, px)
    terms_across("E1", yd, px)
    reduce4("W")
    reduce3("U")
    terms_here("E0", yd, px)
    terms_here("E1", yd, px)
    reduce1("E0")
    reduce1("E1")
    reduce5("W")
    reduce4("U")
    reduce2("E0")
    reduce2("E1")
    reduce5("U")
    reduce3("E0")
    reduce3("E1")
    reduce4("E0")
    reduce4("E1")
    reduced("W")
    reduced("U")
    reduce5("E0")
    reduce5("E1")

    for made in started:
        made.wait_send()
    for k in (E, U, W):
        all_posted(wf.at[k, 0:992], ag_s.at[k])
    all_posted(sbuf.at[0:3], rs_s.at[0])
    all_posted(sbuf.at[0:3], mg_s.at[0])
    for piece in pieces:
        result(piece).wait()

    @pl.when(role == 1)
    def _():
        for k in (E, U, W):
            weights_across(k).wait_send()
        for part in range(4):
            state_home(part).wait()

    @pl.when(role == 0)
    def _():
        for which in (0, 1):
            all_posted(px.at[0:224], x_s.at[which])
        for part in range(4):
            state_across(part).wait_send()
            state_here(part).wait()


def train(state, embed, mlp):
    dma = pltpu.SemaphoreType.DMA
    return pl.pallas_call(
        kernel,
        name="train",
        out_shape=(jax.ShapeDtypeStruct((3, OWN, COLS), F32), jax.ShapeDtypeStruct(state.shape[1:], F32)),
        in_specs=[pl.BlockSpec(memory_space=pltpu.HBM)] * 3,
        out_specs=(pl.BlockSpec(memory_space=pl.ANY), pl.BlockSpec(memory_space=pl.ANY)),
        scratch_shapes=[
            pltpu.VMEM((3, OWN, COLS), F32),
            pltpu.VMEM((2, 2, 8, 80, 256), F32),
            pltpu.VMEM((2, 8, 64, 128), F32),
            pltpu.VMEM((2, 80, 128), F32),
            pltpu.VMEM((2, 80, 128), F32),
            pltpu.VMEM((2048, 256), BF16),
            pltpu.VMEM((128, 2048), BF16),
            pltpu.VMEM((4, OWN, COLS), BF16),
            pltpu.VMEM((4, OWN, COLS), BF16),
            pltpu.VMEM((3, D, COLS), BF16),
            pltpu.VMEM((2 * ROWS, COLS), BF16),
            pltpu.VMEM((2 * ROWS, D), BF16),
            pltpu.VMEM((ROWS, COLS), BF16),
            pltpu.VMEM((ROWS, D), F32),
            pltpu.VMEM((4, ROWS, D), BF16),
            pltpu.VMEM((4, 3, OWN, D), BF16),
            pltpu.VMEM((ROWS, D), BF16),
            pltpu.VMEM((ROWS, D), BF16),
            pltpu.VMEM((ROWS, COLS), BF16),
            pltpu.VMEM((ROWS, COLS), F32),
            pltpu.VMEM((ROWS, COLS), BF16),
            pltpu.VMEM((OWN, D), F32),
            pltpu.VMEM((OWN, D), F32),
            pltpu.VMEM((3, 512, COLS), F32),
            pltpu.VMEM((3, 512, COLS), BF16),
            pltpu.VMEM((3, 512, COLS), BF16),
            pltpu.VMEM((3, 2, 2, 64, COLS), BF16),
            pltpu.VMEM((3, 2, 2, 64, COLS), BF16),
            pltpu.VMEM((3, 2, 64, COLS), BF16),
            pltpu.VMEM((3, 2, 64, COLS), BF16),
            pltpu.VMEM((3, 128, COLS), F32),
            pltpu.VMEM((3, 2, OWN, COLS), BF16),
            pltpu.VMEM((3, 2, OWN, COLS), BF16),
            pltpu.VMEM((3, OWN, COLS), BF16),
            pltpu.VMEM((3, OWN, COLS), BF16),
            dma((9,)), dma((4,)), dma((4,)), dma((8,)), dma((8,)),
            dma((3,)), dma((3,)),
            dma((2,)), dma((2,)),
            dma((3,)), dma((3, 13)),
            dma((1,)), dma((4, 2)),
            dma((1,)), dma((4,)),
            dma((4, 8)), dma((4, 8)),
        ],
        compiler_params=pltpu.CompilerParams(
            collective_id=0, has_side_effects=True, vmem_limit_bytes=52 * 1024 * 1024
        ),
        cost_estimate=pl.CostEstimate(flops=6 * 10**9, bytes_accessed=4 * 10**8, transcendentals=10**5),
    )(state, embed, mlp)


def shards(state, embed, mlp, mom_embed, mom_mlp):
    grads, state_out = train(state, embed, mlp)
    mom_embed_out = MOMENTUM_DECAY * mom_embed + grads[:1]
    mom_mlp_out = MOMENTUM_DECAY * mom_mlp + grads[None, 1:]
    embed_out = (embed.astype(F32) - LEARNING_RATE * mom_embed_out).astype(BF16)
    mlp_out = (mlp.astype(F32) - LEARNING_RATE * mom_mlp_out).astype(BF16)
    return (state_out, embed_out, mlp_out, mom_embed_out, mom_mlp_out)


def solution(mesh):
    placed = (
        P("role", None, None, "dp", "mp"),
        P("role", "dp", "mp"),
        P("role", None, "dp", "mp"),
        P("role", "dp", "mp"),
        P("role", None, "dp", "mp"),
    )
    return jax.shard_map(
        shards,
        mesh=mesh,
        in_specs=placed,
        out_specs=(
            P(None, None, "dp", "mp"),
            P("role", "dp", "mp"),
            P("role", None, "dp", "mp"),
            P("role", "dp", "mp"),
            P("role", None, "dp", "mp"),
        ),
        check_vma=False,
    )
```

```python
import jax
import jax.numpy as jnp
from jax import lax
from jax.experimental import pallas as pl
from jax.experimental.pallas import tpu as pltpu
from jax.sharding import PartitionSpec as P

PATCH = 16
STEPS = 4


SUBSTRATE_DIFFUSION = 0.2
CATALYST_DIFFUSION = 0.1
FEED_RATE = 0.037
KILL_RATE = 0.06
TIME_STEP = 0.8
GELU_FACTOR = 0.7978845608028654
MOMENTUM_DECAY = 0.9
LEARNING_RATE = 0.003

BF16 = jnp.bfloat16
F32 = jnp.float32
MESH = pl.DeviceIdType.MESH
ROWS = 128
OWN = 32
D = 1024
COLS = 1024
E, U, W = 0, 1, 2


def kernel(
    state, embed, mlp, out, state_out,
    total_rows, field, passed, edge, edges, onehot, spread_in, xs, ts, wf, px, yd, tg, part, sbuf, rbuf, nf, dyf, act, slope, dhid, ered, dyred,
    acc, cs, cr, xs1, xr1, xs2, xr2, vsum, zs1, zr1, zs2, zr2,
    in_s, halo_s, halo_r, state_s, state_r, role_s, role_r, x_s, x_r, ag_s, ag_r, rs_s, rs_r, mg_s, mg_r, gr_s, gr_r,
):
    role = lax.axis_index("role")
    dp = lax.axis_index("dp")
    mp = lax.axis_index("mp")
    x, z, c = dp // 8, (dp // 2) % 4, dp % 2

    def dev(x_, z_, c_):
        return {"dp": (x_ * 4 + z_) * 2 + c_}

    x1, x2, x3 = x + 1 - 2 * (x % 2), (x + 2) % 4, 3 - x
    z1, z2 = z + 1 - 2 * (z % 2), (z + 2) % 4
    z3 = (z1 + 2) % 4
    c1 = 1 - c
    zm = 3 - z
    zl = jnp.where(role == 1, z, zm)
    to_c, to_x1, to_x3 = dev(x, z, c1), dev(x1, z, c), dev(x3, z, c)
    to_z1, to_z2 = dev(x, z1, c), dev(x, z2, c)
    after, before = {"dp": (dp + 1) % 32}, {"dp": (dp + 31) % 32}
    east, west = {"mp": (mp + 1) % 4}, {"mp": (mp + 3) % 4}
    mirror = dev(x, zm, c)["dp"]
    center = pltpu.make_async_copy(
        state.at[0], field.at[0, :, :, pl.ds(8, 64), pl.ds(0, 128)], in_s.at[0]
    )
    center.start()
    other = [(mp + o) % 4 for o in range(4)]

    def at(start, size):
        return pl.ds(pl.multiple_of(start, 16), size)

    barrier = pltpu.get_barrier_semaphore()
    friends = [to_c, to_x1, to_x3, to_z1, to_z2, after, before, {"dp": mirror}, {"role": 1 - role}]
    friends += [{"mp": other[o]} for o in (1, 2, 3)]
    friends += [{"role": 1 - role, "dp": mirror, "mp": other[o]} for o in range(4)]
    for friend in friends:
        pl.semaphore_signal(barrier, inc=1, device_id=friend, device_id_type=MESH)
    pl.semaphore_wait(barrier, len(friends))

    started = []

    def copy(src, dst, ssem, rsem, to):
        return pltpu.make_async_remote_copy(
            src_ref=src, dst_ref=dst, send_sem=ssem, recv_sem=rsem, device_id=to, device_id_type=MESH
        )

    def send(src, dst, ssem, rsem, to):
        made = copy(src, dst, ssem, rsem, to)
        made.start()
        started.append(made)

    def arrive(dst, ssem, rsem, frm):
        copy(dst, dst, ssem, rsem, frm).wait_recv()

    def post(src, dst, ssem, rsem, to):
        copy(src, dst, ssem, rsem, to).start()

    def all_posted(whole, ssem):
        pltpu.make_async_copy(whole, whole, ssem).wait()

    own_rows = at(c * 512 + x * 128 + zl * 32, 32)
    far_rows = at(c * 512 + x * 128 + z * 32, 32)
    w = (embed.at[0], mlp.at[0, 0], mlp.at[0, 1])

    def weights_across(k):
        return copy(w[k], wf.at[k, far_rows], role_s.at[k], role_r.at[k], {"role": 0, "dp": mirror})

    def weights_here(k):
        return pltpu.make_async_copy(w[k], wf.at[k, far_rows], role_r.at[k])

    def patches(which, src, dst, base, o):
        rows = at(base + 32 * mp, 32)
        made = []
        for r in (1, 0):
            if o == 0 and r == 0:
                continue
            to = {"role": 1, "dp": mirror, "mp": other[o]} if r == 1 else {"role": 0, "mp": other[o]}
            made.append(copy(src.at[other[o]], dst.at[rows], x_s.at[which], x_r.at[which], to))
        return made

    def patches_here(which, src, dst, base):
        return pltpu.make_async_copy(src.at[mp], dst.at[at(base + 32 * mp, 32)], x_r.at[which])

    def patches_go(which, src, dst, base, some=(0, 1, 2, 3)):
        @pl.when(role == 0)
        def _():
            for o in some:
                for made in patches(which, src, dst, base, o):
                    made.start()
            if 0 in some:
                patches_here(which, src, dst, base).start()

    def state_part(whole, part):
        return whole.at[part // 2, pl.ds(4 * (part % 2), 4)]

    def final_part(part):
        return field.at[0, part // 2, pl.ds(4 * (part % 2), 4), pl.ds(8, 64), pl.ds(0, 128)]

    def state_across(part):
        return copy(final_part(part), state_part(passed, part), state_s.at[part], state_r.at[part],
                    {"role": 1, "dp": mirror})

    def state_here(part):
        return pltpu.make_async_copy(final_part(part), state_part(state_out, part), in_s.at[1 + part])

    def state_home(part):
        return copy(state_part(passed, part), state_part(state_out, part), state_s.at[4 + part], state_r.at[4 + part],
                    {"dp": mirror})

    def state_go(first):
        @pl.when(role == 0)
        def _():
            for part in (first, first + 1):
                state_across(part).start()
                state_here(part).start()

    def state_pass(part):
        @pl.when(role == 1)
        def _():
            state_across(part).wait_recv()
            state_home(part).start()

    @pl.when(role == 1)
    def _():
        weights_across(E).start()
        for k in (E, U, W):
            weights_here(k).start()

    def weights_go(k):
        @pl.when(role == 1)
        def _():
            weights_across(k).start()

    def patches_arrive(which, dst, base):
        arrive(dst.at[base : base + 128], x_s.at[which], x_r.at[which], east)

    lane = lax.broadcasted_iota(jnp.int32, (80, 128), 1)

    def halo_rows(i, src, dst, to):
        ends = [field.at[0, :, :, pl.ds(start, 8), pl.ds(0, 128)] for start in (src, dst)]
        return copy(ends[0], ends[1], halo_s.at[i], halo_r.at[i], to)

    def rows_go():
        for i, src, dst, to in ((0, 8, 72, before), (1, 64, 0, after)):
            halo_rows(i, src, dst, to).start()

    def columns_go():
        halo_rows(0, 72, 72, after).wait_recv()
        halo_rows(1, 0, 0, before).wait_recv()
        halo_rows(0, 8, 72, before).wait_send()
        halo_rows(1, 64, 0, after).wait_send()
        edge[...] = jnp.zeros_like(edge)
        for p in range(16):
            cells = field[0, p // 8, p % 8, :, 0:128]
            inside = (lane >= 4 * p) & (lane < 4 * p + 4)
            edge[0] = jnp.where(inside, pltpu.roll(cells, 4 * p, 1) if p else cells, edge[0])
            edge[1] = jnp.where(inside, pltpu.roll(cells, 4 * p + 4, 1), edge[1])
        send(edge.at[0], edges.at[0], halo_s.at[2], halo_r.at[2], west)
        send(edge.at[1], edges.at[1], halo_s.at[3], halo_r.at[3], east)

    def columns_arrive():
        arrive(edges.at[0], halo_s.at[2], halo_r.at[2], east)
        arrive(edges.at[1], halo_s.at[3], halo_r.at[3], west)
        for p in range(16):
            behind = edges[0] if p == 0 else pltpu.roll(edges[0], 128 - 4 * p, 1)
            ahead = pltpu.roll(edges[1], 124 - 4 * p, 1)
            field[0, p // 8, p % 8, :, 128:256] = jnp.where(lane < 4, behind, jnp.where(lane >= 124, ahead, 0.0))

    def advance(step):
        now, later = step % 2, (step + 1) % 2

        @pl.loop(0, 8)
        def _(p):
            low, high = jnp.maximum(p - 1, 0), jnp.minimum(p + 1, 7)

            def laplace(s):
                mid = field[now, s, p]
                total = field[now, s, low] + field[now, s, high]
                total = total + pltpu.roll(mid, 1, 0) + pltpu.roll(mid, 79, 0)
                total = total + pltpu.roll(mid, 1, 1) + pltpu.roll(mid, 255, 1)
                return mid, total - 6.0 * mid

            substrate, first = laplace(0)
            catalyst, second = laplace(1)
            growth = substrate * catalyst * catalyst
            field[later, 0, p] = substrate + TIME_STEP * (
                SUBSTRATE_DIFFUSION * first - growth + FEED_RATE * (1.0 - substrate)
            )
            field[later, 1, p] = catalyst + TIME_STEP * (
                CATALYST_DIFFUSION * second + growth - (FEED_RATE + KILL_RATE) * catalyst
            )

    def selection():
        feature = lax.broadcasted_iota(jnp.int32, (128, 256), 1)
        inner = lax.broadcasted_iota(jnp.int32, (128, 256), 0) % PATCH
        for r in range(PATCH):
            onehot[128 * r : 128 * r + 128, :] = jnp.where(feature == PATCH * r + inner, 1.0, 0.0).astype(BF16)

    def to_patches(dst):
        patch = lax.broadcasted_iota(jnp.int32, (8, 128), 0)
        own = lax.broadcasted_iota(jnp.int32, (8, 128), 1) // PATCH == patch

        @pl.loop(0, 4)
        def _(j):
            @pl.loop(0, 4)
            def _(q):
                species, plane = j // 2, 4 * (j % 2) + q
                for r in range(PATCH):
                    pieces = []
                    for by in range(4):
                        row = field[0, species, plane, pl.ds(8 + PATCH * by + r, 1), 0:128]
                        pieces.append(jnp.where(own, jnp.broadcast_to(row, (8, 128)), 0.0))
                    rows = pl.ds(pl.multiple_of(32 * q, 32), 32)
                    spread_in[rows, 128 * r : 128 * r + 128] = jnp.concatenate(pieces, axis=0).astype(BF16)

            moved = jnp.dot(spread_in[...], onehot[...], preferred_element_type=F32).astype(BF16)
            for q in range(4):
                dst[j, :, 256 * q : 256 * q + 256] = moved[32 * q : 32 * q + 32, :]

    zl1, zl2 = zl + 1 - 2 * (zl % 2), (zl + 2) % 4
    label = (zl, zl2, zl1, (zl1 + 2) % 4)

    def block(x_, b, c_=c):
        return c_ * 512 + x_ * 128 + label[b] * 32

    def g_send(k, i, start, size, to):
        rows = at(start, size)
        post(wf.at[k, rows], wf.at[k, rows], ag_s.at[k], ag_r.at[k, i], to)

    def g_arrive(k, i, start, size, frm):
        arrive(wf.at[k, at(start, size)], ag_s.at[k], ag_r.at[k, i], frm)

    def along_x(k, b):
        g_send(k, 3 + b, block(x, b), 32, to_x1)
        g_send(k, 7 + b, block(x, b), 32, to_x3)
        g_send(k, 12, block(x, b), 32, to_c)

    def gather0(k):
        arrive(wf.at[k, own_rows], role_s.at[k], role_r.at[k], {"role": 1 - role})
        g_send(k, 0, block(x, 0), 32, to_z2)
        g_send(k, 1, block(x, 0), 32, to_z1)
        along_x(k, 0)

    def gather1(k):
        g_arrive(k, 0, block(x, 1), 32, to_z2)
        g_send(k, 2, block(x, 1), 32, to_z1)
        along_x(k, 1)

    def gather2(k):
        g_arrive(k, 1, block(x, 2), 32, to_z1)
        along_x(k, 2)
        g_arrive(k, 2, block(x, 3), 32, to_z1)
        along_x(k, 3)

    def gather3(k, some):
        for b in some:
            g_arrive(k, 3 + b, block(x1, b), 32, to_x1)
            g_send(k, 11, block(x1, b), 16, to_x3)
            g_send(k, 12, block(x1, b), 32, to_c)
            g_arrive(k, 7 + b, block(x3, b), 32, to_x3)
            g_send(k, 11, block(x3, b) + 16, 16, to_x1)
            g_send(k, 12, block(x3, b), 32, to_c)

    def gather4(k):
        g_arrive(k, 11, c * 512 + x2 * 128, 128, to_x1)
        g_send(k, 12, c * 512 + x2 * 128, 128, to_c)

    def gather5(k):
        g_arrive(k, 12, c1 * 512, 512, to_c)

    def tiles(width, body):
        @pl.loop(0, COLS // width)
        def _(t):
            body(pl.ds(pl.multiple_of(t * width, width), width))

    def with_rows(lhs, k, rows):
        return lax.dot_general(lhs, wf[k, rows, :], (((1,), (1,)), ((), ())), preferred_element_type=F32)

    def with_cols(lhs, k, cols):
        return jnp.dot(lhs, wf[k, :, cols], preferred_element_type=F32)

    mine = at(32 * mp, 32)

    def half(s):
        return pl.ds(512 * s, 512)

    def partial_sums(i, lhs, k):
        for s in (0, 1):

            @pl.loop(0, 2)
            def _(t):
                cols = pl.ds(pl.multiple_of(512 * s + 256 * t, 256), 256)
                value = with_rows(lhs[...], k, cols)
                part[:, cols] = value
                sbuf[i, :, cols] = value.astype(BF16)

            for o in (2, 1, 3):
                post(sbuf.at[i, at(32 * other[o], 32), half(s)], rbuf.at[i, o - 1, :, half(s)],
                     rs_s.at[0], rs_r.at[i, s], {"mp": other[o]})

    def summed(i, s):
        total = part[mine, half(s)]
        arrive(rbuf.at[i, :, :, half(s)], rs_s.at[0], rs_r.at[i, s], east)
        for o in (1, 2, 3):
            total = total + rbuf[i, o - 1, :, half(s)].astype(F32)
        return total

    def all_summed(i):
        return jnp.concatenate([summed(i, 0), summed(i, 1)], axis=1)

    def spread(i, s, dst, base, value):
        rows = at(base + 32 * mp, 32)
        dst[rows, half(s)] = value
        for o in (2, 1, 3):
            post(dst.at[rows, half(s)], dst.at[rows, half(s)], mg_s.at[0], mg_r.at[i], {"mp": other[o]})

    def spread_all(i, dst, base, value):
        for s in (0, 1):
            spread(i, s, dst, base, value[:, 512 * s : 512 * s + 512])

    def spread_arrive(i, dst, base):
        arrive(dst.at[base : base + 96], mg_s.at[0], mg_r.at[i], east)

    pieces = {"W": (0, W, 0, 512), "U": (1, U, 0, 512)}
    parts = ("E0", "E1", "E2", "E3")
    pieces.update({name: (2 + i, E, 256 * i, 256) for i, name in enumerate(parts)})

    def in_matrix(group, k, first, width):
        return pl.ds(first, width) if k == E else pl.ds(pl.multiple_of(512 * group + first, 512), width)

    def product(piece, lhs, rhs, core, store):
        _, k, first, width = pieces[piece]

        @pl.loop(0, 2)
        def _(t):
            rows = pl.ds(pl.multiple_of(core * 512 + t * 256, 256), 256)
            local = pl.ds(pl.multiple_of(t * 256, 256), 256)
            store(local, pl.ds(first, width), lax.dot_general(
                lhs[:, rows], rhs[:, in_matrix(role, k, first, width)], (((0,), (0,)), ((), ())),
                preferred_element_type=F32,
            ))

    def r_copy(piece, i, src, dst, to):
        n = pieces[piece][0]
        return copy(src, dst, gr_s.at[n if i < 7 else 6 + n], gr_r.at[n, i], to)

    def r_send(piece, i, src, dst, to):
        r_copy(piece, i, src, dst, to).start()

    def r_posted(piece):
        n, k, first, width = pieces[piece]
        all_posted(wf.at[k, 0:992, 0:width], gr_s.at[n])
        if k != E:
            all_posted(total_rows.at[k, :, 0:width], gr_s.at[6 + n])

    def terms_across(piece, lhs, rhs):
        _, k, first, width = pieces[piece]

        def store(local, cols, value):
            cs[k, local, cols] = value.astype(BF16)

        product(piece, lhs, rhs, c1, store)
        whole = (k, slice(None), pl.ds(first, width))
        r_send(piece, 0, cs.at[whole], cr.at[whole], to_c)

    def terms_here(piece, lhs, rhs):
        k = pieces[piece][1]

        def store(local, cols, value):
            acc[k, local, cols] = value

        product(piece, lhs, rhs, c, store)

    def chunks(count, body):
        @pl.loop(0, count)
        def _(t):
            body(pl.multiple_of(t * 32, 32))

    def pair(k, start, cols):
        return acc[k, pl.ds(start, 32), cols] + cr[k, pl.ds(start, 32), cols].astype(F32)

    def reduce1(piece):
        _, k, first, width = pieces[piece]
        cols = pl.ds(first, width)
        r_copy(piece, 0, cr.at[k, :, cols], cr.at[k, :, cols], to_c).wait_recv()

        def body(t):
            for h, far in ((0, x3), (1, x1)):
                for i, xb in ((0, far), (1, x2)):
                    value = pair(k, pl.multiple_of(xb * 128 + h * 64 + t, 32), cols)
                    xs1[k, h, i, pl.ds(t, 32), cols] = value.astype(BF16)

        chunks(2, body)
        for h, to in ((0, to_x3), (1, to_x1)):
            r_send(piece, 1 + h, xs1.at[k, h, :, :, cols], xr1.at[k, h, :, :, cols], to)

    def reduce2(piece):
        _, k, first, width = pieces[piece]
        cols = pl.ds(first, width)
        for h, frm in ((0, to_x3), (1, to_x1)):
            r_copy(piece, 1 + h, xr1.at[k, h, :, :, cols], xr1.at[k, h, :, :, cols], frm).wait_recv()

        def body(t):
            for h, near in ((0, x1), (1, x3)):
                value = pair(k, pl.multiple_of(near * 128 + h * 64 + t, 32), cols)
                xs2[k, h, pl.ds(t, 32), cols] = (value + xr1[k, h, 1, pl.ds(t, 32), cols].astype(F32)).astype(BF16)

        chunks(2, body)
        for h, to in ((0, to_x1), (1, to_x3)):
            r_send(piece, 3 + h, xs2.at[k, h, :, cols], xr2.at[k, h, :, cols], to)

    def reduce3(piece):
        _, k, first, width = pieces[piece]
        cols = pl.ds(first, width)
        for h, frm in ((0, to_x1), (1, to_x3)):
            r_copy(piece, 3 + h, xr2.at[k, h, :, cols], xr2.at[k, h, :, cols], frm).wait_recv()

        def body(t):
            for h in (0, 1):
                value = pair(k, pl.multiple_of(x * 128 + h * 64 + t, 32), cols)
                value = value + xr1[k, h, 0, pl.ds(t, 32), cols].astype(F32) + xr2[k, h, pl.ds(t, 32), cols].astype(F32)
                vsum[k, pl.ds(pl.multiple_of(h * 64 + t, 32), 32), cols] = value

        chunks(2, body)
        zs1[k, 0, :, cols] = vsum[k, at(z1 * 32, 32), cols].astype(BF16)
        zs1[k, 1, :, cols] = vsum[k, at(z3 * 32, 32), cols].astype(BF16)
        r_send(piece, 5, zs1.at[k, :, :, cols], zr1.at[k, :, :, cols], to_z1)

    def reduce4(piece):
        _, k, first, width = pieces[piece]
        cols = pl.ds(first, width)
        r_copy(piece, 5, zr1.at[k, :, :, cols], zr1.at[k, :, :, cols], to_z1).wait_recv()
        zs2[k, :, cols] = (vsum[k, at(z2 * 32, 32), cols] + zr1[k, 1, :, cols].astype(F32)).astype(BF16)
        r_send(piece, 6, zs2.at[k, :, cols], zr2.at[k, :, cols], to_z2)

    def result(piece):
        n, k, first, width = pieces[piece]
        part = (k, slice(None), pl.ds(first, width) if k == E else slice(None))
        return pltpu.make_async_copy(total_rows.at[part], out.at[part], in_s.at[5 + n])

    def reduce5(piece):
        _, k, first, width = pieces[piece]
        cols = pl.ds(first, width)
        r_copy(piece, 6, zr2.at[k, :, cols], zr2.at[k, :, cols], to_z2).wait_recv()
        total = vsum[k, at(z * 32, 32), cols] + zr1[k, 0, :, cols].astype(F32)
        here = total_rows.at[k, :, in_matrix(role, k, first, width)]
        here[...] = total + zr2[k, :, cols].astype(F32)
        if k != E:
            r_send(piece, 7, here, here, {"role": 1 - role})
        else:
            result(piece).start()

    def reduced(piece):
        _, k, first, width = pieces[piece]
        there = total_rows.at[k, :, in_matrix(1 - role, k, first, width)]
        r_copy(piece, 7, there, there, {"role": 1 - role}).wait_recv()
        result(piece).start()

    center.wait()
    rows_go()
    selection()
    to_patches(xs)
    gather0(E)
    weights_go(U)
    patches_go(0, xs, px, 128, (2, 0))
    columns_go()
    gather1(E)
    weights_go(W)
    patches_go(0, xs, px, 128, (1, 3))
    gather0(U)
    gather3(E, (0,))
    gather2(E)
    columns_arrive()
    gather3(E, (1,))
    advance(0)
    gather1(U)
    gather0(W)
    advance(1)
    gather3(E, (2, 3))
    advance(2)
    gather2(U)
    gather1(W)
    gather3(U, (0, 1))
    advance(3)
    gather4(E)
    gather5(E)

    patches_arrive(0, px, 128)
    partial_sums(0, px.at[128:256], E)
    to_patches(ts)
    patches_go(1, ts, tg, 0)
    gather3(U, (2, 3))
    gather2(W)
    gather3(W, (0, 1))
    e = all_summed(0)
    recip = lax.rsqrt(jnp.mean(e * e, axis=1, keepdims=True) + 1e-06)
    ered[...] = e
    spread_all(0, nf, 0, (e * recip).astype(BF16))
    gather4(U)
    gather3(W, (2, 3))
    gather5(U)
    spread_arrive(0, nf, 0)

    def hidden(cols):
        pre = with_cols(nf[...], U, cols)
        square = pre * pre
        tangent = jnp.tanh(GELU_FACTOR * (pre + 0.044715 * square * pre))
        act[:, cols] = (0.5 * pre * (1.0 + tangent)).astype(BF16)
        slope[:, cols] = 0.5 * (1.0 + tangent) + 0.5 * pre * (1.0 - tangent * tangent) * GELU_FACTOR * (
            1.0 + 3.0 * 0.044715 * square
        )

    tiles(256, hidden)
    gather4(W)
    gather5(W)
    partial_sums(1, act, W)
    state_go(0)
    for s in (0, 1):
        spread(1, s, yd, 0, (ered[:, half(s)] + summed(1, s)).astype(BF16))
    patches_arrive(1, tg, 0)
    spread_arrive(1, yd, 0)

    def residual(cols):
        pred = px[128:256, cols].astype(F32) + with_cols(yd[0:128, :], E, cols)
        px[0:128, cols] = ((pred - tg[:, cols].astype(F32)) * (1.0 / 64.0)).astype(BF16)

    tiles(256, residual)
    partial_sums(2, px.at[0:128], E)
    state_go(2)
    for s in (0, 1):
        dy = summed(2, s)
        dyred[:, half(s)] = dy
        spread(2, s, dyf, 0, dy.astype(BF16))
    state_pass(0)
    spread_arrive(2, dyf, 0)
    terms_across("W", dyf, act)
    terms_here("W", dyf, act)

    def hidden_back(cols):
        dhid[:, cols] = (with_cols(dyf[...], W, cols) * slope[:, cols]).astype(BF16)

    reduce1("W")
    state_pass(1)
    tiles(256, hidden_back)
    partial_sums(3, dhid, U)
    terms_across("U", nf, dhid)
    terms_here("U", nf, dhid)
    reduce1("U")
    state_pass(2)
    reduce2("W")
    dn = all_summed(3)
    e = ered[...]
    recip = lax.rsqrt(jnp.mean(e * e, axis=1, keepdims=True) + 1e-06)
    de = dyred[...] + recip * dn - e * (recip * recip * recip) * jnp.mean(dn * e, axis=1, keepdims=True)
    spread_all(3, yd, 128, de.astype(BF16))
    state_pass(3)
    reduce3("W")
    reduce2("U")
    spread_arrive(3, yd, 128)
    for piece in parts:
        terms_across(piece, yd, px)
    reduce4("W")
    reduce3("U")
    for piece in parts:
        terms_here(piece, yd, px)
        reduce1(piece)
    reduce5("W")
    reduce4("U")
    reduce2("E0")
    reduce2("E1")
    reduce2("E2")
    reduce5("U")
    reduce2("E3")
    for piece in parts:
        reduce3(piece)
    for piece in parts:
        reduce4(piece)
    reduced("W")
    reduced("U")
    for piece in parts:
        reduce5(piece)

    for made in started:
        made.wait_send()
    for k in (E, U, W):
        all_posted(wf.at[k, 0:992], ag_s.at[k])
    all_posted(sbuf.at[0:3], rs_s.at[0])
    all_posted(sbuf.at[0:3], mg_s.at[0])
    for piece in pieces:
        r_posted(piece)
        result(piece).wait()

    @pl.when(role == 1)
    def _():
        for k in (E, U, W):
            weights_across(k).wait_send()
        for part in range(4):
            state_home(part).wait()

    @pl.when(role == 0)
    def _():
        for which in (0, 1):
            all_posted(px.at[0:224], x_s.at[which])
        for part in range(4):
            state_across(part).wait_send()
            state_here(part).wait()


def train(state, embed, mlp):
    dma = pltpu.SemaphoreType.DMA
    return pl.pallas_call(
        kernel,
        name="train",
        out_shape=(jax.ShapeDtypeStruct((3, OWN, COLS), F32), jax.ShapeDtypeStruct(state.shape[1:], F32)),
        in_specs=[pl.BlockSpec(memory_space=pltpu.HBM)] * 3,
        out_specs=(pl.BlockSpec(memory_space=pl.ANY), pl.BlockSpec(memory_space=pl.ANY)),
        scratch_shapes=[
            pltpu.VMEM((3, OWN, COLS), F32),
            pltpu.VMEM((2, 2, 8, 80, 256), F32),
            pltpu.VMEM((2, 8, 64, 128), F32),
            pltpu.VMEM((2, 80, 128), F32),
            pltpu.VMEM((2, 80, 128), F32),
            pltpu.VMEM((2048, 256), BF16),
            pltpu.VMEM((128, 2048), BF16),
            pltpu.VMEM((4, OWN, COLS), BF16),
            pltpu.VMEM((4, OWN, COLS), BF16),
            pltpu.VMEM((3, D, COLS), BF16),
            pltpu.VMEM((2 * ROWS, COLS), BF16),
            pltpu.VMEM((2 * ROWS, D), BF16),
            pltpu.VMEM((ROWS, COLS), BF16),
            pltpu.VMEM((ROWS, D), F32),
            pltpu.VMEM((4, ROWS, D), BF16),
            pltpu.VMEM((4, 3, OWN, D), BF16),
            pltpu.VMEM((ROWS, D), BF16),
            pltpu.VMEM((ROWS, D), BF16),
            pltpu.VMEM((ROWS, COLS), BF16),
            pltpu.VMEM((ROWS, COLS), F32),
            pltpu.VMEM((ROWS, COLS), BF16),
            pltpu.VMEM((OWN, D), F32),
            pltpu.VMEM((OWN, D), F32),
            pltpu.VMEM((3, 512, COLS), F32),
            pltpu.VMEM((3, 512, COLS), BF16),
            pltpu.VMEM((3, 512, COLS), BF16),
            pltpu.VMEM((3, 2, 2, 64, COLS), BF16),
            pltpu.VMEM((3, 2, 2, 64, COLS), BF16),
            pltpu.VMEM((3, 2, 64, COLS), BF16),
            pltpu.VMEM((3, 2, 64, COLS), BF16),
            pltpu.VMEM((3, 128, COLS), F32),
            pltpu.VMEM((3, 2, OWN, COLS), BF16),
            pltpu.VMEM((3, 2, OWN, COLS), BF16),
            pltpu.VMEM((3, OWN, COLS), BF16),
            pltpu.VMEM((3, OWN, COLS), BF16),
            dma((11,)), dma((4,)), dma((4,)), dma((8,)), dma((8,)),
            dma((3,)), dma((3,)),
            dma((2,)), dma((2,)),
            dma((3,)), dma((3, 13)),
            dma((1,)), dma((4, 2)),
            dma((1,)), dma((4,)),
            dma((8,)), dma((6, 8)),
        ],
        compiler_params=pltpu.CompilerParams(
            collective_id=0, has_side_effects=True, vmem_limit_bytes=60 * 1024 * 1024
        ),
        cost_estimate=pl.CostEstimate(flops=6 * 10**9, bytes_accessed=4 * 10**8, transcendentals=10**5),
    )(state, embed, mlp)


def shards(state, embed, mlp, mom_embed, mom_mlp):
    grads, state_out = train(state, embed, mlp)
    mom_embed_out = MOMENTUM_DECAY * mom_embed + grads[:1]
    mom_mlp_out = MOMENTUM_DECAY * mom_mlp + grads[None, 1:]
    embed_out = (embed.astype(F32) - LEARNING_RATE * mom_embed_out).astype(BF16)
    mlp_out = (mlp.astype(F32) - LEARNING_RATE * mom_mlp_out).astype(BF16)
    return (state_out, embed_out, mlp_out, mom_embed_out, mom_mlp_out)


def solution(mesh):
    placed = (
        P("role", None, None, "dp", "mp"),
        P("role", "dp", "mp"),
        P("role", None, "dp", "mp"),
        P("role", "dp", "mp"),
        P("role", None, "dp", "mp"),
    )
    return jax.shard_map(
        shards,
        mesh=mesh,
        in_specs=placed,
        out_specs=(
            P(None, None, "dp", "mp"),
            P("role", "dp", "mp"),
            P("role", None, "dp", "mp"),
            P("role", "dp", "mp"),
            P("role", None, "dp", "mp"),
        ),
        check_vma=False,
    )
```

```python
import jax
import jax.numpy as jnp
from jax import lax
from jax.experimental import pallas as pl
from jax.experimental.pallas import tpu as pltpu
from jax.sharding import PartitionSpec as P

PATCH = 16
STEPS = 4


SUBSTRATE_DIFFUSION = 0.2
CATALYST_DIFFUSION = 0.1
FEED_RATE = 0.037
KILL_RATE = 0.06
TIME_STEP = 0.8
GELU_FACTOR = 0.7978845608028654
MOMENTUM_DECAY = 0.9
LEARNING_RATE = 0.003

BF16 = jnp.bfloat16
F32 = jnp.float32
MESH = pl.DeviceIdType.MESH
ROWS = 128
OWN = 32
D = 1024
COLS = 1024
E, U, W = 0, 1, 2


def kernel(
    state, embed, mlp, out, state_out,
    total_rows, field, final, passed, edge, edges, onehot, spread_in, xs, ts, wf, px, yd, tg, part, sbuf, rbuf, nf, dyf, act, slope, dhid, ered, dyred,
    acc, cs, cr, xs1, xr1, xs2, xr2, vsum, zs1, zr1, zs2, zr2,
    in_s, halo_s, halo_r, state_s, state_r, role_s, role_r, x_s, x_r, ag_s, ag_r, rs_s, rs_r, mg_s, mg_r, gr_s, gr_r,
):
    role = lax.axis_index("role")
    dp = lax.axis_index("dp")
    mp = lax.axis_index("mp")
    x, z, c = dp // 8, (dp // 2) % 4, dp % 2

    def dev(x_, z_, c_):
        return {"dp": (x_ * 4 + z_) * 2 + c_}

    x1, x2, x3 = x + 1 - 2 * (x % 2), (x + 2) % 4, 3 - x
    z1, z2 = z + 1 - 2 * (z % 2), (z + 2) % 4
    z3 = (z1 + 2) % 4
    c1 = 1 - c
    zm = 3 - z
    zl = jnp.where(role == 1, z, zm)
    to_c, to_x1, to_x3 = dev(x, z, c1), dev(x1, z, c), dev(x3, z, c)
    to_z1, to_z2 = dev(x, z1, c), dev(x, z2, c)
    after, before = {"dp": (dp + 1) % 32}, {"dp": (dp + 31) % 32}
    east, west = {"mp": (mp + 1) % 4}, {"mp": (mp + 3) % 4}
    mirror = dev(x, zm, c)["dp"]
    center = pltpu.make_async_copy(
        state.at[0], field.at[0, :, :, pl.ds(8, 64), pl.ds(0, 128)], in_s.at[0]
    )
    center.start()
    other = [(mp + o) % 4 for o in range(4)]

    def at(start, size):
        return pl.ds(pl.multiple_of(start, 16), size)

    barrier = pltpu.get_barrier_semaphore()
    friends = [to_c, to_x1, to_x3, to_z1, to_z2, after, before, {"dp": mirror}, {"role": 1 - role}]
    friends += [{"mp": other[o]} for o in (1, 2, 3)]
    friends += [{"role": 1 - role, "dp": mirror, "mp": other[o]} for o in range(4)]
    for friend in friends:
        pl.semaphore_signal(barrier, inc=1, device_id=friend, device_id_type=MESH)
    pl.semaphore_wait(barrier, len(friends))

    started = []

    def copy(src, dst, ssem, rsem, to):
        return pltpu.make_async_remote_copy(
            src_ref=src, dst_ref=dst, send_sem=ssem, recv_sem=rsem, device_id=to, device_id_type=MESH
        )

    def send(src, dst, ssem, rsem, to):
        made = copy(src, dst, ssem, rsem, to)
        made.start()
        started.append(made)

    def arrive(dst, ssem, rsem, frm):
        copy(dst, dst, ssem, rsem, frm).wait_recv()

    def post(src, dst, ssem, rsem, to):
        copy(src, dst, ssem, rsem, to).start()

    def all_posted(whole, ssem):
        pltpu.make_async_copy(whole, whole, ssem).wait()

    own_rows = at(c * 512 + x * 128 + zl * 32, 32)
    far_rows = at(c * 512 + x * 128 + z * 32, 32)
    w = (embed.at[0], mlp.at[0, 0], mlp.at[0, 1])

    def weights_across(k):
        return copy(w[k], wf.at[k, far_rows], role_s.at[k], role_r.at[k], {"role": 0, "dp": mirror})

    def weights_here(k):
        return pltpu.make_async_copy(w[k], wf.at[k, far_rows], role_r.at[k])

    def patches(which, src, dst, base, o):
        rows = at(base + 32 * mp, 32)
        made = []
        for r in (1, 0):
            if o == 0 and r == 0:
                continue
            to = {"role": 1, "dp": mirror, "mp": other[o]} if r == 1 else {"role": 0, "mp": other[o]}
            made.append(copy(src.at[other[o]], dst.at[rows], x_s.at[which], x_r.at[which], to))
        return made

    def patches_here(which, src, dst, base):
        return pltpu.make_async_copy(src.at[mp], dst.at[at(base + 32 * mp, 32)], x_r.at[which])

    def patches_go(which, src, dst, base, some=(0, 1, 2, 3)):
        @pl.when(role == 0)
        def _():
            for o in some:
                for made in patches(which, src, dst, base, o):
                    made.start()
            if 0 in some:
                patches_here(which, src, dst, base).start()

    def state_part(whole, part):
        return whole.at[part // 2, pl.ds(4 * (part % 2), 4)]

    def state_across(part):
        return copy(state_part(final, part), state_part(passed, part), state_s.at[part], state_r.at[part],
                    {"role": 1, "dp": mirror})

    def state_home(part):
        return copy(state_part(passed, part), state_part(final, part), state_s.at[4 + part], state_r.at[4 + part],
                    {"dp": mirror})

    def state_here(part):
        rounded = field.at[1, part // 2, pl.ds(4 * (part % 2), 4), pl.ds(8, 64), pl.ds(0, 128)]
        return pltpu.make_async_copy(rounded, state_part(state_out, part), in_s.at[1 + part])

    def state_widen(part):
        species, planes = part // 2, pl.ds(4 * (part % 2), 4)
        field[1, species, planes, 8:72, 0:128] = final[species, planes].astype(F32)
        state_here(part).start()

    def state_go():
        @pl.when(role == 0)
        def _():
            for part in range(4):
                species, planes = part // 2, pl.ds(4 * (part % 2), 4)
                final[species, planes] = field[0, species, planes, 8:72, 0:128].astype(BF16)
                state_across(part).start()
            for part in range(4):
                state_widen(part)

    def state_arrive():
        @pl.when(role == 1)
        def _():
            for part in range(4):
                state_home(part).wait_recv()
                state_widen(part)

    def state_pass(part):
        @pl.when(role == 1)
        def _():
            state_across(part).wait_recv()
            state_home(part).start()

    @pl.when(role == 1)
    def _():
        weights_across(E).start()
        for k in (E, U, W):
            weights_here(k).start()

    def weights_go(k):
        @pl.when(role == 1)
        def _():
            weights_across(k).start()

    def patches_arrive(which, dst, base):
        arrive(dst.at[base : base + 128], x_s.at[which], x_r.at[which], east)

    lane = lax.broadcasted_iota(jnp.int32, (80, 128), 1)

    def halo_rows(i, src, dst, to):
        ends = [field.at[0, :, :, pl.ds(start, 8), pl.ds(0, 128)] for start in (src, dst)]
        return copy(ends[0], ends[1], halo_s.at[i], halo_r.at[i], to)

    def rows_go():
        for i, src, dst, to in ((0, 8, 72, before), (1, 64, 0, after)):
            halo_rows(i, src, dst, to).start()

    def columns_go():
        halo_rows(0, 72, 72, after).wait_recv()
        halo_rows(1, 0, 0, before).wait_recv()
        halo_rows(0, 8, 72, before).wait_send()
        halo_rows(1, 64, 0, after).wait_send()
        edge[...] = jnp.zeros_like(edge)
        for p in range(16):
            cells = field[0, p // 8, p % 8, :, 0:128]
            inside = (lane >= 4 * p) & (lane < 4 * p + 4)
            edge[0] = jnp.where(inside, pltpu.roll(cells, 4 * p, 1) if p else cells, edge[0])
            edge[1] = jnp.where(inside, pltpu.roll(cells, 4 * p + 4, 1), edge[1])
        send(edge.at[0], edges.at[0], halo_s.at[2], halo_r.at[2], west)
        send(edge.at[1], edges.at[1], halo_s.at[3], halo_r.at[3], east)

    def columns_arrive():
        arrive(edges.at[0], halo_s.at[2], halo_r.at[2], east)
        arrive(edges.at[1], halo_s.at[3], halo_r.at[3], west)
        for p in range(16):
            behind = edges[0] if p == 0 else pltpu.roll(edges[0], 128 - 4 * p, 1)
            ahead = pltpu.roll(edges[1], 124 - 4 * p, 1)
            field[0, p // 8, p % 8, :, 128:256] = jnp.where(lane < 4, behind, jnp.where(lane >= 124, ahead, 0.0))

    def advance(step):
        now, later = step % 2, (step + 1) % 2

        @pl.loop(0, 8)
        def _(p):
            low, high = jnp.maximum(p - 1, 0), jnp.minimum(p + 1, 7)

            def laplace(s):
                mid = field[now, s, p]
                total = field[now, s, low] + field[now, s, high]
                total = total + pltpu.roll(mid, 1, 0) + pltpu.roll(mid, 79, 0)
                total = total + pltpu.roll(mid, 1, 1) + pltpu.roll(mid, 255, 1)
                return mid, total - 6.0 * mid

            substrate, first = laplace(0)
            catalyst, second = laplace(1)
            growth = substrate * catalyst * catalyst
            field[later, 0, p] = substrate + TIME_STEP * (
                SUBSTRATE_DIFFUSION * first - growth + FEED_RATE * (1.0 - substrate)
            )
            field[later, 1, p] = catalyst + TIME_STEP * (
                CATALYST_DIFFUSION * second + growth - (FEED_RATE + KILL_RATE) * catalyst
            )

    def selection():
        feature = lax.broadcasted_iota(jnp.int32, (128, 256), 1)
        inner = lax.broadcasted_iota(jnp.int32, (128, 256), 0) % PATCH
        for r in range(PATCH):
            onehot[128 * r : 128 * r + 128, :] = jnp.where(feature == PATCH * r + inner, 1.0, 0.0).astype(BF16)

    def to_patches(dst):
        patch = lax.broadcasted_iota(jnp.int32, (8, 128), 0)
        own = lax.broadcasted_iota(jnp.int32, (8, 128), 1) // PATCH == patch

        @pl.loop(0, 4)
        def _(j):
            @pl.loop(0, 4)
            def _(q):
                species, plane = j // 2, 4 * (j % 2) + q
                for r in range(PATCH):
                    pieces = []
                    for by in range(4):
                        row = field[0, species, plane, pl.ds(8 + PATCH * by + r, 1), 0:128]
                        pieces.append(jnp.where(own, jnp.broadcast_to(row, (8, 128)), 0.0))
                    rows = pl.ds(pl.multiple_of(32 * q, 32), 32)
                    spread_in[rows, 128 * r : 128 * r + 128] = jnp.concatenate(pieces, axis=0).astype(BF16)

            moved = jnp.dot(spread_in[...], onehot[...], preferred_element_type=F32).astype(BF16)
            for q in range(4):
                dst[j, :, 256 * q : 256 * q + 256] = moved[32 * q : 32 * q + 32, :]

    zl1, zl2 = zl + 1 - 2 * (zl % 2), (zl + 2) % 4
    label = (zl, zl2, zl1, (zl1 + 2) % 4)

    def block(x_, b, c_=c):
        return c_ * 512 + x_ * 128 + label[b] * 32

    def g_send(k, i, start, size, to):
        rows = at(start, size)
        post(wf.at[k, rows], wf.at[k, rows], ag_s.at[k], ag_r.at[k, i], to)

    def g_arrive(k, i, start, size, frm):
        arrive(wf.at[k, at(start, size)], ag_s.at[k], ag_r.at[k, i], frm)

    def along_x(k, b):
        g_send(k, 3 + b, block(x, b), 32, to_x1)
        g_send(k, 7 + b, block(x, b), 32, to_x3)
        g_send(k, 12, block(x, b), 32, to_c)

    def gather0(k):
        arrive(wf.at[k, own_rows], role_s.at[k], role_r.at[k], {"role": 1 - role})
        g_send(k, 0, block(x, 0), 32, to_z2)
        g_send(k, 1, block(x, 0), 32, to_z1)
        along_x(k, 0)

    def gather1(k):
        g_arrive(k, 0, block(x, 1), 32, to_z2)
        g_send(k, 2, block(x, 1), 32, to_z1)
        along_x(k, 1)

    def gather2(k):
        g_arrive(k, 1, block(x, 2), 32, to_z1)
        along_x(k, 2)
        g_arrive(k, 2, block(x, 3), 32, to_z1)
        along_x(k, 3)

    def gather3(k, some):
        for b in some:
            g_arrive(k, 3 + b, block(x1, b), 32, to_x1)
            g_send(k, 11, block(x1, b), 16, to_x3)
            g_send(k, 12, block(x1, b), 32, to_c)
            g_arrive(k, 7 + b, block(x3, b), 32, to_x3)
            g_send(k, 11, block(x3, b) + 16, 16, to_x1)
            g_send(k, 12, block(x3, b), 32, to_c)

    def gather4(k):
        g_arrive(k, 11, c * 512 + x2 * 128, 128, to_x1)
        g_send(k, 12, c * 512 + x2 * 128, 128, to_c)

    def gather5(k):
        g_arrive(k, 12, c1 * 512, 512, to_c)

    def tiles(width, body):
        @pl.loop(0, COLS // width)
        def _(t):
            body(pl.ds(pl.multiple_of(t * width, width), width))

    def with_rows(lhs, k, rows):
        return lax.dot_general(lhs, wf[k, rows, :], (((1,), (1,)), ((), ())), preferred_element_type=F32)

    def with_cols(lhs, k, cols):
        return jnp.dot(lhs, wf[k, :, cols], preferred_element_type=F32)

    mine = at(32 * mp, 32)

    def half(s):
        return pl.ds(512 * s, 512)

    def partial_sums(i, lhs, k):
        for s in (0, 1):

            @pl.loop(0, 2)
            def _(t):
                cols = pl.ds(pl.multiple_of(512 * s + 256 * t, 256), 256)
                value = with_rows(lhs[...], k, cols)
                part[:, cols] = value
                sbuf[i, :, cols] = value.astype(BF16)

            for o in (2, 1, 3):
                post(sbuf.at[i, at(32 * other[o], 32), half(s)], rbuf.at[i, o - 1, :, half(s)],
                     rs_s.at[0], rs_r.at[i, s], {"mp": other[o]})

    def summed(i, s):
        total = part[mine, half(s)]
        arrive(rbuf.at[i, :, :, half(s)], rs_s.at[0], rs_r.at[i, s], east)
        for o in (1, 2, 3):
            total = total + rbuf[i, o - 1, :, half(s)].astype(F32)
        return total

    def all_summed(i):
        return jnp.concatenate([summed(i, 0), summed(i, 1)], axis=1)

    def spread(i, s, dst, base, value):
        rows = at(base + 32 * mp, 32)
        dst[rows, half(s)] = value
        for o in (2, 1, 3):
            post(dst.at[rows, half(s)], dst.at[rows, half(s)], mg_s.at[0], mg_r.at[i], {"mp": other[o]})

    def spread_all(i, dst, base, value):
        for s in (0, 1):
            spread(i, s, dst, base, value[:, 512 * s : 512 * s + 512])

    def spread_arrive(i, dst, base):
        arrive(dst.at[base : base + 96], mg_s.at[0], mg_r.at[i], east)

    pieces = {"W": (0, W, 0, 512), "U": (1, U, 0, 512)}
    parts = ("E0", "E1", "E2", "E3")
    pieces.update({name: (2 + i, E, 256 * i, 256) for i, name in enumerate(parts)})

    def in_matrix(group, k, first, width):
        return pl.ds(first, width) if k == E else pl.ds(pl.multiple_of(512 * group + first, 512), width)

    def product(piece, lhs, rhs, core, store):
        _, k, first, width = pieces[piece]

        @pl.loop(0, 2)
        def _(t):
            rows = pl.ds(pl.multiple_of(core * 512 + t * 256, 256), 256)
            local = pl.ds(pl.multiple_of(t * 256, 256), 256)
            store(local, pl.ds(first, width), lax.dot_general(
                lhs[:, rows], rhs[:, in_matrix(role, k, first, width)], (((0,), (0,)), ((), ())),
                preferred_element_type=F32,
            ))

    def r_copy(piece, i, src, dst, to):
        n = pieces[piece][0]
        return copy(src, dst, gr_s.at[n if i < 7 else 6 + n], gr_r.at[n, i], to)

    def r_send(piece, i, src, dst, to):
        r_copy(piece, i, src, dst, to).start()

    def r_posted(piece):
        n, k, first, width = pieces[piece]
        all_posted(wf.at[k, 0:992, 0:width], gr_s.at[n])
        if k != E:
            all_posted(total_rows.at[k, :, 0:width], gr_s.at[6 + n])

    def terms_across(piece, lhs, rhs):
        _, k, first, width = pieces[piece]

        def store(local, cols, value):
            cs[k, local, cols] = value.astype(BF16)

        product(piece, lhs, rhs, c1, store)
        whole = (k, slice(None), pl.ds(first, width))
        r_send(piece, 0, cs.at[whole], cr.at[whole], to_c)

    def terms_here(piece, lhs, rhs):
        k = pieces[piece][1]

        def store(local, cols, value):
            acc[k, local, cols] = value

        product(piece, lhs, rhs, c, store)

    def chunks(count, body):
        @pl.loop(0, count)
        def _(t):
            body(pl.multiple_of(t * 32, 32))

    def pair(k, start, cols):
        return acc[k, pl.ds(start, 32), cols] + cr[k, pl.ds(start, 32), cols].astype(F32)

    def reduce1(piece):
        _, k, first, width = pieces[piece]
        cols = pl.ds(first, width)
        r_copy(piece, 0, cr.at[k, :, cols], cr.at[k, :, cols], to_c).wait_recv()

        def body(t):
            for h, far in ((0, x3), (1, x1)):
                for i, xb in ((0, far), (1, x2)):
                    value = pair(k, pl.multiple_of(xb * 128 + h * 64 + t, 32), cols)
                    xs1[k, h, i, pl.ds(t, 32), cols] = value.astype(BF16)

        chunks(2, body)
        for h, to in ((0, to_x3), (1, to_x1)):
            r_send(piece, 1 + h, xs1.at[k, h, :, :, cols], xr1.at[k, h, :, :, cols], to)

    def reduce2(piece):
        _, k, first, width = pieces[piece]
        cols = pl.ds(first, width)
        for h, frm in ((0, to_x3), (1, to_x1)):
            r_copy(piece, 1 + h, xr1.at[k, h, :, :, cols], xr1.at[k, h, :, :, cols], frm).wait_recv()

        def body(t):
            for h, near in ((0, x1), (1, x3)):
                value = pair(k, pl.multiple_of(near * 128 + h * 64 + t, 32), cols)
                xs2[k, h, pl.ds(t, 32), cols] = (value + xr1[k, h, 1, pl.ds(t, 32), cols].astype(F32)).astype(BF16)

        chunks(2, body)
        for h, to in ((0, to_x1), (1, to_x3)):
            r_send(piece, 3 + h, xs2.at[k, h, :, cols], xr2.at[k, h, :, cols], to)

    def reduce3(piece):
        _, k, first, width = pieces[piece]
        cols = pl.ds(first, width)
        for h, frm in ((0, to_x1), (1, to_x3)):
            r_copy(piece, 3 + h, xr2.at[k, h, :, cols], xr2.at[k, h, :, cols], frm).wait_recv()

        def body(t):
            for h in (0, 1):
                value = pair(k, pl.multiple_of(x * 128 + h * 64 + t, 32), cols)
                value = value + xr1[k, h, 0, pl.ds(t, 32), cols].astype(F32) + xr2[k, h, pl.ds(t, 32), cols].astype(F32)
                vsum[k, pl.ds(pl.multiple_of(h * 64 + t, 32), 32), cols] = value

        chunks(2, body)
        zs1[k, 0, :, cols] = vsum[k, at(z1 * 32, 32), cols].astype(BF16)
        zs1[k, 1, :, cols] = vsum[k, at(z3 * 32, 32), cols].astype(BF16)
        r_send(piece, 5, zs1.at[k, :, :, cols], zr1.at[k, :, :, cols], to_z1)

    def reduce4(piece):
        _, k, first, width = pieces[piece]
        cols = pl.ds(first, width)
        r_copy(piece, 5, zr1.at[k, :, :, cols], zr1.at[k, :, :, cols], to_z1).wait_recv()
        zs2[k, :, cols] = (vsum[k, at(z2 * 32, 32), cols] + zr1[k, 1, :, cols].astype(F32)).astype(BF16)
        r_send(piece, 6, zs2.at[k, :, cols], zr2.at[k, :, cols], to_z2)

    def result(piece):
        n, k, first, width = pieces[piece]
        part = (k, slice(None), pl.ds(first, width) if k == E else slice(None))
        return pltpu.make_async_copy(total_rows.at[part], out.at[part], in_s.at[5 + n])

    def reduce5(piece):
        _, k, first, width = pieces[piece]
        cols = pl.ds(first, width)
        r_copy(piece, 6, zr2.at[k, :, cols], zr2.at[k, :, cols], to_z2).wait_recv()
        total = vsum[k, at(z * 32, 32), cols] + zr1[k, 0, :, cols].astype(F32)
        here = total_rows.at[k, :, in_matrix(role, k, first, width)]
        here[...] = total + zr2[k, :, cols].astype(F32)
        if k != E:
            r_send(piece, 7, here, here, {"role": 1 - role})
        else:
            result(piece).start()

    def reduced(piece):
        _, k, first, width = pieces[piece]
        there = total_rows.at[k, :, in_matrix(1 - role, k, first, width)]
        r_copy(piece, 7, there, there, {"role": 1 - role}).wait_recv()
        result(piece).start()

    center.wait()
    rows_go()
    selection()
    to_patches(xs)
    gather0(E)
    weights_go(U)
    patches_go(0, xs, px, 128, (2, 0))
    columns_go()
    gather1(E)
    weights_go(W)
    patches_go(0, xs, px, 128, (1, 3))
    gather0(U)
    gather3(E, (0,))
    gather2(E)
    columns_arrive()
    gather3(E, (1,))
    advance(0)
    gather1(U)
    gather0(W)
    advance(1)
    gather3(E, (2, 3))
    advance(2)
    gather2(U)
    gather1(W)
    gather3(U, (0, 1))
    advance(3)
    gather4(E)
    gather5(E)

    patches_arrive(0, px, 128)
    partial_sums(0, px.at[128:256], E)
    to_patches(ts)
    patches_go(1, ts, tg, 0)
    gather3(U, (2, 3))
    gather2(W)
    gather3(W, (0, 1))
    e = all_summed(0)
    recip = lax.rsqrt(jnp.mean(e * e, axis=1, keepdims=True) + 1e-06)
    ered[...] = e
    spread_all(0, nf, 0, (e * recip).astype(BF16))
    gather4(U)
    gather3(W, (2, 3))
    gather5(U)
    spread_arrive(0, nf, 0)

    def hidden(cols):
        pre = with_cols(nf[...], U, cols)
        square = pre * pre
        tangent = jnp.tanh(GELU_FACTOR * (pre + 0.044715 * square * pre))
        act[:, cols] = (0.5 * pre * (1.0 + tangent)).astype(BF16)
        slope[:, cols] = 0.5 * (1.0 + tangent) + 0.5 * pre * (1.0 - tangent * tangent) * GELU_FACTOR * (
            1.0 + 3.0 * 0.044715 * square
        )

    tiles(256, hidden)
    gather4(W)
    gather5(W)
    partial_sums(1, act, W)
    state_go()
    for s in (0, 1):
        spread(1, s, yd, 0, (ered[:, half(s)] + summed(1, s)).astype(BF16))
    patches_arrive(1, tg, 0)
    spread_arrive(1, yd, 0)

    def residual(cols):
        pred = px[128:256, cols].astype(F32) + with_cols(yd[0:128, :], E, cols)
        px[0:128, cols] = ((pred - tg[:, cols].astype(F32)) * (1.0 / 64.0)).astype(BF16)

    tiles(256, residual)
    partial_sums(2, px.at[0:128], E)
    for s in (0, 1):
        dy = summed(2, s)
        dyred[:, half(s)] = dy
        spread(2, s, dyf, 0, dy.astype(BF16))
    state_pass(0)
    state_pass(1)
    spread_arrive(2, dyf, 0)
    terms_across("W", dyf, act)
    terms_here("W", dyf, act)

    def hidden_back(cols):
        dhid[:, cols] = (with_cols(dyf[...], W, cols) * slope[:, cols]).astype(BF16)

    reduce1("W")
    state_pass(2)
    state_pass(3)
    tiles(256, hidden_back)
    partial_sums(3, dhid, U)
    terms_across("U", nf, dhid)
    terms_here("U", nf, dhid)
    reduce1("U")
    reduce2("W")
    dn = all_summed(3)
    e = ered[...]
    recip = lax.rsqrt(jnp.mean(e * e, axis=1, keepdims=True) + 1e-06)
    de = dyred[...] + recip * dn - e * (recip * recip * recip) * jnp.mean(dn * e, axis=1, keepdims=True)
    spread_all(3, yd, 128, de.astype(BF16))
    reduce3("W")
    reduce2("U")
    spread_arrive(3, yd, 128)
    for piece in parts:
        terms_across(piece, yd, px)
    reduce4("W")
    reduce3("U")
    for piece in parts:
        terms_here(piece, yd, px)
        reduce1(piece)
    reduce5("W")
    reduce4("U")
    reduce2("E0")
    reduce2("E1")
    reduce2("E2")
    reduce5("U")
    reduce2("E3")
    state_arrive()
    for piece in parts:
        reduce3(piece)
    for piece in parts:
        reduce4(piece)
    reduced("W")
    reduced("U")
    for piece in parts:
        reduce5(piece)

    for made in started:
        made.wait_send()
    for k in (E, U, W):
        all_posted(wf.at[k, 0:992], ag_s.at[k])
    all_posted(sbuf.at[0:3], rs_s.at[0])
    all_posted(sbuf.at[0:3], mg_s.at[0])
    for part in range(4):
        state_here(part).wait()
    for piece in pieces:
        r_posted(piece)
        result(piece).wait()

    @pl.when(role == 1)
    def _():
        for k in (E, U, W):
            weights_across(k).wait_send()
        for part in range(4):
            state_home(part).wait_send()

    @pl.when(role == 0)
    def _():
        for which in (0, 1):
            all_posted(px.at[0:224], x_s.at[which])
        for part in range(4):
            state_across(part).wait_send()


def train(state, embed, mlp):
    dma = pltpu.SemaphoreType.DMA
    return pl.pallas_call(
        kernel,
        name="train",
        out_shape=(jax.ShapeDtypeStruct((3, OWN, COLS), F32), jax.ShapeDtypeStruct(state.shape[1:], F32)),
        in_specs=[pl.BlockSpec(memory_space=pltpu.HBM)] * 3,
        out_specs=(pl.BlockSpec(memory_space=pl.ANY), pl.BlockSpec(memory_space=pl.ANY)),
        scratch_shapes=[
            pltpu.VMEM((3, OWN, COLS), F32),
            pltpu.VMEM((2, 2, 8, 80, 256), F32),
            pltpu.VMEM((2, 8, 64, 128), BF16),
            pltpu.VMEM((2, 8, 64, 128), BF16),
            pltpu.VMEM((2, 80, 128), F32),
            pltpu.VMEM((2, 80, 128), F32),
            pltpu.VMEM((2048, 256), BF16),
            pltpu.VMEM((128, 2048), BF16),
            pltpu.VMEM((4, OWN, COLS), BF16),
            pltpu.VMEM((4, OWN, COLS), BF16),
            pltpu.VMEM((3, D, COLS), BF16),
            pltpu.VMEM((2 * ROWS, COLS), BF16),
            pltpu.VMEM((2 * ROWS, D), BF16),
            pltpu.VMEM((ROWS, COLS), BF16),
            pltpu.VMEM((ROWS, D), F32),
            pltpu.VMEM((4, ROWS, D), BF16),
            pltpu.VMEM((4, 3, OWN, D), BF16),
            pltpu.VMEM((ROWS, D), BF16),
            pltpu.VMEM((ROWS, D), BF16),
            pltpu.VMEM((ROWS, COLS), BF16),
            pltpu.VMEM((ROWS, COLS), F32),
            pltpu.VMEM((ROWS, COLS), BF16),
            pltpu.VMEM((OWN, D), F32),
            pltpu.VMEM((OWN, D), F32),
            pltpu.VMEM((3, 512, COLS), F32),
            pltpu.VMEM((3, 512, COLS), BF16),
            pltpu.VMEM((3, 512, COLS), BF16),
            pltpu.VMEM((3, 2, 2, 64, COLS), BF16),
            pltpu.VMEM((3, 2, 2, 64, COLS), BF16),
            pltpu.VMEM((3, 2, 64, COLS), BF16),
            pltpu.VMEM((3, 2, 64, COLS), BF16),
            pltpu.VMEM((3, 128, COLS), F32),
            pltpu.VMEM((3, 2, OWN, COLS), BF16),
            pltpu.VMEM((3, 2, OWN, COLS), BF16),
            pltpu.VMEM((3, OWN, COLS), BF16),
            pltpu.VMEM((3, OWN, COLS), BF16),
            dma((11,)), dma((4,)), dma((4,)), dma((8,)), dma((8,)),
            dma((3,)), dma((3,)),
            dma((2,)), dma((2,)),
            dma((3,)), dma((3, 13)),
            dma((1,)), dma((4, 2)),
            dma((1,)), dma((4,)),
            dma((8,)), dma((6, 8)),
        ],
        compiler_params=pltpu.CompilerParams(
            collective_id=0, has_side_effects=True, vmem_limit_bytes=60 * 1024 * 1024
        ),
        cost_estimate=pl.CostEstimate(flops=6 * 10**9, bytes_accessed=4 * 10**8, transcendentals=10**5),
    )(state, embed, mlp)


def shards(state, embed, mlp, mom_embed, mom_mlp):
    grads, state_out = train(state, embed, mlp)
    mom_embed_out = MOMENTUM_DECAY * mom_embed + grads[:1]
    mom_mlp_out = MOMENTUM_DECAY * mom_mlp + grads[None, 1:]
    embed_out = (embed.astype(F32) - LEARNING_RATE * mom_embed_out).astype(BF16)
    mlp_out = (mlp.astype(F32) - LEARNING_RATE * mom_mlp_out).astype(BF16)
    return (state_out, embed_out, mlp_out, mom_embed_out, mom_mlp_out)


def solution(mesh):
    placed = (
        P("role", None, None, "dp", "mp"),
        P("role", "dp", "mp"),
        P("role", None, "dp", "mp"),
        P("role", "dp", "mp"),
        P("role", None, "dp", "mp"),
    )
    return jax.shard_map(
        shards,
        mesh=mesh,
        in_specs=placed,
        out_specs=(
            P(None, None, "dp", "mp"),
            P("role", "dp", "mp"),
            P("role", None, "dp", "mp"),
            P("role", "dp", "mp"),
            P("role", None, "dp", "mp"),
        ),
        check_vma=False,
    )
```

```python
import jax
import jax.numpy as jnp
from jax import lax
from jax.experimental import pallas as pl
from jax.experimental.pallas import tpu as pltpu
from jax.sharding import PartitionSpec as P

PATCH = 16
STEPS = 4


SUBSTRATE_DIFFUSION = 0.2
CATALYST_DIFFUSION = 0.1
FEED_RATE = 0.037
KILL_RATE = 0.06
TIME_STEP = 0.8
GELU_FACTOR = 0.7978845608028654
MOMENTUM_DECAY = 0.9
LEARNING_RATE = 0.003

BF16 = jnp.bfloat16
F32 = jnp.float32
MESH = pl.DeviceIdType.MESH
ROWS = 128
OWN = 32
D = 1024
COLS = 1024
E, U, W = 0, 1, 2


def kernel(
    state, embed, mlp, out, state_out,
    total_rows, field, final, passed, edge, edges, onehot, spread_in, xs, ts, wf, px, yd, tg, part, sbuf, rbuf, nf, dyf, act, slope, dhid, ered, dyred,
    acc, cs, cr, xs1, xr1, xs2, xr2, vsum, zs1, zr1, zs2, zr2,
    in_s, halo_s, halo_r, state_s, state_r, role_s, role_r, x_s, x_r, ag_s, ag_r, rs_s, rs_r, mg_s, mg_r, gr_s, gr_r,
):
    role = lax.axis_index("role")
    dp = lax.axis_index("dp")
    mp = lax.axis_index("mp")
    x, z, c = dp // 8, (dp // 2) % 4, dp % 2

    def dev(x_, z_, c_):
        return {"dp": (x_ * 4 + z_) * 2 + c_}

    x1, x2, x3 = x + 1 - 2 * (x % 2), (x + 2) % 4, 3 - x
    z1, z2 = z + 1 - 2 * (z % 2), (z + 2) % 4
    z3 = (z1 + 2) % 4
    c1 = 1 - c
    zm = 3 - z
    zl = jnp.where(role == 1, z, zm)
    to_c, to_x1, to_x3 = dev(x, z, c1), dev(x1, z, c), dev(x3, z, c)
    to_z1, to_z2 = dev(x, z1, c), dev(x, z2, c)
    after, before = {"dp": (dp + 1) % 32}, {"dp": (dp + 31) % 32}
    east, west = {"mp": (mp + 1) % 4}, {"mp": (mp + 3) % 4}
    mirror = dev(x, zm, c)["dp"]
    center = pltpu.make_async_copy(
        state.at[0], field.at[0, :, :, pl.ds(8, 64), pl.ds(0, 128)], in_s.at[0]
    )
    center.start()
    other = [(mp + o) % 4 for o in range(4)]

    def at(start, size):
        return pl.ds(pl.multiple_of(start, 16), size)

    barrier = pltpu.get_barrier_semaphore()
    friends = [to_c, to_x1, to_x3, to_z1, to_z2, after, before, {"dp": mirror}, {"role": 1 - role}]
    friends += [{"mp": other[o]} for o in (1, 2, 3)]
    friends += [{"role": 1 - role, "dp": mirror, "mp": other[o]} for o in range(4)]
    for friend in friends:
        pl.semaphore_signal(barrier, inc=1, device_id=friend, device_id_type=MESH)
    pl.semaphore_wait(barrier, len(friends))

    started = []

    def copy(src, dst, ssem, rsem, to):
        return pltpu.make_async_remote_copy(
            src_ref=src, dst_ref=dst, send_sem=ssem, recv_sem=rsem, device_id=to, device_id_type=MESH
        )

    def send(src, dst, ssem, rsem, to):
        made = copy(src, dst, ssem, rsem, to)
        made.start()
        started.append(made)

    def arrive(dst, ssem, rsem, frm):
        copy(dst, dst, ssem, rsem, frm).wait_recv()

    def post(src, dst, ssem, rsem, to):
        copy(src, dst, ssem, rsem, to).start()

    def all_posted(whole, ssem):
        pltpu.make_async_copy(whole, whole, ssem).wait()

    own_rows = at(c * 512 + x * 128 + zl * 32, 32)
    far_rows = at(c * 512 + x * 128 + z * 32, 32)
    w = (embed.at[0], mlp.at[0, 0], mlp.at[0, 1])

    def weights_across(k):
        return copy(w[k], wf.at[k, far_rows], role_s.at[k], role_r.at[k], {"role": 0, "dp": mirror})

    def weights_here(k):
        return pltpu.make_async_copy(w[k], wf.at[k, far_rows], role_r.at[k])

    def patches(which, src, dst, base, o):
        rows = at(base + 32 * mp, 32)
        made = []
        for r in (1, 0):
            if o == 0 and r == 0:
                continue
            to = {"role": 1, "dp": mirror, "mp": other[o]} if r == 1 else {"role": 0, "mp": other[o]}
            made.append(copy(src.at[other[o]], dst.at[rows], x_s.at[which], x_r.at[which], to))
        return made

    def patches_here(which, src, dst, base):
        return pltpu.make_async_copy(src.at[mp], dst.at[at(base + 32 * mp, 32)], x_r.at[which])

    def patches_go(which, src, dst, base, some=(0, 1, 2, 3)):
        @pl.when(role == 0)
        def _():
            for o in some:
                for made in patches(which, src, dst, base, o):
                    made.start()
            if 0 in some:
                patches_here(which, src, dst, base).start()

    def state_part(whole, part):
        return whole.at[part // 2, pl.ds(4 * (part % 2), 4)]

    def state_across(part):
        return copy(state_part(final, part), state_part(passed, part), state_s.at[part], state_r.at[part],
                    {"role": 1, "dp": mirror})

    def state_home(part):
        return copy(state_part(passed, part), state_part(final, part), state_s.at[4 + part], state_r.at[4 + part],
                    {"dp": mirror})

    def state_here(part):
        rounded = field.at[1, part // 2, pl.ds(4 * (part % 2), 4), pl.ds(8, 64), pl.ds(0, 128)]
        return pltpu.make_async_copy(rounded, state_part(state_out, part), in_s.at[1 + part])

    def state_widen(part):
        species, planes = part // 2, pl.ds(4 * (part % 2), 4)
        field[1, species, planes, 8:72, 0:128] = final[species, planes].astype(F32)
        state_here(part).start()

    def state_go():
        @pl.when(role == 0)
        def _():
            for part in range(4):
                species, planes = part // 2, pl.ds(4 * (part % 2), 4)
                final[species, planes] = field[0, species, planes, 8:72, 0:128].astype(BF16)
                state_across(part).start()
            for part in range(4):
                state_widen(part)

    def state_arrive():
        @pl.when(role == 1)
        def _():
            for part in range(4):
                state_home(part).wait_recv()
                state_widen(part)

    def state_pass(part):
        @pl.when(role == 1)
        def _():
            state_across(part).wait_recv()
            state_home(part).start()

    @pl.when(role == 1)
    def _():
        weights_across(E).start()
        for k in (E, U, W):
            weights_here(k).start()

    def weights_go(k):
        @pl.when(role == 1)
        def _():
            weights_across(k).start()

    def patches_arrive(which, dst, base):
        arrive(dst.at[base : base + 128], x_s.at[which], x_r.at[which], east)

    lane = lax.broadcasted_iota(jnp.int32, (80, 128), 1)

    def halo_rows(i, src, dst, to):
        ends = [field.at[0, :, :, pl.ds(start, 8), pl.ds(0, 128)] for start in (src, dst)]
        return copy(ends[0], ends[1], halo_s.at[i], halo_r.at[i], to)

    def rows_go():
        for i, src, dst, to in ((0, 8, 72, before), (1, 64, 0, after)):
            halo_rows(i, src, dst, to).start()

    def columns_go():
        halo_rows(0, 72, 72, after).wait_recv()
        halo_rows(1, 0, 0, before).wait_recv()
        halo_rows(0, 8, 72, before).wait_send()
        halo_rows(1, 64, 0, after).wait_send()
        edge[...] = jnp.zeros_like(edge)
        for p in range(16):
            cells = field[0, p // 8, p % 8, :, 0:128]
            inside = (lane >= 4 * p) & (lane < 4 * p + 4)
            edge[0] = jnp.where(inside, pltpu.roll(cells, 4 * p, 1) if p else cells, edge[0])
            edge[1] = jnp.where(inside, pltpu.roll(cells, 4 * p + 4, 1), edge[1])
        send(edge.at[0], edges.at[0], halo_s.at[2], halo_r.at[2], west)
        send(edge.at[1], edges.at[1], halo_s.at[3], halo_r.at[3], east)

    def columns_arrive():
        arrive(edges.at[0], halo_s.at[2], halo_r.at[2], east)
        arrive(edges.at[1], halo_s.at[3], halo_r.at[3], west)
        for p in range(16):
            behind = edges[0] if p == 0 else pltpu.roll(edges[0], 128 - 4 * p, 1)
            ahead = pltpu.roll(edges[1], 124 - 4 * p, 1)
            field[0, p // 8, p % 8, :, 128:256] = jnp.where(lane < 4, behind, jnp.where(lane >= 124, ahead, 0.0))

    def advance(step):
        now, later = step % 2, (step + 1) % 2

        @pl.loop(0, 8)
        def _(p):
            low, high = jnp.maximum(p - 1, 0), jnp.minimum(p + 1, 7)

            def laplace(s):
                mid = field[now, s, p]
                total = field[now, s, low] + field[now, s, high]
                total = total + pltpu.roll(mid, 1, 0) + pltpu.roll(mid, 79, 0)
                total = total + pltpu.roll(mid, 1, 1) + pltpu.roll(mid, 255, 1)
                return mid, total - 6.0 * mid

            substrate, first = laplace(0)
            catalyst, second = laplace(1)
            growth = substrate * catalyst * catalyst
            field[later, 0, p] = substrate + TIME_STEP * (
                SUBSTRATE_DIFFUSION * first - growth + FEED_RATE * (1.0 - substrate)
            )
            field[later, 1, p] = catalyst + TIME_STEP * (
                CATALYST_DIFFUSION * second + growth - (FEED_RATE + KILL_RATE) * catalyst
            )

    def selection():
        feature = lax.broadcasted_iota(jnp.int32, (128, 256), 1)
        inner = lax.broadcasted_iota(jnp.int32, (128, 256), 0) % PATCH
        for r in range(PATCH):
            onehot[128 * r : 128 * r + 128, :] = jnp.where(feature == PATCH * r + inner, 1.0, 0.0).astype(BF16)

    def to_patches(dst):
        patch = lax.broadcasted_iota(jnp.int32, (8, 128), 0)
        own = lax.broadcasted_iota(jnp.int32, (8, 128), 1) // PATCH == patch

        @pl.loop(0, 4)
        def _(j):
            @pl.loop(0, 4)
            def _(q):
                species, plane = j // 2, 4 * (j % 2) + q
                for r in range(PATCH):
                    pieces = []
                    for by in range(4):
                        row = field[0, species, plane, pl.ds(8 + PATCH * by + r, 1), 0:128]
                        pieces.append(jnp.where(own, jnp.broadcast_to(row, (8, 128)), 0.0))
                    rows = pl.ds(pl.multiple_of(32 * q, 32), 32)
                    spread_in[rows, 128 * r : 128 * r + 128] = jnp.concatenate(pieces, axis=0).astype(BF16)

            moved = jnp.dot(spread_in[...], onehot[...], preferred_element_type=F32).astype(BF16)
            for q in range(4):
                dst[j, :, 256 * q : 256 * q + 256] = moved[32 * q : 32 * q + 32, :]

    zl1, zl2 = zl + 1 - 2 * (zl % 2), (zl + 2) % 4
    label = (zl, zl2, zl1, (zl1 + 2) % 4)

    def block(x_, b, c_=c):
        return c_ * 512 + x_ * 128 + label[b] * 32

    def g_send(k, i, start, size, to):
        rows = at(start, size)
        post(wf.at[k, rows], wf.at[k, rows], ag_s.at[k], ag_r.at[k, i], to)

    def g_arrive(k, i, start, size, frm):
        arrive(wf.at[k, at(start, size)], ag_s.at[k], ag_r.at[k, i], frm)

    def along_x(k, b):
        g_send(k, 3 + b, block(x, b), 32, to_x1)
        g_send(k, 7 + b, block(x, b), 32, to_x3)
        g_send(k, 12, block(x, b), 32, to_c)

    def gather0(k):
        arrive(wf.at[k, own_rows], role_s.at[k], role_r.at[k], {"role": 1 - role})
        g_send(k, 0, block(x, 0), 32, to_z2)
        g_send(k, 1, block(x, 0), 32, to_z1)
        along_x(k, 0)

    def gather1(k):
        g_arrive(k, 0, block(x, 1), 32, to_z2)
        g_send(k, 2, block(x, 1), 32, to_z1)
        along_x(k, 1)

    def gather2(k):
        g_arrive(k, 1, block(x, 2), 32, to_z1)
        along_x(k, 2)
        g_arrive(k, 2, block(x, 3), 32, to_z1)
        along_x(k, 3)

    def gather3(k, some):
        for b in some:
            g_arrive(k, 3 + b, block(x1, b), 32, to_x1)
            g_send(k, 11, block(x1, b), 16, to_x3)
            g_send(k, 12, block(x1, b), 32, to_c)
            g_arrive(k, 7 + b, block(x3, b), 32, to_x3)
            g_send(k, 11, block(x3, b) + 16, 16, to_x1)
            g_send(k, 12, block(x3, b), 32, to_c)

    def gather4(k):
        g_arrive(k, 11, c * 512 + x2 * 128, 128, to_x1)
        g_send(k, 12, c * 512 + x2 * 128, 128, to_c)

    def gather5(k):
        g_arrive(k, 12, c1 * 512, 512, to_c)

    def tiles(width, body, first=0, last=COLS):
        @pl.loop(first // width, last // width)
        def _(t):
            body(pl.ds(pl.multiple_of(t * width, width), width))

    def with_rows(lhs, k, rows):
        return lax.dot_general(lhs, wf[k, rows, :], (((1,), (1,)), ((), ())), preferred_element_type=F32)

    def with_cols(lhs, k, cols):
        return jnp.dot(lhs, wf[k, :, cols], preferred_element_type=F32)

    mine = at(32 * mp, 32)

    def half(s):
        return pl.ds(512 * s, 512)

    def partial_sums(i, lhs, k):
        for s in (0, 1):

            @pl.loop(0, 2)
            def _(t):
                cols = pl.ds(pl.multiple_of(512 * s + 256 * t, 256), 256)
                value = with_rows(lhs[...], k, cols)
                part[:, cols] = value
                sbuf[i, :, cols] = value.astype(BF16)

            for o in (2, 1, 3):
                post(sbuf.at[i, at(32 * other[o], 32), half(s)], rbuf.at[i, o - 1, :, half(s)],
                     rs_s.at[0], rs_r.at[i, s], {"mp": other[o]})

    def summed(i, s):
        total = part[mine, half(s)]
        arrive(rbuf.at[i, :, :, half(s)], rs_s.at[0], rs_r.at[i, s], east)
        for o in (1, 2, 3):
            total = total + rbuf[i, o - 1, :, half(s)].astype(F32)
        return total

    def all_summed(i):
        return jnp.concatenate([summed(i, 0), summed(i, 1)], axis=1)

    def spread(i, s, dst, base, value):
        rows = at(base + 32 * mp, 32)
        dst[rows, half(s)] = value
        for o in (2, 1, 3):
            post(dst.at[rows, half(s)], dst.at[rows, half(s)], mg_s.at[0], mg_r.at[i], {"mp": other[o]})

    def spread_all(i, dst, base, value):
        for s in (0, 1):
            spread(i, s, dst, base, value[:, 512 * s : 512 * s + 512])

    def spread_arrive(i, dst, base):
        arrive(dst.at[base : base + 96], mg_s.at[0], mg_r.at[i], east)

    pieces = {"W": (0, W, 0, 512), "U": (1, U, 0, 512)}
    parts = ("E0", "E1", "E2", "E3")
    pieces.update({name: (2 + i, E, 256 * i, 256) for i, name in enumerate(parts)})

    def in_matrix(group, k, first, width):
        return pl.ds(first, width) if k == E else pl.ds(pl.multiple_of(512 * group + first, 512), width)

    def product(piece, lhs, rhs, core, store):
        _, k, first, width = pieces[piece]

        @pl.loop(0, 2)
        def _(t):
            rows = pl.ds(pl.multiple_of(core * 512 + t * 256, 256), 256)
            local = pl.ds(pl.multiple_of(t * 256, 256), 256)
            store(local, pl.ds(first, width), lax.dot_general(
                lhs[:, rows], rhs[:, in_matrix(role, k, first, width)], (((0,), (0,)), ((), ())),
                preferred_element_type=F32,
            ))

    def r_copy(piece, i, src, dst, to):
        n = pieces[piece][0]
        return copy(src, dst, gr_s.at[n if i < 7 else 6 + n], gr_r.at[n, i], to)

    def r_send(piece, i, src, dst, to):
        r_copy(piece, i, src, dst, to).start()

    def r_posted(piece):
        n, k, first, width = pieces[piece]
        all_posted(wf.at[k, 0:992, 0:width], gr_s.at[n])
        if k != E:
            all_posted(total_rows.at[k, :, 0:width], gr_s.at[6 + n])

    def terms_across(piece, lhs, rhs):
        _, k, first, width = pieces[piece]

        def store(local, cols, value):
            cs[k, local, cols] = value.astype(BF16)

        product(piece, lhs, rhs, c1, store)
        whole = (k, slice(None), pl.ds(first, width))
        r_send(piece, 0, cs.at[whole], cr.at[whole], to_c)

    def terms_here(piece, lhs, rhs):
        k = pieces[piece][1]

        def store(local, cols, value):
            acc[k, local, cols] = value

        product(piece, lhs, rhs, c, store)

    def chunks(count, body):
        @pl.loop(0, count)
        def _(t):
            body(pl.multiple_of(t * 32, 32))

    def pair(k, start, cols):
        return acc[k, pl.ds(start, 32), cols] + cr[k, pl.ds(start, 32), cols].astype(F32)

    def reduce1(piece):
        _, k, first, width = pieces[piece]
        cols = pl.ds(first, width)
        r_copy(piece, 0, cr.at[k, :, cols], cr.at[k, :, cols], to_c).wait_recv()

        def body(t):
            for h, far in ((0, x3), (1, x1)):
                for i, xb in ((0, far), (1, x2)):
                    value = pair(k, pl.multiple_of(xb * 128 + h * 64 + t, 32), cols)
                    xs1[k, h, i, pl.ds(t, 32), cols] = value.astype(BF16)

        chunks(2, body)
        for h, to in ((0, to_x3), (1, to_x1)):
            r_send(piece, 1 + h, xs1.at[k, h, :, :, cols], xr1.at[k, h, :, :, cols], to)

    def reduce2(piece):
        _, k, first, width = pieces[piece]
        cols = pl.ds(first, width)
        for h, frm in ((0, to_x3), (1, to_x1)):
            r_copy(piece, 1 + h, xr1.at[k, h, :, :, cols], xr1.at[k, h, :, :, cols], frm).wait_recv()

        def body(t):
            for h, near in ((0, x1), (1, x3)):
                value = pair(k, pl.multiple_of(near * 128 + h * 64 + t, 32), cols)
                xs2[k, h, pl.ds(t, 32), cols] = (value + xr1[k, h, 1, pl.ds(t, 32), cols].astype(F32)).astype(BF16)

        chunks(2, body)
        for h, to in ((0, to_x1), (1, to_x3)):
            r_send(piece, 3 + h, xs2.at[k, h, :, cols], xr2.at[k, h, :, cols], to)

    def reduce3(piece):
        _, k, first, width = pieces[piece]
        cols = pl.ds(first, width)
        for h, frm in ((0, to_x1), (1, to_x3)):
            r_copy(piece, 3 + h, xr2.at[k, h, :, cols], xr2.at[k, h, :, cols], frm).wait_recv()

        def body(t):
            for h in (0, 1):
                value = pair(k, pl.multiple_of(x * 128 + h * 64 + t, 32), cols)
                value = value + xr1[k, h, 0, pl.ds(t, 32), cols].astype(F32) + xr2[k, h, pl.ds(t, 32), cols].astype(F32)
                vsum[k, pl.ds(pl.multiple_of(h * 64 + t, 32), 32), cols] = value

        chunks(2, body)
        zs1[k, 0, :, cols] = vsum[k, at(z1 * 32, 32), cols].astype(BF16)
        zs1[k, 1, :, cols] = vsum[k, at(z3 * 32, 32), cols].astype(BF16)
        r_send(piece, 5, zs1.at[k, :, :, cols], zr1.at[k, :, :, cols], to_z1)

    def reduce4(piece):
        _, k, first, width = pieces[piece]
        cols = pl.ds(first, width)
        r_copy(piece, 5, zr1.at[k, :, :, cols], zr1.at[k, :, :, cols], to_z1).wait_recv()
        zs2[k, :, cols] = (vsum[k, at(z2 * 32, 32), cols] + zr1[k, 1, :, cols].astype(F32)).astype(BF16)
        r_send(piece, 6, zs2.at[k, :, cols], zr2.at[k, :, cols], to_z2)

    def result(piece):
        n, k, first, width = pieces[piece]
        part = (k, slice(None), pl.ds(first, width) if k == E else slice(None))
        return pltpu.make_async_copy(total_rows.at[part], out.at[part], in_s.at[5 + n])

    def reduce5(piece):
        _, k, first, width = pieces[piece]
        cols = pl.ds(first, width)
        r_copy(piece, 6, zr2.at[k, :, cols], zr2.at[k, :, cols], to_z2).wait_recv()
        total = vsum[k, at(z * 32, 32), cols] + zr1[k, 0, :, cols].astype(F32)
        here = total_rows.at[k, :, in_matrix(role, k, first, width)]
        here[...] = total + zr2[k, :, cols].astype(F32)
        if k != E:
            r_send(piece, 7, here, here, {"role": 1 - role})
        else:
            result(piece).start()

    def reduced(piece):
        _, k, first, width = pieces[piece]
        there = total_rows.at[k, :, in_matrix(1 - role, k, first, width)]
        r_copy(piece, 7, there, there, {"role": 1 - role}).wait_recv()
        result(piece).start()

    center.wait()
    rows_go()
    selection()
    to_patches(xs)
    gather0(E)
    weights_go(U)
    patches_go(0, xs, px, 128, (2, 0))
    columns_go()
    gather1(E)
    weights_go(W)
    patches_go(0, xs, px, 128, (1, 3))
    gather0(U)
    gather3(E, (0,))
    gather2(E)
    columns_arrive()
    gather3(E, (1,))
    advance(0)
    gather1(U)
    gather0(W)
    advance(1)
    gather3(E, (2, 3))
    advance(2)
    gather2(U)
    gather1(W)
    gather3(U, (0, 1))
    advance(3)
    gather4(E)
    gather5(E)

    patches_arrive(0, px, 128)
    partial_sums(0, px.at[128:256], E)
    to_patches(ts)
    patches_go(1, ts, tg, 0)
    gather3(U, (2, 3))
    gather2(W)
    gather3(W, (0, 1))
    e = all_summed(0)
    recip = lax.rsqrt(jnp.mean(e * e, axis=1, keepdims=True) + 1e-06)
    ered[...] = e
    spread_all(0, nf, 0, (e * recip).astype(BF16))
    gather4(U)
    gather3(W, (2, 3))
    gather5(U)
    spread_arrive(0, nf, 0)

    def hidden(cols):
        pre = with_cols(nf[...], U, cols)
        square = pre * pre
        tangent = jnp.tanh(GELU_FACTOR * (pre + 0.044715 * square * pre))
        act[:, cols] = (0.5 * pre * (1.0 + tangent)).astype(BF16)
        slope[:, cols] = 0.5 * (1.0 + tangent) + 0.5 * pre * (1.0 - tangent * tangent) * GELU_FACTOR * (
            1.0 + 3.0 * 0.044715 * square
        )

    tiles(256, hidden, 0, 512)
    gather4(W)
    tiles(256, hidden, 512, 1024)
    gather5(W)
    partial_sums(1, act, W)
    state_go()
    for s in (0, 1):
        spread(1, s, yd, 0, (ered[:, half(s)] + summed(1, s)).astype(BF16))
    patches_arrive(1, tg, 0)
    spread_arrive(1, yd, 0)

    def residual(cols):
        pred = px[128:256, cols].astype(F32) + with_cols(yd[0:128, :], E, cols)
        px[0:128, cols] = ((pred - tg[:, cols].astype(F32)) * (1.0 / 64.0)).astype(BF16)

    tiles(256, residual)
    partial_sums(2, px.at[0:128], E)
    for s in (0, 1):
        dy = summed(2, s)
        dyred[:, half(s)] = dy
        spread(2, s, dyf, 0, dy.astype(BF16))
    state_pass(0)
    state_pass(1)
    spread_arrive(2, dyf, 0)
    terms_across("W", dyf, act)
    terms_here("W", dyf, act)

    def hidden_back(cols):
        dhid[:, cols] = (with_cols(dyf[...], W, cols) * slope[:, cols]).astype(BF16)

    reduce1("W")
    state_pass(2)
    state_pass(3)
    tiles(256, hidden_back)
    partial_sums(3, dhid, U)
    terms_across("U", nf, dhid)
    terms_here("U", nf, dhid)
    reduce1("U")
    reduce2("W")
    dn = all_summed(3)
    e = ered[...]
    recip = lax.rsqrt(jnp.mean(e * e, axis=1, keepdims=True) + 1e-06)
    de = dyred[...] + recip * dn - e * (recip * recip * recip) * jnp.mean(dn * e, axis=1, keepdims=True)
    spread_all(3, yd, 128, de.astype(BF16))
    reduce3("W")
    reduce2("U")
    spread_arrive(3, yd, 128)
    for piece in parts:
        terms_across(piece, yd, px)
    reduce4("W")
    reduce3("U")
    for piece in parts:
        terms_here(piece, yd, px)
        reduce1(piece)
    reduce5("W")
    reduce4("U")
    reduce2("E0")
    reduce2("E1")
    reduce2("E2")
    reduce5("U")
    reduce2("E3")
    state_arrive()
    for piece in parts:
        reduce3(piece)
    for piece in parts:
        reduce4(piece)
    reduced("W")
    reduced("U")
    for piece in parts:
        reduce5(piece)

    for made in started:
        made.wait_send()
    for k in (E, U, W):
        all_posted(wf.at[k, 0:992], ag_s.at[k])
    all_posted(sbuf.at[0:3], rs_s.at[0])
    all_posted(sbuf.at[0:3], mg_s.at[0])
    for part in range(4):
        state_here(part).wait()
    for piece in pieces:
        r_posted(piece)
        result(piece).wait()

    @pl.when(role == 1)
    def _():
        for k in (E, U, W):
            weights_across(k).wait_send()
        for part in range(4):
            state_home(part).wait_send()

    @pl.when(role == 0)
    def _():
        for which in (0, 1):
            all_posted(px.at[0:224], x_s.at[which])
        for part in range(4):
            state_across(part).wait_send()


def train(state, embed, mlp):
    dma = pltpu.SemaphoreType.DMA
    return pl.pallas_call(
        kernel,
        name="train",
        out_shape=(jax.ShapeDtypeStruct((3, OWN, COLS), F32), jax.ShapeDtypeStruct(state.shape[1:], F32)),
        in_specs=[pl.BlockSpec(memory_space=pltpu.HBM)] * 3,
        out_specs=(pl.BlockSpec(memory_space=pl.ANY), pl.BlockSpec(memory_space=pl.ANY)),
        scratch_shapes=[
            pltpu.VMEM((3, OWN, COLS), F32),
            pltpu.VMEM((2, 2, 8, 80, 256), F32),
            pltpu.VMEM((2, 8, 64, 128), BF16),
            pltpu.VMEM((2, 8, 64, 128), BF16),
            pltpu.VMEM((2, 80, 128), F32),
            pltpu.VMEM((2, 80, 128), F32),
            pltpu.VMEM((2048, 256), BF16),
            pltpu.VMEM((128, 2048), BF16),
            pltpu.VMEM((4, OWN, COLS), BF16),
            pltpu.VMEM((4, OWN, COLS), BF16),
            pltpu.VMEM((3, D, COLS), BF16),
            pltpu.VMEM((2 * ROWS, COLS), BF16),
            pltpu.VMEM((2 * ROWS, D), BF16),
            pltpu.VMEM((ROWS, COLS), BF16),
            pltpu.VMEM((ROWS, D), F32),
            pltpu.VMEM((4, ROWS, D), BF16),
            pltpu.VMEM((4, 3, OWN, D), BF16),
            pltpu.VMEM((ROWS, D), BF16),
            pltpu.VMEM((ROWS, D), BF16),
            pltpu.VMEM((ROWS, COLS), BF16),
            pltpu.VMEM((ROWS, COLS), F32),
            pltpu.VMEM((ROWS, COLS), BF16),
            pltpu.VMEM((OWN, D), F32),
            pltpu.VMEM((OWN, D), F32),
            pltpu.VMEM((3, 512, COLS), F32),
            pltpu.VMEM((3, 512, COLS), BF16),
            pltpu.VMEM((3, 512, COLS), BF16),
            pltpu.VMEM((3, 2, 2, 64, COLS), BF16),
            pltpu.VMEM((3, 2, 2, 64, COLS), BF16),
            pltpu.VMEM((3, 2, 64, COLS), BF16),
            pltpu.VMEM((3, 2, 64, COLS), BF16),
            pltpu.VMEM((3, 128, COLS), F32),
            pltpu.VMEM((3, 2, OWN, COLS), BF16),
            pltpu.VMEM((3, 2, OWN, COLS), BF16),
            pltpu.VMEM((3, OWN, COLS), BF16),
            pltpu.VMEM((3, OWN, COLS), BF16),
            dma((11,)), dma((4,)), dma((4,)), dma((8,)), dma((8,)),
            dma((3,)), dma((3,)),
            dma((2,)), dma((2,)),
            dma((3,)), dma((3, 13)),
            dma((1,)), dma((4, 2)),
            dma((1,)), dma((4,)),
            dma((8,)), dma((6, 8)),
        ],
        compiler_params=pltpu.CompilerParams(
            collective_id=0, has_side_effects=True, vmem_limit_bytes=60 * 1024 * 1024
        ),
        cost_estimate=pl.CostEstimate(flops=6 * 10**9, bytes_accessed=4 * 10**8, transcendentals=10**5),
    )(state, embed, mlp)


def shards(state, embed, mlp, mom_embed, mom_mlp):
    grads, state_out = train(state, embed, mlp)
    mom_embed_out = MOMENTUM_DECAY * mom_embed + grads[:1]
    mom_mlp_out = MOMENTUM_DECAY * mom_mlp + grads[None, 1:]
    embed_out = (embed.astype(F32) - LEARNING_RATE * mom_embed_out).astype(BF16)
    mlp_out = (mlp.astype(F32) - LEARNING_RATE * mom_mlp_out).astype(BF16)
    return (state_out, embed_out, mlp_out, mom_embed_out, mom_mlp_out)


def solution(mesh):
    placed = (
        P("role", None, None, "dp", "mp"),
        P("role", "dp", "mp"),
        P("role", None, "dp", "mp"),
        P("role", "dp", "mp"),
        P("role", None, "dp", "mp"),
    )
    return jax.shard_map(
        shards,
        mesh=mesh,
        in_specs=placed,
        out_specs=(
            P(None, None, "dp", "mp"),
            P("role", "dp", "mp"),
            P("role", None, "dp", "mp"),
            P("role", "dp", "mp"),
            P("role", None, "dp", "mp"),
        ),
        check_vma=False,
    )
```
